256 devices in a mesh: tm: 4 (over y_hi, core), space: 64 (over x, y_lo, z).
Axes of the slice: x: 4, y: 4 (y_hi: 2, y_lo: 2; y = y_hi * 2 + y_lo), z: 8, core: 2. Of those that a mesh axis runs over, the one named last changes fastest.
Arguments:
- initial: float32 [4, 3, 64, 16, 16, 128], P('tm', None, 'space'), may hold values from -3 to 3
Outputs:
- end_state: float32 [4, 3, 64, 16, 16, 128], P('tm', None, 'space')
The draws below stay inside these ranges and needn't reach their ends.
All inputs are finite; a program needn't handle non-finite values.
Results may differ from the reference program's by a relative error of at most 0.0001.
Values sent between devices are 32-bit elements; how exact they have to be, the bound alone decides.
No kernel may reach another device: no remote copies, remote signals or barrier semaphores. Data moves between devices by JAX's collectives and lax.ppermute only.
A program may use at most 128 MiB of HBM per device.

```python
import jax
import jax.numpy as jnp
import numpy as np
from jax import lax

SIDE = 16
YBRICKS = 4
ZCELLS = 128
BRICKS = 64
SLICES = 4
N_TM = 4


def steps_of(rng, shape, split, smallest, high):
    level, own = 1.0, jax.random.fold_in(rng, 6)
    for dim, blocks in split:
        heights = jnp.exp(jax.random.uniform(jax.random.fold_in(own, dim), (blocks,), jnp.float32, smallest / len(split), high / len(split)))
        level = level * jnp.repeat(heights, shape[dim] // blocks).reshape([-1 if axis == dim else 1 for axis in range(len(shape))])
    return level


def scatter_about(own_key, extent, deviation, limit, cuts=(), kind=jnp.bfloat16):
    entries = deviation * jax.random.normal(own_key, extent, jnp.float32)
    if cuts:
        entries = entries * steps_of(own_key, extent, cuts, -0.22, 0.18)
    return jnp.clip(entries, -limit, limit).astype(kind)


def setup_inputs(seed: int = 0) -> dict:
    key_of = jax.random.split(jax.random.key(seed), 2)
    initial = scatter_about(key_of[0], (SLICES, 3, BRICKS, SIDE, SIDE, ZCELLS), 0.5, 3.0, ((0, 4), (2, 64)), jnp.float32)
    return {"initial": initial}


EXACT = lax.Precision.HIGHEST
TIME_STEP = 0.001
VISCOSITY = 0.05
QUAD_WEIGHTS = ((5.0 / 24.0, 1.0 / 3.0, -1.0 / 24.0), (-1.0 / 24.0, 1.0 / 3.0, 5.0 / 24.0))


def cheb_tables(count):
    index = np.arange(count)
    points = -np.cos(np.pi * index / (count - 1))
    weights = (-1.0) ** index
    weights[0] = weights[0] * 0.5
    weights[-1] = weights[-1] * 0.5
    return points, weights


def diff_matrix(points, weights):
    count = points.shape[0]
    ident = np.eye(count)
    gaps = points[:, None] - points[None, :] + ident
    matrix = (weights[None, :] / weights[:, None]) / gaps
    matrix = matrix * (1.0 - ident)
    return matrix - ident * matrix.sum(axis=1)[:, None]


def interp_matrix(points, weights, targets):
    gaps = targets[:, None] - points[None, :]
    exact_hit = np.abs(gaps) < 1e-12
    safe_gaps = np.where(exact_hit, 1.0, gaps)
    terms = weights[None, :] / safe_gaps
    matrix = terms / terms.sum(axis=1, keepdims=True)
    any_hit = exact_hit.any(axis=1)
    return np.where(any_hit[:, None], np.where(exact_hit, 1.0, 0.0), matrix)


def apply_along(values, matrix, axis):
    full_shape = values.shape
    rows_out, rows_in = matrix.shape
    elements = full_shape[axis] // rows_in
    blocked = values.reshape(full_shape[:axis] + (elements, rows_in) + full_shape[axis + 1:])
    einsum_forms = {1: "ij,cejyz->ceiyz", 2: "ij,cxejz->cxeiz", 3: "ij,cxyej->cxyei"}
    result = jnp.einsum(einsum_forms[axis], matrix, blocked, precision=EXACT)
    return result.reshape(full_shape[:axis] + (elements * rows_out,) + full_shape[axis + 1:])


def derivative(values, axis, diff, lift_coef):
    count = diff.shape[0]
    length = values.shape[axis]
    position = jnp.arange(length) % count
    bshape = [1, 1, 1, 1]
    bshape[axis] = length
    is_first = (position == 0).astype(jnp.float32).reshape(bshape)
    is_last = (position == count - 1).astype(jnp.float32).reshape(bshape)
    inner = apply_along(values, diff, axis)
    return inner + lift_coef * (is_first * (values - jnp.roll(values, 1, axis)) + is_last * (jnp.roll(values, -1, axis) - values))


def tendency(field, diff, lift_coef):
    grad_x = derivative(field, 1, diff, lift_coef)
    grad_y = derivative(field, 2, diff, lift_coef)
    grad_z = derivative(field, 3, diff, lift_coef)
    advect = -(field[0:1] * grad_x + field[1:2] * grad_y + field[2:3] * grad_z)
    viscous = derivative(grad_x, 1, diff, lift_coef) + derivative(grad_y, 2, diff, lift_coef) + derivative(grad_z, 3, diff, lift_coef)
    return advect + VISCOSITY * viscous


def quadrature(rates, which):
    weight_row = QUAD_WEIGHTS[which]
    return weight_row[0] * rates[0] + weight_row[1] * rates[1] + weight_row[2] * rates[2]


def sdc_sweep(start, old_rates, start_rate, rate_fn, fas_terms, need_last):
    states = [start]
    rates = [start_rate]
    for which in range(2):
        advanced = states[which] + (TIME_STEP / 2.0) * (rates[which] - old_rates[which]) + TIME_STEP * quadrature(old_rates, which)
        if fas_terms is not None:
            advanced = advanced + fas_terms[which]
        states.append(advanced)
        if which == 0 or need_last:
            rates.append(rate_fn(advanced))
    return states, rates


def bricks_to_grid(field):
    chans, bricks, side, unused_side, depth = field.shape
    rows = bricks // YBRICKS
    blocked = field.reshape(chans, rows, YBRICKS, side, side, depth).transpose(0, 1, 3, 2, 4, 5)
    return blocked.reshape(chans, rows * side, YBRICKS * side, depth)


def grid_to_bricks(field, side):
    chans, width_x, width_y, depth = field.shape
    rows = width_x // side
    blocked = field.reshape(chans, rows, side, YBRICKS, side, depth).transpose(0, 1, 3, 2, 4, 5)
    return blocked.reshape(chans, rows * YBRICKS, side, side, depth)


def reference(initial):
    fine_points, fine_weights = cheb_tables(16)
    coarse_points, coarse_weights = cheb_tables(8)
    fine_diff = jnp.asarray(diff_matrix(fine_points, fine_weights), jnp.float32)
    coarse_diff = jnp.asarray(diff_matrix(coarse_points, coarse_weights), jnp.float32)
    restrict_mat = jnp.asarray(interp_matrix(fine_points, fine_weights, coarse_points), jnp.float32)
    prolong_mat = jnp.asarray(interp_matrix(coarse_points, coarse_weights, fine_points), jnp.float32)
    fine_lift = 15.0 ** 2 / 2.0
    coarse_lift = 7.0 ** 2 / 2.0
    side = initial.shape[3]

    def fine_rate(field):
        return tendency(field, fine_diff, fine_lift)

    def coarse_rate(field):
        return tendency(field, coarse_diff, coarse_lift)

    def restrict(field):
        return apply_along(apply_along(apply_along(field, restrict_mat, 1), restrict_mat, 2), restrict_mat, 3)

    def prolong(field):
        return apply_along(apply_along(apply_along(field, prolong_mat, 3), prolong_mat, 2), prolong_mat, 1)

    results = []
    prev_coarse = None
    prev_fine = None
    for slice_index in range(N_TM):
        start_state = bricks_to_grid(initial[slice_index])
        first_rate = fine_rate(start_state)
        fine_one, fine_rates = sdc_sweep(start_state, [first_rate, first_rate, first_rate], first_rate, fine_rate, None, True)
        coarse_nodes = [restrict(state) for state in fine_one]
        coarse_rates = [coarse_rate(state) for state in coarse_nodes]
        fas_terms = [restrict(TIME_STEP * quadrature(fine_rates, which)) - TIME_STEP * quadrature(coarse_rates, which) for which in range(2)]
        if slice_index == 0:
            coarse_start = restrict(start_state)
            fine_start = start_state
        else:
            coarse_start = prev_coarse
            fine_start = prev_fine
        coarse_out, unused_rates = sdc_sweep(coarse_start, coarse_rates, coarse_rate(coarse_start), coarse_rate, fas_terms, False)
        prev_coarse = coarse_out[2]
        prev_fine = fine_one[2]
        node_zero = fine_start + prolong(coarse_out[0] - restrict(fine_start))
        node_one = fine_one[1] + prolong(coarse_out[1] - coarse_nodes[1])
        node_two = fine_one[2] + prolong(coarse_out[2] - coarse_nodes[2])
        new_rates = [fine_rate(node_zero), fine_rate(node_one), fine_rate(node_two)]
        fine_two, unused_fine = sdc_sweep(node_zero, new_rates, new_rates[0], fine_rate, None, False)
        results.append(grid_to_bricks(fine_two[2], side))
    return jnp.stack(results)
```

```python
import functools

import jax
import jax.numpy as jnp
import ml_dtypes
import numpy as np
from jax import lax
from jax.experimental import pallas as pl
from jax.experimental.pallas import tpu as pltpu
from jax.sharding import PartitionSpec as P

H = 0.001
NU = 0.05
W0 = (5.0 / 24.0, 1.0 / 3.0, -1.0 / 24.0)
W1 = (-1.0 / 24.0, 1.0 / 3.0, 5.0 / 24.0)
F32 = jnp.float32
BF = jnp.bfloat16
AX = ("tm", "space")


def cheb_tables(count):
    index = np.arange(count)
    points = -np.cos(np.pi * index / (count - 1))
    weights = (-1.0) ** index
    weights[0] = weights[0] * 0.5
    weights[-1] = weights[-1] * 0.5
    return points, weights


def diff_matrix(points, weights):
    count = points.shape[0]
    ident = np.eye(count)
    gaps = points[:, None] - points[None, :] + ident
    matrix = weights[None, :] / weights[:, None] / gaps
    matrix = matrix * (1.0 - ident)
    return matrix - ident * matrix.sum(axis=1)[:, None]


def interp_matrix(points, weights, targets):
    gaps = targets[:, None] - points[None, :]
    exact_hit = np.abs(gaps) < 1e-12
    safe_gaps = np.where(exact_hit, 1.0, gaps)
    terms = weights[None, :] / safe_gaps
    matrix = terms / terms.sum(axis=1, keepdims=True)
    any_hit = exact_hit.any(axis=1)
    return np.where(any_hit[:, None], np.where(exact_hit, 1.0, 0.0), matrix)


def lifted_matrix(count, length, periodic):
    points, weights = cheb_tables(count)
    matrix = np.kron(np.eye(length // count), diff_matrix(points, weights))
    lift = (count - 1) ** 2 / 2.0
    for place in range(length):
        if place % count == 0:
            matrix[place, place] += lift
            if place > 0:
                matrix[place, place - 1] -= lift
            elif periodic:
                matrix[place, length - 1] -= lift
        if place % count == count - 1:
            matrix[place, place] -= lift
            if place < length - 1:
                matrix[place, place + 1] += lift
            elif periodic:
                matrix[place, 0] += lift
    return matrix


def hilo(matrix):
    hi = matrix.astype(ml_dtypes.bfloat16)
    lo = (matrix - hi.astype(np.float64)).astype(ml_dtypes.bfloat16)
    return hi, lo


def level_ops(n, zlen):
    m = lifted_matrix(n, n, False)
    c = (n - 1) ** 2 / 2.0
    eye = np.eye(n)
    e0, e1 = eye[:, :1], eye[:, -1:]
    mm = m @ m - c * c * (e0 @ e0.T + e1 @ e1.T)
    a = np.concatenate([np.kron(m, eye), np.kron(eye, m), NU * (np.kron(mm, eye) + np.kron(eye, mm))])
    zero = np.zeros((n, 1))
    gb, ga = -c * e0, c * e1
    lb = [-c * NU * m[:, :1], -c * NU * e0]
    la = [c * NU * m[:, -1:], c * NU * e1]

    def bx(col):
        return np.kron(col, eye)

    def by(col):
        return np.kron(eye, col)

    hx = np.concatenate([bx(gb), bx(zero), bx(ga), bx(zero), by(zero), by(zero), by(zero), by(zero)], 1)
    hy = np.concatenate([bx(zero), bx(zero), bx(zero), bx(zero), by(gb), by(zero), by(ga), by(zero)], 1)
    hl = np.concatenate([bx(lb[0]), bx(lb[1]), bx(la[0]), bx(la[1]), by(lb[0]), by(lb[1]), by(la[0]), by(la[1])], 1)
    h = np.concatenate([hx, hy, hl])
    z = lifted_matrix(n, zlen, True)
    return m, a, h, z.T, NU * (z @ z).T


def faces_matrix(rows_val, rows_par, n_in):
    eye = np.eye(n_in)
    out = []
    for side in (0, 1):
        out += [np.kron(rows_val[side][None], eye), np.kron(rows_par[side][None], eye)]
    for side in (0, 1):
        out += [np.kron(eye, rows_val[side][None]), np.kron(eye, rows_par[side][None])]
    return np.concatenate(out)


def tables():
    fp, fw = cheb_tables(16)
    cp, cw = cheb_tables(8)
    r = interp_matrix(fp, fw, cp)
    p = interp_matrix(cp, cw, fp)
    t = {}
    m, a, h, zg, zl = level_ops(16, 128)
    t["fa"] = a
    t["fh"] = h[256:]
    t["fz"] = np.concatenate([zg, zl], 1)
    part = faces_matrix((m[0] * 0, m[0] * 0), (m[0], m[-1]), 16)
    t["fe"] = np.concatenate([part[16:32], part[48:64], part[80:96], part[112:128]])
    mc, ac, hc, zgc, zlc = level_ops(8, 64)
    t["ca"] = np.concatenate([ac, hc], 1)
    two = np.eye(2)
    t["cg"] = np.kron(two, zgc)
    t["cl"] = np.kron(two, zlc)
    e8 = np.eye(8)
    t["cf"] = faces_matrix((e8[0], e8[-1]), (mc[0], mc[-1]), 8)
    mp = m @ p
    t["xf"] = faces_matrix((p[0], p[-1]), (mp[0], mp[-1]), 8)
    t["rxy"] = np.kron(r, r)
    t["rz"] = np.kron(np.eye(8), r).T
    t["pxy"] = np.kron(p, p)
    t["pz"] = np.kron(np.eye(8), p).T
    t["ph"] = np.kron(np.eye(8), p)
    return {k: hilo(v) for k, v in t.items()}


def split(x):
    hi = x.astype(BF)
    lo = (x - hi.astype(F32)).astype(BF)
    return hi, lo


def mm(a, b):
    return jnp.dot(a, b, preferred_element_type=F32)


def ldot(t, x):
    th, tl = t[0][...], t[1][...]
    xh, xl = split(x)
    return mm(th, xh) + (mm(tl, xh) + mm(th, xl))


def rdot(x, t):
    th, tl = t[0][...], t[1][...]
    xh, xl = split(x)
    return mm(xh, th) + (mm(xh, tl) + mm(xl, th))


def cat3(v):
    return jnp.concatenate([v[0], v[1], v[2]], axis=1)


def cut3(x, width=128):
    return [x[:, i * width : (i + 1) * width] for i in range(3)]


def fine_local(v, fa, fz):
    g = ldot(fa, cat3(v))
    z = rdot(jnp.concatenate(v, axis=0), fz)
    out = []
    for c in range(3):
        s = slice(128 * c, 128 * c + 128)
        zc = z[256 * c : 256 * c + 256]
        adv = v[0] * g[0:256, s] + v[1] * g[256:512, s] + v[2] * zc[:, :128]
        out.append(g[512:768, s] + zc[:, 128:] - adv)
    return out


def fine_halo(v, halo, fh):
    k = ldot(fh, cat3(halo))
    c = 112.5
    out = []
    for i in range(3):
        s = slice(128 * i, 128 * i + 128)
        r = k[256:512, s] - v[1] * k[0:256, s]
        first = r[0:16] + c * v[0][0:16] * halo[i][0:16]
        last = r[240:256] - c * v[0][240:256] * halo[i][32:48]
        out.append(jnp.concatenate([first, r[16:240], last], axis=0))
    return out


def halo_of(flags, h, c, lo, hi):
    p1, p2, c1, c2 = [r[c, lo:hi] for r in h]
    rodd, codd = flags[1] == 1, flags[2] == 1
    return jnp.concatenate(
        [jnp.where(rodd, p1, p2), jnp.where(rodd, p2, p1), jnp.where(codd, c1, c2), jnp.where(codd, c2, c1)], axis=0
    )


def send_faces(flags, outs, c, rows, xlo, xhi, ylo, yhi):
    rodd, codd = flags[1] == 1, flags[2] == 1
    outs[0][c, rows] = jnp.where(rodd, xlo, xhi)
    outs[1][c, rows] = jnp.where(rodd, xhi, xlo)
    outs[2][c, rows] = jnp.where(codd, ylo, yhi)
    outs[3][c, rows] = jnp.where(codd, yhi, ylo)


def fine_faces(flags, outs, vref, fe):
    v = [vref[c] for c in range(3)]
    part = ldot(fe, cat3(v))
    for c in range(3):
        pc = part[:, 128 * c : 128 * c + 128]
        send_faces(
            flags, outs, c, slice(0, 16),
            v[c][0:16], v[c][240:256],
            vref[c, pl.ds(0, 16, stride=16), :], vref[c, pl.ds(15, 16, stride=16), :],
        )
        send_faces(flags, outs, c, slice(16, 32), pc[0:16], pc[16:32], pc[32:48], pc[48:64])


def coarse_faces(flags, outs, rows, e, cf):
    for c in range(3):
        f = ldot(cf, e[c])
        send_faces(flags, outs, c, rows, f[0:16], f[16:32], f[32:48], f[48:64])


def coarse_rate(w, halo, ca, cg, cl):
    g = [ldot(ca, jnp.concatenate([w[c], halo[c]], axis=0)) for c in range(3)]
    all_w = jnp.concatenate(w, axis=0)
    gz = rdot(all_w, cg)
    lz = rdot(all_w, cl)
    out = []
    for c in range(3):
        s = slice(64 * c, 64 * c + 64)
        adv = w[0] * g[c][0:64] + w[1] * g[c][64:128] + w[2] * gz[s]
        out.append(g[c][128:192] + lz[s] - adv)
    return out


def restrict(v, rxy, rz):
    s = ldot(rxy, cat3(v))
    r = rdot(jnp.concatenate(cut3(s), axis=0), rz)
    return [r[64 * c : 64 * c + 64] for c in range(3)]


def prolong(e, pxy, pz):
    s = rdot(jnp.concatenate(e, axis=0), pz)
    return cut3(ldot(pxy, jnp.concatenate([s[0:64], s[64:128], s[128:192]], axis=1)))


def wide(x):
    return jnp.concatenate([x, x], axis=1)


def load3(r):
    return [r[c] for c in range(3)]


def store3(r, v):
    for c in range(3):
        r[c] = v[c]


def k_start(flags, v, feh, fel, *outs):
    fine_faces(flags, outs, v, (feh, fel))


def k_bulk1(v, fah, fal, fzh, fzl, out):
    store3(out, fine_local(load3(v), (fah, fal), (fzh, fzl)))


def k_post1(flags, v, loc, h1, h2, h3, h4, fhh, fhl, feh, fel, f0, v1, *outs):
    h = (h1, h2, h3, h4)
    halo = [halo_of(flags, h, c, 0, 32) for c in range(3)]
    vv = load3(v)
    add = fine_halo(vv, halo, (fhh, fhl))
    for c in range(3):
        f = loc[c] + add[c]
        f0[c] = f
        v1[c] = vv[c] + (H / 2.0) * f
    fine_faces(flags, outs, v1, (feh, fel))


def k_bulk2(flags, v, q, fah, fal, fzh, fzl, rxh, rxl, rzh, rzl, cfh, cfl, out, w, *outs):
    vv = load3(v)
    store3(out, fine_local(vv, (fah, fal), (fzh, fzl)))
    w0 = restrict(load3(q), (rxh, rxl), (rzh, rzl))
    w1 = restrict(vv, (rxh, rxl), (rzh, rzl))
    both = [jnp.concatenate([w0[c], w1[c]], axis=1) for c in range(3)]
    store3(w, both)
    coarse_faces(flags, outs, slice(0, 16), both, (cfh, cfl))


def k_post2(flags, v, loc, h1, h2, h3, h4, d1, d2, d3, d4, fhh, fhl, feh, fel, b1, v2, *outs):
    h = (h1, h2, h3, h4)
    halo = [halo_of(flags, h, c, 0, 32) for c in range(3)]
    vv = load3(v)
    add = fine_halo(vv, halo, (fhh, fhl))
    for c in range(3):
        f = loc[c] + add[c]
        b1[c] = f
        v2[c] = vv[c] + (H / 2.0) * f
    fine_faces(flags, outs, v2, (feh, fel))
    for o, d in zip(outs, (d1, d2, d3, d4)):
        for c in range(3):
            o[c, 32:48] = d[c]


def k_bulk3(v, f0, b1, fah, fal, fzh, fzl, rxh, rxl, rzh, rzl, out, w2, ta, tb):
    vv = load3(v)
    store3(out, fine_local(vv, (fah, fal), (fzh, fzl)))
    store3(w2, restrict(vv, (rxh, rxl), (rzh, rzl)))
    rf = restrict(load3(f0), (rxh, rxl), (rzh, rzl))
    rb = restrict(load3(b1), (rxh, rxl), (rzh, rzl))
    for c in range(3):
        ta[c] = (H * W0[0]) * rf[c] + (H * W0[1]) * rb[c]
        tb[c] = (H * W1[0]) * rf[c] + (H * W1[1]) * rb[c]


def k_post3(flags, v, loc, h1, h2, h3, h4, w, ta, tb, fhh, fhl, rxh, rxl, rzh, rzl, cah, cal, cgh, cgl, clh, cll,
            cfh, cfl, e1, r0, r1, vh, *outs):
    h = (h1, h2, h3, h4)
    halo = [halo_of(flags, h, c, 0, 32) for c in range(3)]
    vv = load3(v)
    add = fine_halo(vv, halo, (fhh, fhl))
    b2 = [loc[c] + add[c] for c in range(3)]
    rb = restrict(b2, (rxh, rxl), (rzh, rzl))
    ww = load3(w)
    chalo = [halo_of(flags, h, c, 32, 48) for c in range(3)]
    cr = coarse_rate(ww, chalo, (cah, cal), (cgh, cgl), (clh, cll))
    first = []
    for c in range(3):
        t0 = ta[c] + (H * W0[2]) * rb[c]
        t1 = tb[c] + (H * W1[2]) * rb[c]
        r0[c] = t0 - (H / 2.0) * cr[c][:, :64]
        r1[c] = t1 - (H / 2.0) * cr[c][:, 64:]
        first.append(ww[c][:, :64] + t0)
        e1[c] = first[c]
        vh[c, 0:256] = vv[c]
        vh[c, 256:384] = halo[c]
    coarse_faces(flags, outs, slice(0, 16), first, (cfh, cfl))


def k_chain(flags, e, h1, h2, h3, h4, r, first, cah, cal, cgh, cgl, clh, cll, cfh, cfl, out, *outs, use_first):
    h = (h1, h2, h3, h4)
    ee = load3(e)
    halo = [halo_of(flags, h, c, 0, 16) for c in range(3)]
    rate = coarse_rate([wide(x) for x in ee], [wide(x) for x in halo], (cah, cal), (cgh, cgl), (clh, cll))
    new = []
    for c in range(3):
        n = ee[c] + (H / 2.0) * rate[c][:, :64] + r[c]
        if use_first:
            n = jnp.where(flags[0] == 1, first[c], n)
        new.append(n)
        out[c] = n
    if outs:
        coarse_faces(flags, outs, slice(0, 16), new, (cfh, cfl))


def k_dstart(flags, k, e1, e2, w, w2, ws, xfh, xfl, de, *outs):
    first = flags[0] == 1
    for c in range(3):
        d0 = jnp.where(first, 0.0, k[c] - ws[c])
        d1 = e1[c] - w[c][:, 64:]
        d2 = e2[c] - w2[c]
        de[0, c] = d0
        de[1, c] = d1
        de[2, c] = d2
        f = ldot((xfh, xfl), jnp.concatenate([d0, d1], axis=1))
        g = ldot((xfh, xfl), d2)
        send_faces(flags, outs, c, slice(0, 16), f[0:16], f[16:32], f[32:48], f[48:64])
        send_faces(flags, outs, c, slice(16, 32), *[wide(g[16 * i : 16 * i + 16]) for i in range(4)])


def k_ws(vh, rxh, rxl, rzh, rzl, ws):
    store3(ws, restrict([vh[c, 0:256] for c in range(3)], (rxh, rxl), (rzh, rzl)))


def k_xbulk(flags, de, q, v1, v2, vh, fah, fal, fzh, fzl, pxh, pxl, pzh, pzl, x, loc):
    first = flags[0] == 1
    for m in range(3):
        pr = prolong([de[m, c] for c in range(3)], (pxh, pxl), (pzh, pzl))
        xs = []
        for c in range(3):
            if m == 0:
                base = jnp.where(first, q[c], vh[c, 0:256])
            else:
                base = (v1 if m == 1 else v2)[c]
            xs.append(base + pr[c])
            x[m, c] = xs[c]
        lo = fine_local(xs, (fah, fal), (fzh, fzl))
        for c in range(3):
            loc[m, c] = lo[c]


def k_xpost(flags, x, loc, h1, h2, h3, h4, a1, a2, a3, a4, b1, b2, b3, b4, v2h, vh, fhh, fhl, feh, fel, pzh, pzl,
            phh, phl, u1, d, *outs):
    first = flags[0] == 1
    h = (h1, h2, h3, h4)
    g = []
    lo = [halo_of(flags, h, c, 0, 16) for c in range(3)]
    hi = [halo_of(flags, h, c, 16, 32) for c in range(3)]
    for m in range(3):
        co = [lo[c][:, :64] if m == 0 else lo[c][:, 64:] if m == 1 else hi[c][:, :64] for c in range(3)]
        s = rdot(jnp.concatenate(co, axis=0), (pzh, pzl))
        fine = cut3(ldot((phh, phl), jnp.concatenate([s[0:64], s[64:128], s[128:192]], axis=1)))
        halo = []
        for c in range(3):
            if m == 0:
                base = jnp.where(first, halo_of(flags, (a1, a2, a3, a4), c, 0, 32), vh[c, 256:384])
            elif m == 1:
                base = halo_of(flags, (b1, b2, b3, b4), c, 0, 32)
            else:
                base = v2h[c, 256:384]
            halo.append(base + fine[c])
        xs = [x[m, c] for c in range(3)]
        add = fine_halo(xs, halo, (fhh, fhl))
        g.append([loc[m, c] + add[c] for c in range(3)])
    for c in range(3):
        u = x[0, c] + H * (W0[0] * g[0][c] + W0[1] * g[1][c] + W0[2] * g[2][c])
        u1[c] = u
        d[c] = u + H * (W1[0] * g[0][c] + (W1[1] - 0.5) * g[1][c] + W1[2] * g[2][c])
    fine_faces(flags, outs, u1, (feh, fel))


def k_last(flags, v, d, loc, h1, h2, h3, h4, fhh, fhl, out):
    h = (h1, h2, h3, h4)
    halo = [halo_of(flags, h, c, 0, 32) for c in range(3)]
    add = fine_halo(load3(v), halo, (fhh, fhl))
    for c in range(3):
        out[c] = d[c] + (H / 2.0) * (loc[c] + add[c])


def call(kernel, args, outs, cost=0):
    flat = []
    for a in args:
        if isinstance(a, tuple):
            flat += list(a)
        else:
            flat.append(a)
    specs = [
        pl.BlockSpec(memory_space=pltpu.SMEM if a.dtype == jnp.int32 else pltpu.VMEM) for a in flat
    ]
    shapes = [jax.ShapeDtypeStruct(s, F32) for s in outs]
    size = sum(int(np.prod(a.shape)) * a.dtype.itemsize for a in flat) + sum(int(np.prod(s)) * 4 for s in outs)
    return pl.pallas_call(
        kernel,
        out_shape=shapes,
        in_specs=specs,
        out_specs=[pl.BlockSpec(memory_space=pltpu.VMEM) for _ in outs],
        cost_estimate=pl.CostEstimate(flops=cost, bytes_accessed=size, transcendentals=0),
        compiler_params=pltpu.CompilerParams(vmem_limit_bytes=48 * 1024 * 1024),
    )(*flat)


def routes(shift):
    def dev(t, r, c):
        return t * 64 + (r % 16) * 4 + c % 4

    out = []
    for kind in range(4):
        pairs = []
        for t in range(4):
            if not 0 <= t + shift < 4:
                continue
            for r in range(16):
                for c in range(4):
                    if kind == 0:
                        to = (r ^ 1, c)
                    elif kind == 1:
                        to = (r + 1 if r & 1 else r - 1, c)
                    elif kind == 2:
                        to = (r, c ^ 1)
                    else:
                        to = (r, c + 1 if c & 1 else c - 1)
                    pairs.append((dev(t, r, c), dev(t + shift, *to)))
        out.append(pairs)
    return out


def shards(initial):
    tab = {k: (jnp.asarray(a), jnp.asarray(b)) for k, (a, b) in tables().items()}
    space = lax.axis_index("space")
    flags = jnp.stack([
        (lax.axis_index("tm") == 0).astype(jnp.int32), (space // 4) % 2, space % 2, jnp.zeros((), jnp.int32)
    ]).astype(jnp.int32)
    here = routes(0)
    on = routes(1)
    same = [(t * 64 + b, t * 64 + 64 + b) for t in range(3) for b in range(64)]

    def swap(pieces, way):
        return [lax.ppermute(p, AX, w) for p, w in zip(pieces, way)]

    st, pay, co = (3, 256, 128), (3, 32, 128), (3, 64, 64)
    cpay, c2pay, bpay = (3, 16, 64), (3, 16, 128), (3, 48, 128)
    q = initial.reshape(st)
    big = 2_000_000_000
    p = call(k_start, [flags, q, tab["fe"]], [pay] * 4)
    h1 = swap(p, here)
    (loc,) = call(k_bulk1, [q, tab["fa"], tab["fz"]], [st], big)
    f0, v1, *p = call(k_post1, [flags, q, loc, *h1, tab["fh"], tab["fe"]], [st, st] + [pay] * 4)
    h2 = swap(p, here)
    loc, w, *cp = call(
        k_bulk2, [flags, v1, q, tab["fa"], tab["fz"], tab["rxy"], tab["rz"], tab["cf"]],
        [st, (3, 64, 128)] + [c2pay] * 4, big,
    )
    b1, v2, *p = call(k_post2, [flags, v1, loc, *h2, *cp, tab["fh"], tab["fe"]], [st, st] + [bpay] * 4)
    h3 = swap(p, here)
    loc, w2, ta, tb = call(
        k_bulk3, [v2, f0, b1, tab["fa"], tab["fz"], tab["rxy"], tab["rz"]], [st, co, co, co], big
    )
    coarse = [tab["ca"], tab["cg"], tab["cl"], tab["cf"]]
    first, r0, r1, vh, *p = call(
        k_post3,
        [flags, v2, loc, *h3, w, ta, tb, tab["fh"], tab["rxy"], tab["rz"], *coarse],
        [co, co, co, (3, 384, 128)] + [cpay] * 4,
    )
    vprev = lax.ppermute(vh, AX, same)
    (ws,) = call(k_ws, [vprev, tab["rxy"], tab["rz"]], [co])
    e1 = first
    k = first
    for s in range(4):
        h = swap(p, here)
        res = call(
            functools.partial(k_chain, use_first=False), [flags, e1, *h, r1, first, *coarse],
            [co] + ([cpay] * 4 if s < 3 else []),
        )
        e2 = res[0]
        if s < 3:
            h = swap(res[1:], on)
            k = lax.ppermute(e2, AX, same)
            e1, *p = call(
                functools.partial(k_chain, use_first=True), [flags, k, *h, r0, first, *coarse], [co] + [cpay] * 4
            )
    de, *p = call(k_dstart, [flags, k, e1, e2, w, w2, ws, tab["xf"]], [(3, 3, 64, 64)] + [pay] * 4)
    h = swap(p, here)
    x, loc = call(
        k_xbulk, [flags, de, q, v1, v2, vprev, tab["fa"], tab["fz"], tab["pxy"], tab["pz"]],
        [(3, 3, 256, 128)] * 2, 3 * big,
    )
    u1, d, *p = call(
        k_xpost, [flags, x, loc, *h, *h1, *h2, vh, vprev, tab["fh"], tab["fe"], tab["pz"], tab["ph"]],
        [st, st] + [pay] * 4,
    )
    h = swap(p, here)
    (loc,) = call(k_bulk1, [u1, tab["fa"], tab["fz"]], [st], big)
    (out,) = call(k_last, [flags, u1, d, loc, *h, tab["fh"]], [st])
    return out.reshape(initial.shape)


def solution(mesh):
    return jax.shard_map(
        shards,
        mesh=mesh,
        in_specs=(P("tm", None, "space", None, None, None),),
        out_specs=P("tm", None, "space", None, None, None),
        check_vma=False,
    )
```

```python
import functools

import jax
import jax.numpy as jnp
import ml_dtypes
import numpy as np
from jax import lax
from jax.experimental import pallas as pl
from jax.experimental.pallas import tpu as pltpu
from jax.sharding import PartitionSpec as P

H = 0.001
NU = 0.05
W0 = (5.0 / 24.0, 1.0 / 3.0, -1.0 / 24.0)
W1 = (-1.0 / 24.0, 1.0 / 3.0, 5.0 / 24.0)
F32 = jnp.float32
BF = jnp.bfloat16
AX = ("tm", "space")


def cheb_tables(count):
    index = np.arange(count)
    points = -np.cos(np.pi * index / (count - 1))
    weights = (-1.0) ** index
    weights[0] = weights[0] * 0.5
    weights[-1] = weights[-1] * 0.5
    return points, weights


def diff_matrix(points, weights):
    count = points.shape[0]
    ident = np.eye(count)
    gaps = points[:, None] - points[None, :] + ident
    matrix = weights[None, :] / weights[:, None] / gaps
    matrix = matrix * (1.0 - ident)
    return matrix - ident * matrix.sum(axis=1)[:, None]


def interp_matrix(points, weights, targets):
    gaps = targets[:, None] - points[None, :]
    exact_hit = np.abs(gaps) < 1e-12
    safe_gaps = np.where(exact_hit, 1.0, gaps)
    terms = weights[None, :] / safe_gaps
    matrix = terms / terms.sum(axis=1, keepdims=True)
    any_hit = exact_hit.any(axis=1)
    return np.where(any_hit[:, None], np.where(exact_hit, 1.0, 0.0), matrix)


def lifted_matrix(count, length, periodic):
    points, weights = cheb_tables(count)
    matrix = np.kron(np.eye(length // count), diff_matrix(points, weights))
    lift = (count - 1) ** 2 / 2.0
    for place in range(length):
        if place % count == 0:
            matrix[place, place] += lift
            if place > 0:
                matrix[place, place - 1] -= lift
            elif periodic:
                matrix[place, length - 1] -= lift
        if place % count == count - 1:
            matrix[place, place] -= lift
            if place < length - 1:
                matrix[place, place + 1] += lift
            elif periodic:
                matrix[place, 0] += lift
    return matrix


def hilo(matrix):
    hi = matrix.astype(ml_dtypes.bfloat16)
    lo = (matrix - hi.astype(np.float64)).astype(ml_dtypes.bfloat16)
    return hi, lo


def level_ops(n, zlen):
    m = lifted_matrix(n, n, False)
    c = (n - 1) ** 2 / 2.0
    eye = np.eye(n)
    e0, e1 = eye[:, :1], eye[:, -1:]
    mm = m @ m - c * c * (e0 @ e0.T + e1 @ e1.T)
    a = np.concatenate([np.kron(m, eye), np.kron(eye, m), NU * (np.kron(mm, eye) + np.kron(eye, mm))])
    zero = np.zeros((n, 1))
    gb, ga = -c * e0, c * e1
    lb = [-c * NU * m[:, :1], -c * NU * e0]
    la = [c * NU * m[:, -1:], c * NU * e1]

    def bx(col):
        return np.kron(col, eye)

    def by(col):
        return np.kron(eye, col)

    hx = np.concatenate([bx(gb), bx(zero), bx(ga), bx(zero), by(zero), by(zero), by(zero), by(zero)], 1)
    hy = np.concatenate([bx(zero), bx(zero), bx(zero), bx(zero), by(gb), by(zero), by(ga), by(zero)], 1)
    hl = np.concatenate([bx(lb[0]), bx(lb[1]), bx(la[0]), bx(la[1]), by(lb[0]), by(lb[1]), by(la[0]), by(la[1])], 1)
    h = np.concatenate([hx, hy, hl])
    z = lifted_matrix(n, zlen, True)
    return m, a, h, z.T, NU * (z @ z).T


def faces_matrix(rows_val, rows_par, n_in):
    eye = np.eye(n_in)
    out = []
    for side in (0, 1):
        out += [np.kron(rows_val[side][None], eye), np.kron(rows_par[side][None], eye)]
    for side in (0, 1):
        out += [np.kron(eye, rows_val[side][None]), np.kron(eye, rows_par[side][None])]
    return np.concatenate(out)


def tables():
    fp, fw = cheb_tables(16)
    cp, cw = cheb_tables(8)
    r = interp_matrix(fp, fw, cp)
    p = interp_matrix(cp, cw, fp)
    t = {}
    m, a, h, zg, zl = level_ops(16, 128)
    t["fa"] = a
    t["fh"] = h[256:]
    t["fz"] = np.concatenate([zg, zl], 1)
    part = faces_matrix((m[0] * 0, m[0] * 0), (m[0], m[-1]), 16)
    t["fe"] = np.concatenate([part[16:32], part[48:64], part[80:96], part[112:128]])
    mc, ac, hc, zgc, zlc = level_ops(8, 64)
    t["ca"] = np.concatenate([ac, hc], 1)
    two = np.eye(2)
    t["cg"] = np.kron(two, zgc)
    t["cl"] = np.kron(two, zlc)
    e8 = np.eye(8)
    t["cf"] = faces_matrix((e8[0], e8[-1]), (mc[0], mc[-1]), 8)
    mp = m @ p
    t["xf"] = faces_matrix((p[0], p[-1]), (mp[0], mp[-1]), 8)
    t["rxy"] = np.kron(r, r)
    t["rz"] = np.kron(np.eye(8), r).T
    t["pxy"] = np.kron(p, p)
    t["pz"] = np.kron(np.eye(8), p).T
    t["ph"] = np.kron(np.eye(8), p)
    return {k: hilo(v) for k, v in t.items()}


def split(x):
    hi = x.astype(BF)
    lo = (x - hi.astype(F32)).astype(BF)
    return hi, lo


def mm(a, b):
    return jnp.dot(a, b, preferred_element_type=F32)


def ldot(t, x):
    th, tl = t[0][...], t[1][...]
    xh, xl = split(x)
    return mm(th, xh) + (mm(tl, xh) + mm(th, xl))


def rdot(x, t):
    th, tl = t[0][...], t[1][...]
    xh, xl = split(x)
    return mm(xh, th) + (mm(xh, tl) + mm(xl, th))


def cat3(v):
    return jnp.concatenate([v[0], v[1], v[2]], axis=1)


def cut3(x, width=128):
    return [x[:, i * width : (i + 1) * width] for i in range(3)]


def fine_local(v, fa, fz):
    g = ldot(fa, cat3(v))
    z = rdot(jnp.concatenate(v, axis=0), fz)
    out = []
    for c in range(3):
        s = slice(128 * c, 128 * c + 128)
        zc = z[256 * c : 256 * c + 256]
        adv = v[0] * g[0:256, s] + v[1] * g[256:512, s] + v[2] * zc[:, :128]
        out.append(g[512:768, s] + zc[:, 128:] - adv)
    return out


def fine_halo(v, halo, fh):
    k = ldot(fh, cat3(halo))
    c = 112.5
    out = []
    for i in range(3):
        s = slice(128 * i, 128 * i + 128)
        r = k[256:512, s] - v[1] * k[0:256, s]
        first = r[0:16] + c * v[0][0:16] * halo[i][0:16]
        last = r[240:256] - c * v[0][240:256] * halo[i][32:48]
        out.append(jnp.concatenate([first, r[16:240], last], axis=0))
    return out


def halo_of(flags, h, c, lo, hi):
    p1, p2, c1, c2 = [r[c, lo:hi] for r in h]
    rodd, codd = flags[1] == 1, flags[2] == 1
    return jnp.concatenate(
        [jnp.where(rodd, p1, p2), jnp.where(rodd, p2, p1), jnp.where(codd, c1, c2), jnp.where(codd, c2, c1)], axis=0
    )


def send_faces(flags, outs, c, rows, xlo, xhi, ylo, yhi):
    rodd, codd = flags[1] == 1, flags[2] == 1
    outs[0][c, rows] = jnp.where(rodd, xlo, xhi)
    outs[1][c, rows] = jnp.where(rodd, xhi, xlo)
    outs[2][c, rows] = jnp.where(codd, ylo, yhi)
    outs[3][c, rows] = jnp.where(codd, yhi, ylo)


def fine_faces(flags, outs, vref, fe):
    v = [vref[c] for c in range(3)]
    part = ldot(fe, cat3(v))
    for c in range(3):
        pc = part[:, 128 * c : 128 * c + 128]
        send_faces(
            flags, outs, c, slice(0, 16),
            v[c][0:16], v[c][240:256],
            vref[c, pl.ds(0, 16, stride=16), :], vref[c, pl.ds(15, 16, stride=16), :],
        )
        send_faces(flags, outs, c, slice(16, 32), pc[0:16], pc[16:32], pc[32:48], pc[48:64])


def coarse_faces(flags, outs, rows, e, cf):
    for c in range(3):
        f = ldot(cf, e[c])
        send_faces(flags, outs, c, rows, f[0:16], f[16:32], f[32:48], f[48:64])


def coarse_rate(w, halo, ca, cg, cl):
    g = [ldot(ca, jnp.concatenate([w[c], halo[c]], axis=0)) for c in range(3)]
    all_w = jnp.concatenate(w, axis=0)
    gz = rdot(all_w, cg)
    lz = rdot(all_w, cl)
    out = []
    for c in range(3):
        s = slice(64 * c, 64 * c + 64)
        adv = w[0] * g[c][0:64] + w[1] * g[c][64:128] + w[2] * gz[s]
        out.append(g[c][128:192] + lz[s] - adv)
    return out


def restrict(v, rxy, rz):
    s = ldot(rxy, cat3(v))
    r = rdot(jnp.concatenate(cut3(s), axis=0), rz)
    return [r[64 * c : 64 * c + 64] for c in range(3)]


def prolong(e, pxy, pz):
    s = rdot(jnp.concatenate(e, axis=0), pz)
    return cut3(ldot(pxy, jnp.concatenate([s[0:64], s[64:128], s[128:192]], axis=1)))


def wide(x):
    return jnp.concatenate([x, x], axis=1)


def load3(r):
    return [r[c] for c in range(3)]


def store3(r, v):
    for c in range(3):
        r[c] = v[c]


def k_start(flags, v, feh, fel, *outs):
    fine_faces(flags, outs, v, (feh, fel))


def k_bulk1(v, fah, fal, fzh, fzl, out):
    store3(out, fine_local(load3(v), (fah, fal), (fzh, fzl)))


def k_post1(flags, v, loc, h1, h2, h3, h4, fhh, fhl, feh, fel, f0, v1, *outs):
    h = (h1, h2, h3, h4)
    halo = [halo_of(flags, h, c, 0, 32) for c in range(3)]
    vv = load3(v)
    add = fine_halo(vv, halo, (fhh, fhl))
    for c in range(3):
        f = loc[c] + add[c]
        f0[c] = f
        v1[c] = vv[c] + (H / 2.0) * f
    fine_faces(flags, outs, v1, (feh, fel))


def k_bulk2(flags, v, q, fah, fal, fzh, fzl, rxh, rxl, rzh, rzl, cfh, cfl, out, w, *outs):
    vv = load3(v)
    store3(out, fine_local(vv, (fah, fal), (fzh, fzl)))
    w0 = restrict(load3(q), (rxh, rxl), (rzh, rzl))
    w1 = restrict(vv, (rxh, rxl), (rzh, rzl))
    both = [jnp.concatenate([w0[c], w1[c]], axis=1) for c in range(3)]
    store3(w, both)
    coarse_faces(flags, outs, slice(0, 16), both, (cfh, cfl))


def k_post2(flags, v, loc, h1, h2, h3, h4, d1, d2, d3, d4, fhh, fhl, feh, fel, b1, v2, *outs):
    h = (h1, h2, h3, h4)
    halo = [halo_of(flags, h, c, 0, 32) for c in range(3)]
    vv = load3(v)
    add = fine_halo(vv, halo, (fhh, fhl))
    for c in range(3):
        f = loc[c] + add[c]
        b1[c] = f
        v2[c] = vv[c] + (H / 2.0) * f
    fine_faces(flags, outs, v2, (feh, fel))
    for o, d in zip(outs, (d1, d2, d3, d4)):
        for c in range(3):
            o[c, 32:48] = d[c]


def k_bulk3(v, f0, b1, fah, fal, fzh, fzl, rxh, rxl, rzh, rzl, out, w2, ta, tb):
    vv = load3(v)
    store3(out, fine_local(vv, (fah, fal), (fzh, fzl)))
    store3(w2, restrict(vv, (rxh, rxl), (rzh, rzl)))
    rf = restrict(load3(f0), (rxh, rxl), (rzh, rzl))
    rb = restrict(load3(b1), (rxh, rxl), (rzh, rzl))
    for c in range(3):
        ta[c] = (H * W0[0]) * rf[c] + (H * W0[1]) * rb[c]
        tb[c] = (H * W1[0]) * rf[c] + (H * W1[1]) * rb[c]


def k_post3(flags, v, loc, h1, h2, h3, h4, w, ta, tb, fhh, fhl, rxh, rxl, rzh, rzl, cah, cal, cgh, cgl, clh, cll,
            a, vh):
    h = (h1, h2, h3, h4)
    halo = [halo_of(flags, h, c, 0, 32) for c in range(3)]
    vv = load3(v)
    add = fine_halo(vv, halo, (fhh, fhl))
    b2 = [loc[c] + add[c] for c in range(3)]
    rb = restrict(b2, (rxh, rxl), (rzh, rzl))
    ww = load3(w)
    chalo = [halo_of(flags, h, c, 32, 48) for c in range(3)]
    cr = coarse_rate(ww, chalo, (cah, cal), (cgh, cgl), (clh, cll))
    for c in range(3):
        t0 = ta[c] + (H * W0[2]) * rb[c]
        t1 = tb[c] + (H * W1[2]) * rb[c]
        start = jnp.where(flags[0] == 1, ww[c][:, :64], (-H / 2.0) * cr[c][:, :64])
        a[c] = jnp.concatenate([start + t0, t1 - (H / 2.0) * cr[c][:, 64:]], axis=1)
        vh[c, 0:256] = vv[c]
        vh[c, 256:384] = halo[c]


def k_pair(flags, own, other, d):
    odd = flags[1] == 1
    for c in range(3):
        a = jnp.where(odd, other[c], own[c])
        b = jnp.where(odd, own[c], other[c])
        d[c, 0:64] = jnp.concatenate([a[:, :64], b[:, :64]], axis=1)
        d[c, 64:128] = jnp.concatenate([a[:, 64:], b[:, 64:]], axis=1)


def pair_faces(e, cf, out, up, down, left, right):
    for c in range(3):
        out[c, 0:64] = e[c]
        f = ldot(cf, e[c])
        up[c] = f[0:16, :64]
        down[c] = f[16:32, 64:]
        left[c] = f[32:48]
        right[c] = f[48:64]
        out[c, 64:80] = jnp.concatenate([f[0:16, 64:], f[16:32, :64]], axis=1)


def k_begin(flags, own, other, cfh, cfl, even, odd, *outs):
    second = flags[3] == 1
    e = []
    for c in range(3):
        a = jnp.where(second, other[c], own[c])
        even[c] = a
        odd[c] = jnp.where(second, own[c], other[c])
        e.append(a[0:64])
    pair_faces(e, (cfh, cfl), *outs)


def k_chain(e, up, down, left, right, r, cah, cal, cgh, cgl, clh, cll, cfh, cfl, out, *outs, rows):
    ee = [e[c, 0:64] for c in range(3)]
    halo = []
    for c in range(3):
        i = e[c, 64:80]
        halo.append(jnp.concatenate([
            jnp.concatenate([up[c], i[:, 64:]], axis=1), jnp.concatenate([i[:, :64], down[c]], axis=1), left[c], right[c]
        ], axis=0))
    rate = coarse_rate(ee, halo, (cah, cal), (cgh, cgl), (clh, cll))
    new = [ee[c] + (H / 2.0) * rate[c] + r[c, rows : rows + 64] for c in range(3)]
    if outs:
        pair_faces(new, (cfh, cfl), out, *outs)
    else:
        store3(out, new)


def k_dstart(flags, d, a2e, a1o, a2o, bk, b1e, b2e, b1o, b2o, w, w2, ws, xfh, xfl, de, *outs):
    first, odd, second, late = flags[0] == 1, flags[1] == 1, flags[3] == 1, flags[4] == 1

    def mine(x):
        return jnp.where(odd, x[:, 64:], x[:, :64])

    for c in range(3):
        a2, b2 = a2e[c, 0:64], b2e[c, 0:64]
        k = jnp.where(second, jnp.where(late, b2, a2), bk[c, 0:64])
        e1 = jnp.where(
            late, jnp.where(second, b1o[c, 0:64], b1e[c, 0:64]), jnp.where(second, a1o[c, 0:64], d[c, 0:64])
        )
        e2 = jnp.where(late, jnp.where(second, b2o[c], b2), jnp.where(second, a2o[c, 0:64], a2))
        d0 = jnp.where(first, 0.0, mine(k) - ws[c])
        d1 = mine(e1) - w[c][:, 64:]
        d2 = mine(e2) - w2[c]
        de[0, c] = d0
        de[1, c] = d1
        de[2, c] = d2
        f = ldot((xfh, xfl), jnp.concatenate([d0, d1], axis=1))
        g = ldot((xfh, xfl), d2)
        send_faces(flags, outs, c, slice(0, 16), f[0:16], f[16:32], f[32:48], f[48:64])
        send_faces(flags, outs, c, slice(16, 32), *[wide(g[16 * i : 16 * i + 16]) for i in range(4)])


def k_ws(vh, rxh, rxl, rzh, rzl, ws):
    store3(ws, restrict([vh[c, 0:256] for c in range(3)], (rxh, rxl), (rzh, rzl)))


def k_xbulk(flags, de, q, v1, v2, vh, fah, fal, fzh, fzl, pxh, pxl, pzh, pzl, x, loc):
    first = flags[0] == 1
    for m in range(3):
        pr = prolong([de[m, c] for c in range(3)], (pxh, pxl), (pzh, pzl))
        xs = []
        for c in range(3):
            if m == 0:
                base = jnp.where(first, q[c], vh[c, 0:256])
            else:
                base = (v1 if m == 1 else v2)[c]
            xs.append(base + pr[c])
            x[m, c] = xs[c]
        lo = fine_local(xs, (fah, fal), (fzh, fzl))
        for c in range(3):
            loc[m, c] = lo[c]


def k_xpost(flags, x, loc, h1, h2, h3, h4, a1, a2, a3, a4, b1, b2, b3, b4, v2h, vh, fhh, fhl, feh, fel, pzh, pzl,
            phh, phl, u1, d, *outs):
    first = flags[0] == 1
    h = (h1, h2, h3, h4)
    g = []
    lo = [halo_of(flags, h, c, 0, 16) for c in range(3)]
    hi = [halo_of(flags, h, c, 16, 32) for c in range(3)]
    for m in range(3):
        co = [lo[c][:, :64] if m == 0 else lo[c][:, 64:] if m == 1 else hi[c][:, :64] for c in range(3)]
        s = rdot(jnp.concatenate(co, axis=0), (pzh, pzl))
        fine = cut3(ldot((phh, phl), jnp.concatenate([s[0:64], s[64:128], s[128:192]], axis=1)))
        halo = []
        for c in range(3):
            if m == 0:
                base = jnp.where(first, halo_of(flags, (a1, a2, a3, a4), c, 0, 32), vh[c, 256:384])
            elif m == 1:
                base = halo_of(flags, (b1, b2, b3, b4), c, 0, 32)
            else:
                base = v2h[c, 256:384]
            halo.append(base + fine[c])
        xs = [x[m, c] for c in range(3)]
        add = fine_halo(xs, halo, (fhh, fhl))
        g.append([loc[m, c] + add[c] for c in range(3)])
    for c in range(3):
        u = x[0, c] + H * (W0[0] * g[0][c] + W0[1] * g[1][c] + W0[2] * g[2][c])
        u1[c] = u
        d[c] = u + H * (W1[0] * g[0][c] + (W1[1] - 0.5) * g[1][c] + W1[2] * g[2][c])
    fine_faces(flags, outs, u1, (feh, fel))


def k_last(flags, v, d, loc, h1, h2, h3, h4, fhh, fhl, out):
    h = (h1, h2, h3, h4)
    halo = [halo_of(flags, h, c, 0, 32) for c in range(3)]
    add = fine_halo(load3(v), halo, (fhh, fhl))
    for c in range(3):
        out[c] = d[c] + (H / 2.0) * (loc[c] + add[c])


def call(kernel, args, outs, cost=0):
    flat = []
    for a in args:
        if isinstance(a, tuple):
            flat += list(a)
        else:
            flat.append(a)
    specs = [
        pl.BlockSpec(memory_space=pltpu.SMEM if a.dtype == jnp.int32 else pltpu.VMEM) for a in flat
    ]
    shapes = [jax.ShapeDtypeStruct(s, F32) for s in outs]
    size = sum(int(np.prod(a.shape)) * a.dtype.itemsize for a in flat) + sum(int(np.prod(s)) * 4 for s in outs)
    return pl.pallas_call(
        kernel,
        out_shape=shapes,
        in_specs=specs,
        out_specs=[pl.BlockSpec(memory_space=pltpu.VMEM) for _ in outs],
        cost_estimate=pl.CostEstimate(flops=cost, bytes_accessed=size, transcendentals=0),
        compiler_params=pltpu.CompilerParams(vmem_limit_bytes=48 * 1024 * 1024),
    )(*flat)


def routes(shift):
    def dev(t, r, c):
        return t * 64 + (r % 16) * 4 + c % 4

    out = []
    for kind in range(4):
        pairs = []
        for t in range(4):
            if not 0 <= t + shift < 4:
                continue
            for r in range(16):
                for c in range(4):
                    if kind == 0:
                        to = (r ^ 1, c)
                    elif kind == 1:
                        to = (r + 1 if r & 1 else r - 1, c)
                    elif kind == 2:
                        to = (r, c ^ 1)
                    else:
                        to = (r, c + 1 if c & 1 else c - 1)
                    pairs.append((dev(t, r, c), dev(t + shift, *to)))
        out.append(pairs)
    return out


def ring_routes(late):
    out = []
    for dk, dz in ((-1, 0), (1, 0), (0, -1), (0, 1)):
        pairs = []
        for t in range(4):
            to = t + 2 * late
            if to > 3:
                continue
            for k in range(8):
                for z in range(8):
                    pairs.append((t * 64 + k * 8 + z, to * 64 + ((k + dk) % 8) * 8 + (z + dz) % 8))
        out.append(pairs)
    return out


def shards(initial):
    tab = {k: (jnp.asarray(a), jnp.asarray(b)) for k, (a, b) in tables().items()}
    space, tm = lax.axis_index("space"), lax.axis_index("tm")
    flags = jnp.stack([(tm == 0).astype(jnp.int32), (space // 4) % 2, space % 2, tm % 2, tm // 2]).astype(jnp.int32)
    here = routes(0)
    ring, cross = ring_routes(0), ring_routes(1)
    same = [(t * 64 + b, t * 64 + 64 + b) for t in range(3) for b in range(64)]
    two_on = [(t * 64 + b, t * 64 + 128 + b) for t in range(2) for b in range(64)]
    partner = [(t * 64 + b, (t ^ 1) * 64 + b) for t in range(4) for b in range(64)]

    def swap(pieces, way):
        return [lax.ppermute(p, AX, w) for p, w in zip(pieces, way)]

    st, pay, co, duo = (3, 256, 128), (3, 32, 128), (3, 64, 64), (3, 64, 128)
    c2pay, bpay = (3, 16, 128), (3, 48, 128)
    faces = [(3, 80, 128), (3, 16, 64), (3, 16, 64), (3, 16, 128), (3, 16, 128)]
    q = initial.reshape(st)
    big = 2_000_000_000
    p = call(k_start, [flags, q, tab["fe"]], [pay] * 4)
    h1 = swap(p, here)
    (loc,) = call(k_bulk1, [q, tab["fa"], tab["fz"]], [st], big)
    f0, v1, *p = call(k_post1, [flags, q, loc, *h1, tab["fh"], tab["fe"]], [st, st] + [pay] * 4)
    h2 = swap(p, here)
    loc, w, *cp = call(
        k_bulk2, [flags, v1, q, tab["fa"], tab["fz"], tab["rxy"], tab["rz"], tab["cf"]],
        [st, (3, 64, 128)] + [c2pay] * 4, big,
    )
    b1, v2, *p = call(k_post2, [flags, v1, loc, *h2, *cp, tab["fh"], tab["fe"]], [st, st] + [bpay] * 4)
    h3 = swap(p, here)
    loc, w2, ta, tb = call(
        k_bulk3, [v2, f0, b1, tab["fa"], tab["fz"], tab["rxy"], tab["rz"]], [st, co, co, co], big
    )
    coarse = [tab["ca"], tab["cg"], tab["cl"]]
    a, vh = call(
        k_post3,
        [flags, v2, loc, *h3, w, ta, tb, tab["fh"], tab["rxy"], tab["rz"], *coarse],
        [duo, (3, 384, 128)],
    )
    (mine,) = call(k_pair, [flags, a, lax.ppermute(a, AX, here[0])], [(3, 128, 128)])
    other = lax.ppermute(mine, AX, partner)
    even, odd, e, *p = call(k_begin, [flags, mine, other, tab["cf"]], [(3, 128, 128)] * 2 + faces)
    vprev = lax.ppermute(vh, AX, same)
    (ws,) = call(k_ws, [vprev, tab["rxy"], tab["rz"]], [co])

    def step(e, p, way, r, rows, last=False):
        below, above, right, left = swap(p, way)
        return call(
            functools.partial(k_chain, rows=rows), [e, above, below, left, right, r, *coarse, tab["cf"]], [duo] if last else faces
        )

    a2e, *p = step(e, p, ring, even, 64)
    a1o, *p = step(a2e, p, ring, odd, 0)
    a2o, *p = step(a1o, p, ring, odd, 64)
    bk = lax.ppermute(a2o, AX, two_on)
    b1e, *p = step(bk, p, cross, even, 0)
    b2e, *p = step(b1e, p, ring, even, 64)
    b1o, *p = step(b2e, p, ring, odd, 0)
    (b2o,) = step(b1o, p, ring, odd, 64, True)
    de, *p = call(
        k_dstart, [flags, even, a2e, a1o, a2o, bk, b1e, b2e, b1o, b2o, w, w2, ws, tab["xf"]],
        [(3, 3, 64, 64)] + [pay] * 4,
    )
    h = swap(p, here)
    x, loc = call(
        k_xbulk, [flags, de, q, v1, v2, vprev, tab["fa"], tab["fz"], tab["pxy"], tab["pz"]],
        [(3, 3, 256, 128)] * 2, 3 * big,
    )
    u1, d, *p = call(
        k_xpost, [flags, x, loc, *h, *h1, *h2, vh, vprev, tab["fh"], tab["fe"], tab["pz"], tab["ph"]],
        [st, st] + [pay] * 4,
    )
    h = swap(p, here)
    (loc,) = call(k_bulk1, [u1, tab["fa"], tab["fz"]], [st], big)
    (out,) = call(k_last, [flags, u1, d, loc, *h, tab["fh"]], [st])
    return out.reshape(initial.shape)


def solution(mesh):
    return jax.shard_map(
        shards,
        mesh=mesh,
        in_specs=(P("tm", None, "space", None, None, None),),
        out_specs=P("tm", None, "space", None, None, None),
        check_vma=False,
    )
```

```python
import functools

import jax
import jax.numpy as jnp
import ml_dtypes
import numpy as np
from jax import lax
from jax.experimental import pallas as pl
from jax.experimental.pallas import tpu as pltpu
from jax.sharding import PartitionSpec as P

H = 0.001
NU = 0.05
W0 = (5.0 / 24.0, 1.0 / 3.0, -1.0 / 24.0)
W1 = (-1.0 / 24.0, 1.0 / 3.0, 5.0 / 24.0)
F32 = jnp.float32
BF = jnp.bfloat16
AX = ("tm", "space")


def cheb_tables(count):
    index = np.arange(count)
    points = -np.cos(np.pi * index / (count - 1))
    weights = (-1.0) ** index
    weights[0] = weights[0] * 0.5
    weights[-1] = weights[-1] * 0.5
    return points, weights


def diff_matrix(points, weights):
    count = points.shape[0]
    ident = np.eye(count)
    gaps = points[:, None] - points[None, :] + ident
    matrix = weights[None, :] / weights[:, None] / gaps
    matrix = matrix * (1.0 - ident)
    return matrix - ident * matrix.sum(axis=1)[:, None]


def interp_matrix(points, weights, targets):
    gaps = targets[:, None] - points[None, :]
    exact_hit = np.abs(gaps) < 1e-12
    safe_gaps = np.where(exact_hit, 1.0, gaps)
    terms = weights[None, :] / safe_gaps
    matrix = terms / terms.sum(axis=1, keepdims=True)
    any_hit = exact_hit.any(axis=1)
    return np.where(any_hit[:, None], np.where(exact_hit, 1.0, 0.0), matrix)


def lifted_matrix(count, length, periodic):
    points, weights = cheb_tables(count)
    matrix = np.kron(np.eye(length // count), diff_matrix(points, weights))
    lift = (count - 1) ** 2 / 2.0
    for place in range(length):
        if place % count == 0:
            matrix[place, place] += lift
            if place > 0:
                matrix[place, place - 1] -= lift
            elif periodic:
                matrix[place, length - 1] -= lift
        if place % count == count - 1:
            matrix[place, place] -= lift
            if place < length - 1:
                matrix[place, place + 1] += lift
            elif periodic:
                matrix[place, 0] += lift
    return matrix


def hilo(matrix):
    hi = matrix.astype(ml_dtypes.bfloat16)
    lo = (matrix - hi.astype(np.float64)).astype(ml_dtypes.bfloat16)
    return hi, lo


def left_pieces(matrix):
    h, l = hilo(matrix)
    if matrix.shape[1] <= 64:
        return [np.concatenate([h, l, h], 1)]
    if matrix.shape[1] <= 128:
        return [np.concatenate([h, h], 1), l]
    return [h, l]


def right_pieces(matrix):
    h, l = hilo(matrix)
    return [np.concatenate([h, h], 0), l]


def level_ops(n, zlen):
    m = lifted_matrix(n, n, False)
    c = (n - 1) ** 2 / 2.0
    eye = np.eye(n)
    e0, e1 = eye[:, :1], eye[:, -1:]
    mm = m @ m - c * c * (e0 @ e0.T + e1 @ e1.T)
    a = np.concatenate([np.kron(m, eye), np.kron(eye, m), NU * (np.kron(mm, eye) + np.kron(eye, mm))])
    zero = np.zeros((n, 1))
    gb, ga = -c * e0, c * e1
    lb = [-c * NU * m[:, :1], -c * NU * e0]
    la = [c * NU * m[:, -1:], c * NU * e1]

    def bx(col):
        return np.kron(col, eye)

    def by(col):
        return np.kron(eye, col)

    hx = np.concatenate([bx(gb), bx(zero), bx(ga), bx(zero), by(zero), by(zero), by(zero), by(zero)], 1)
    hy = np.concatenate([bx(zero), bx(zero), bx(zero), bx(zero), by(gb), by(zero), by(ga), by(zero)], 1)
    hl = np.concatenate([bx(lb[0]), bx(lb[1]), bx(la[0]), bx(la[1]), by(lb[0]), by(lb[1]), by(la[0]), by(la[1])], 1)
    h = np.concatenate([hx, hy, hl])
    z = lifted_matrix(n, zlen, True)
    return m, a, h, z.T, NU * (z @ z).T


def faces_matrix(rows_val, rows_par, n_in):
    eye = np.eye(n_in)
    out = []
    for side in (0, 1):
        out += [np.kron(rows_val[side][None], eye), np.kron(rows_par[side][None], eye)]
    for side in (0, 1):
        out += [np.kron(eye, rows_val[side][None]), np.kron(eye, rows_par[side][None])]
    return np.concatenate(out)


def tables():
    fp, fw = cheb_tables(16)
    cp, cw = cheb_tables(8)
    r = interp_matrix(fp, fw, cp)
    p = interp_matrix(cp, cw, fp)
    t = {}
    m, a, h, zg, zl = level_ops(16, 128)
    t["fa"] = a
    t["fh"] = h[256:]
    t["fz"] = np.concatenate([zg, zl], 1)
    part = faces_matrix((m[0] * 0, m[0] * 0), (m[0], m[-1]), 16)
    t["fe"] = np.concatenate([part[16:32], part[48:64], part[80:96], part[112:128]])
    mc, ac, hc, zgc, zlc = level_ops(8, 64)
    t["ca"] = np.concatenate([ac, hc], 1)
    two = np.eye(2)
    t["cz"] = np.concatenate([np.kron(two, zgc), np.kron(two, zlc)], 1)
    e8 = np.eye(8)
    t["cf"] = faces_matrix((e8[0], e8[-1]), (mc[0], mc[-1]), 8)
    mp = m @ p
    t["xf"] = faces_matrix((p[0], p[-1]), (mp[0], mp[-1]), 8)
    t["rxy"] = np.kron(r, r)
    t["rz"] = np.kron(np.eye(8), r).T
    t["pxy"] = np.kron(p, p)
    t["pz"] = np.kron(np.eye(8), p).T
    t["ph"] = np.kron(np.eye(8), p)
    return t


def packed(names, table):
    where, rows, at = {}, [], 0
    for name in names:
        for i, piece in enumerate((right_pieces if name in RIGHT else left_pieces)(table[name])):
            n, k = piece.shape
            where[name, i] = (at, n, k)
            full = np.zeros((-(-n // 16) * 16, 256), ml_dtypes.bfloat16)
            full[:n, :k] = piece
            rows.append(full)
            at += full.shape[0]
    return np.concatenate(rows), where


RIGHT = ("fz", "cz", "rz", "pz")
TABLES = tables()
PACK_A, WHERE = packed(["fe"], TABLES)
PACK_B, WHERE_B = packed([n for n in TABLES if n != "fe"], TABLES)
WHERE.update(WHERE_B)


def split(x):
    hi = x.astype(BF)
    lo = (x - hi.astype(F32)).astype(BF)
    return hi, lo


def mm(a, b):
    return jnp.dot(a, b, preferred_element_type=F32)


def piece(t, name, i):
    at, n, k = WHERE[name, i]
    return t[at : at + n, :k]


def ldot(t, name, x):
    xh, xl = split(x)
    if x.shape[0] <= 64:
        return mm(piece(t, name, 0), jnp.concatenate([xh, xh, xl], axis=0))
    if x.shape[0] <= 128:
        return mm(piece(t, name, 0), jnp.concatenate([xh, xl], axis=0)) + mm(piece(t, name, 1), xh)
    th = piece(t, name, 0)
    return mm(th, xh) + (mm(piece(t, name, 1), xh) + mm(th, xl))


def rdot(x, t, name):
    xh, xl = split(x)
    return mm(jnp.concatenate([xh, xl], axis=1), piece(t, name, 0)) + mm(xh, piece(t, name, 1))


def cat3(v):
    return jnp.concatenate([v[0], v[1], v[2]], axis=1)


def cut3(x, width=128):
    return [x[:, i * width : (i + 1) * width] for i in range(3)]


def fine_local(v, t):
    g = ldot(t, "fa", cat3(v))
    z = rdot(jnp.concatenate(v, axis=0), t, "fz")
    out = []
    for c in range(3):
        s = slice(128 * c, 128 * c + 128)
        zc = z[256 * c : 256 * c + 256]
        adv = v[0] * g[0:256, s] + v[1] * g[256:512, s] + v[2] * zc[:, :128]
        out.append(g[512:768, s] + zc[:, 128:] - adv)
    return out


def fine_halo(v, halo, t):
    k = ldot(t, "fh", cat3(halo))
    c = 112.5
    out = []
    for i in range(3):
        s = slice(128 * i, 128 * i + 128)
        r = k[256:512, s] - v[1] * k[0:256, s]
        first = r[0:16] + c * v[0][0:16] * halo[i][0:16]
        last = r[240:256] - c * v[0][240:256] * halo[i][32:48]
        out.append(jnp.concatenate([first, r[16:240], last], axis=0))
    return out


def halo_of(flags, h, c, lo, hi):
    p1, p2, c1, c2 = [r[c, lo:hi] for r in h]
    rodd, codd = flags[1] == 1, flags[2] == 1
    return jnp.concatenate(
        [jnp.where(rodd, p1, p2), jnp.where(rodd, p2, p1), jnp.where(codd, c1, c2), jnp.where(codd, c2, c1)], axis=0
    )


def send_faces(flags, outs, c, rows, xlo, xhi, ylo, yhi):
    rodd, codd = flags[1] == 1, flags[2] == 1
    outs[0][c, rows] = jnp.where(rodd, xlo, xhi)
    outs[1][c, rows] = jnp.where(rodd, xhi, xlo)
    outs[2][c, rows] = jnp.where(codd, ylo, yhi)
    outs[3][c, rows] = jnp.where(codd, yhi, ylo)


def fine_faces(flags, outs, vref, t):
    v = [vref[c] for c in range(3)]
    part = ldot(t, "fe", cat3(v))
    for c in range(3):
        pc = part[:, 128 * c : 128 * c + 128]
        send_faces(
            flags, outs, c, slice(0, 16),
            v[c][0:16], v[c][240:256],
            vref[c, pl.ds(0, 16, stride=16), :], vref[c, pl.ds(15, 16, stride=16), :],
        )
        send_faces(flags, outs, c, slice(16, 32), pc[0:16], pc[16:32], pc[32:48], pc[48:64])


def coarse_faces(flags, outs, rows, e, t):
    for c in range(3):
        f = ldot(t, "cf", e[c])
        send_faces(flags, outs, c, rows, f[0:16], f[16:32], f[32:48], f[48:64])


def coarse_rate(w, halo, t):
    g = cut3(ldot(t, "ca", jnp.concatenate([cat3(w), cat3(halo)], axis=0)))
    z = rdot(jnp.concatenate(w, axis=0), t, "cz")
    out = []
    for c in range(3):
        s = slice(64 * c, 64 * c + 64)
        adv = w[0] * g[c][0:64] + w[1] * g[c][64:128] + w[2] * z[s, :128]
        out.append(g[c][128:192] + z[s, 128:] - adv)
    return out


def restrict(v, t):
    s = ldot(t, "rxy", cat3(v))
    r = rdot(jnp.concatenate(cut3(s), axis=0), t, "rz")
    return [r[64 * c : 64 * c + 64] for c in range(3)]


def prolong(e, t):
    s = rdot(jnp.concatenate(e, axis=0), t, "pz")
    return cut3(ldot(t, "pxy", jnp.concatenate([s[0:64], s[64:128], s[128:192]], axis=1)))


def wide(x):
    return jnp.concatenate([x, x], axis=1)


def load3(r):
    return [r[c] for c in range(3)]


def store3(r, v):
    for c in range(3):
        r[c] = v[c]


def k_start(flags, v, ta, *outs):
    fine_faces(flags, outs, v, ta)


def k_bulk1(v, t, out):
    store3(out, fine_local(load3(v), t))


def k_post1(flags, v, loc, h1, h2, h3, h4, ta, t, f0, v1, *outs):
    h = (h1, h2, h3, h4)
    halo = [halo_of(flags, h, c, 0, 32) for c in range(3)]
    vv = load3(v)
    add = fine_halo(vv, halo, t)
    for c in range(3):
        f = loc[c] + add[c]
        f0[c] = f
        v1[c] = vv[c] + (H / 2.0) * f
    fine_faces(flags, outs, v1, ta)


def k_bulk2(flags, v, q, t, out, w, *outs):
    vv = load3(v)
    store3(out, fine_local(vv, t))
    w0 = restrict(load3(q), t)
    w1 = restrict(vv, t)
    both = [jnp.concatenate([w0[c], w1[c]], axis=1) for c in range(3)]
    store3(w, both)
    coarse_faces(flags, outs, slice(0, 16), both, t)


def k_post2(flags, v, loc, h1, h2, h3, h4, d1, d2, d3, d4, ta, t, b1, v2, *outs):
    h = (h1, h2, h3, h4)
    halo = [halo_of(flags, h, c, 0, 32) for c in range(3)]
    vv = load3(v)
    add = fine_halo(vv, halo, t)
    for c in range(3):
        f = loc[c] + add[c]
        b1[c] = f
        v2[c] = vv[c] + (H / 2.0) * f
    fine_faces(flags, outs, v2, ta)
    for o, d in zip(outs, (d1, d2, d3, d4)):
        for c in range(3):
            o[c, 32:48] = d[c]


def k_bulk3(v, f0, b1, t, out, w2, fa, fb):
    vv = load3(v)
    store3(out, fine_local(vv, t))
    store3(w2, restrict(vv, t))
    rf = restrict(load3(f0), t)
    rb = restrict(load3(b1), t)
    for c in range(3):
        fa[c] = (H * W0[0]) * rf[c] + (H * W0[1]) * rb[c]
        fb[c] = (H * W1[0]) * rf[c] + (H * W1[1]) * rb[c]


def k_post3(flags, v, loc, h1, h2, h3, h4, w, fa, fb, t, a, vh):
    h = (h1, h2, h3, h4)
    halo = [halo_of(flags, h, c, 0, 32) for c in range(3)]
    vv = load3(v)
    add = fine_halo(vv, halo, t)
    b2 = [loc[c] + add[c] for c in range(3)]
    rb = restrict(b2, t)
    ww = load3(w)
    chalo = [halo_of(flags, h, c, 32, 48) for c in range(3)]
    cr = coarse_rate(ww, chalo, t)
    for c in range(3):
        t0 = fa[c] + (H * W0[2]) * rb[c]
        t1 = fb[c] + (H * W1[2]) * rb[c]
        start = jnp.where(flags[0] == 1, ww[c][:, :64], (-H / 2.0) * cr[c][:, :64])
        a[c] = jnp.concatenate([start + t0, t1 - (H / 2.0) * cr[c][:, 64:]], axis=1)
        vh[c, 0:256] = vv[c]
        vh[c, 256:384] = halo[c]


def k_pair(flags, own, other, d):
    odd = flags[1] == 1
    for c in range(3):
        a = jnp.where(odd, other[c], own[c])
        b = jnp.where(odd, own[c], other[c])
        d[c, 0:64] = jnp.concatenate([a[:, :64], b[:, :64]], axis=1)
        d[c, 64:128] = jnp.concatenate([a[:, 64:], b[:, 64:]], axis=1)


def pair_faces(e, t, out, up, down, left, right):
    for c in range(3):
        out[c, 0:64] = e[c]
        f = ldot(t, "cf", e[c])
        up[c] = f[0:16, :64]
        down[c] = f[16:32, 64:]
        left[c] = f[32:48]
        right[c] = f[48:64]
        out[c, 64:80] = jnp.concatenate([f[0:16, 64:], f[16:32, :64]], axis=1)


def k_begin(flags, own, other, t, even, odd, *outs):
    second = flags[3] == 1
    e = []
    for c in range(3):
        a = jnp.where(second, other[c], own[c])
        even[c] = a
        odd[c] = jnp.where(second, own[c], other[c])
        e.append(a[0:64])
    pair_faces(e, t, *outs)


def k_chain(e, up, down, left, right, r, t, out, *outs, rows):
    ee = [e[c, 0:64] for c in range(3)]
    halo = []
    for c in range(3):
        i = e[c, 64:80]
        halo.append(jnp.concatenate([
            jnp.concatenate([up[c], i[:, 64:]], axis=1), jnp.concatenate([i[:, :64], down[c]], axis=1), left[c], right[c]
        ], axis=0))
    rate = coarse_rate(ee, halo, t)
    new = [ee[c] + (H / 2.0) * rate[c] + r[c, rows : rows + 64] for c in range(3)]
    if outs:
        pair_faces(new, t, out, *outs)
    else:
        store3(out, new)


def k_dstart(flags, d, a2e, a1o, a2o, bk, b1e, b2e, b1o, b2o, w, w2, ws, t, de, *outs):
    first, odd, second, late = flags[0] == 1, flags[1] == 1, flags[3] == 1, flags[4] == 1

    def mine(x):
        return jnp.where(odd, x[:, 64:], x[:, :64])

    for c in range(3):
        a2, b2 = a2e[c, 0:64], b2e[c, 0:64]
        k = jnp.where(second, jnp.where(late, b2, a2), bk[c, 0:64])
        e1 = jnp.where(
            late, jnp.where(second, b1o[c, 0:64], b1e[c, 0:64]), jnp.where(second, a1o[c, 0:64], d[c, 0:64])
        )
        e2 = jnp.where(late, jnp.where(second, b2o[c], b2), jnp.where(second, a2o[c, 0:64], a2))
        d0 = jnp.where(first, 0.0, mine(k) - ws[c])
        d1 = mine(e1) - w[c][:, 64:]
        d2 = mine(e2) - w2[c]
        de[0, c] = d0
        de[1, c] = d1
        de[2, c] = d2
        f = ldot(t, "xf", jnp.concatenate([d0, d1], axis=1))
        g = ldot(t, "xf", d2)
        send_faces(flags, outs, c, slice(0, 16), f[0:16], f[16:32], f[32:48], f[48:64])
        send_faces(flags, outs, c, slice(16, 32), *[wide(g[16 * i : 16 * i + 16]) for i in range(4)])


def k_ws(vh, t, ws):
    store3(ws, restrict([vh[c, 0:256] for c in range(3)], t))


def k_xbulk(flags, de, q, v1, v2, vh, t, x, loc):
    first = flags[0] == 1
    for c in range(3):
        x[0, c] = jnp.where(first, q[c], vh[c, 0:256])
        x[1, c] = v1[c]
        x[2, c] = v2[c]

    def node(m, carry):
        pr = prolong([de[m, c] for c in range(3)], t)
        xs = [x[m, c] + pr[c] for c in range(3)]
        lo = fine_local(xs, t)
        for c in range(3):
            x[m, c] = xs[c]
            loc[m, c] = lo[c]
        return carry

    lax.fori_loop(0, 3, node, 0)


def k_xpost(flags, x, loc, h1, h2, h3, h4, a1, a2, a3, a4, b1, b2, b3, b4, v2h, vh, ta, t, u1, d, o1, o2, o3, o4,
            base, co, g):
    first = flags[0] == 1
    h = (h1, h2, h3, h4)
    for c in range(3):
        lo = halo_of(flags, h, c, 0, 16)
        co[0, c] = lo[:, :64]
        co[1, c] = lo[:, 64:]
        co[2, c] = halo_of(flags, h, c, 16, 32)[:, :64]
        base[0, c] = jnp.where(first, halo_of(flags, (a1, a2, a3, a4), c, 0, 32), vh[c, 256:384])
        base[1, c] = halo_of(flags, (b1, b2, b3, b4), c, 0, 32)
        base[2, c] = v2h[c, 256:384]

    def node(m, carry):
        s = rdot(jnp.concatenate([co[m, c] for c in range(3)], axis=0), t, "pz")
        fine = cut3(ldot(t, "ph", jnp.concatenate([s[0:64], s[64:128], s[128:192]], axis=1)))
        xs = [x[m, c] for c in range(3)]
        add = fine_halo(xs, [base[m, c] + fine[c] for c in range(3)], t)
        for c in range(3):
            g[m, c] = loc[m, c] + add[c]
        return carry

    lax.fori_loop(0, 3, node, 0)
    for c in range(3):
        u = x[0, c] + H * (W0[0] * g[0, c] + W0[1] * g[1, c] + W0[2] * g[2, c])
        u1[c] = u
        d[c] = u + H * (W1[0] * g[0, c] + (W1[1] - 0.5) * g[1, c] + W1[2] * g[2, c])
    fine_faces(flags, (o1, o2, o3, o4), u1, ta)


def k_last(flags, v, d, loc, h1, h2, h3, h4, t, out):
    h = (h1, h2, h3, h4)
    halo = [halo_of(flags, h, c, 0, 32) for c in range(3)]
    add = fine_halo(load3(v), halo, t)
    for c in range(3):
        out[c] = d[c] + (H / 2.0) * (loc[c] + add[c])


def call(kernel, args, outs, cost=0, scratch=()):
    flat = args
    specs = [
        pl.BlockSpec(memory_space=pltpu.SMEM if a.dtype == jnp.int32 else pltpu.VMEM) for a in flat
    ]
    shapes = [jax.ShapeDtypeStruct(s, F32) for s in outs]
    size = sum(int(np.prod(a.shape)) * a.dtype.itemsize for a in flat) + sum(int(np.prod(s)) * 4 for s in outs)
    return pl.pallas_call(
        kernel,
        out_shape=shapes,
        in_specs=specs,
        out_specs=[pl.BlockSpec(memory_space=pltpu.VMEM) for _ in outs],
        scratch_shapes=[pltpu.VMEM(s, F32) for s in scratch],
        cost_estimate=pl.CostEstimate(flops=cost, bytes_accessed=size, transcendentals=0),
        compiler_params=pltpu.CompilerParams(vmem_limit_bytes=48 * 1024 * 1024),
    )(*flat)


def routes(shift):
    def dev(t, r, c):
        return t * 64 + (r % 16) * 4 + c % 4

    out = []
    for kind in range(4):
        pairs = []
        for t in range(4):
            if not 0 <= t + shift < 4:
                continue
            for r in range(16):
                for c in range(4):
                    if kind == 0:
                        to = (r ^ 1, c)
                    elif kind == 1:
                        to = (r + 1 if r & 1 else r - 1, c)
                    elif kind == 2:
                        to = (r, c ^ 1)
                    else:
                        to = (r, c + 1 if c & 1 else c - 1)
                    pairs.append((dev(t, r, c), dev(t + shift, *to)))
        out.append(pairs)
    return out


def ring_routes(late):
    out = []
    for dk, dz in ((-1, 0), (1, 0), (0, -1), (0, 1)):
        pairs = []
        for t in range(4):
            to = t + 2 * late
            if to > 3:
                continue
            for k in range(8):
                for z in range(8):
                    pairs.append((t * 64 + k * 8 + z, to * 64 + ((k + dk) % 8) * 8 + (z + dz) % 8))
        out.append(pairs)
    return out


def shards(initial):
    ta, tb = jnp.asarray(PACK_A), jnp.asarray(PACK_B)
    space, tm = lax.axis_index("space"), lax.axis_index("tm")
    flags = jnp.stack([(tm == 0).astype(jnp.int32), (space // 4) % 2, space % 2, tm % 2, tm // 2]).astype(jnp.int32)
    here = routes(0)
    ring, cross = ring_routes(0), ring_routes(1)
    same = [(t * 64 + b, t * 64 + 64 + b) for t in range(3) for b in range(64)]
    two_on = [(t * 64 + b, t * 64 + 128 + b) for t in range(2) for b in range(64)]
    partner = [(t * 64 + b, (t ^ 1) * 64 + b) for t in range(4) for b in range(64)]

    def swap(pieces, way, order=(1, 0, 3, 2)):
        got = {i: lax.ppermute(pieces[i], AX, way[i]) for i in order}
        return [got[i] for i in range(4)]

    st, pay, co, duo = (3, 256, 128), (3, 32, 128), (3, 64, 64), (3, 64, 128)
    c2pay, bpay = (3, 16, 128), (3, 48, 128)
    faces = [(3, 80, 128), (3, 16, 64), (3, 16, 64), (3, 16, 128), (3, 16, 128)]
    q = initial.reshape(st)
    big = 2_000_000_000
    p = call(k_start, [flags, q, ta], [pay] * 4)
    h1 = swap(p, here)
    (loc,) = call(k_bulk1, [q, tb], [st], big)
    f0, v1, *p = call(k_post1, [flags, q, loc, *h1, ta, tb], [st, st] + [pay] * 4)
    h2 = swap(p, here)
    loc, w, *cp = call(k_bulk2, [flags, v1, q, tb], [st, duo] + [c2pay] * 4, big)
    b1, v2, *p = call(k_post2, [flags, v1, loc, *h2, *cp, ta, tb], [st, st] + [bpay] * 4)
    h3 = swap(p, here)
    loc, w2, fa, fb = call(k_bulk3, [v2, f0, b1, tb], [st, co, co, co], big)
    a, vh = call(k_post3, [flags, v2, loc, *h3, w, fa, fb, tb], [duo, (3, 384, 128)])
    (mine,) = call(k_pair, [flags, a, lax.ppermute(a, AX, here[0])], [(3, 128, 128)])
    other = lax.ppermute(mine, AX, partner)
    even, odd, e, *p = call(k_begin, [flags, mine, other, tb], [(3, 128, 128)] * 2 + faces)

    def step(e, p, way, r, rows, last=False):
        below, above, right, left = swap(p, way, (0, 1, 2, 3))
        return call(
            functools.partial(k_chain, rows=rows), [e, above, below, left, right, r, tb], [duo] if last else faces
        )

    a2e, *p = step(e, p, ring, even, 64)
    a2e, vh = lax.optimization_barrier((a2e, vh))
    vprev = lax.ppermute(vh, AX, same)
    (ws,) = call(k_ws, [vprev, tb], [co])
    a1o, *p = step(a2e, p, ring, odd, 0)
    a2o, *p = step(a1o, p, ring, odd, 64)
    bk = lax.ppermute(a2o, AX, two_on)
    b1e, *p = step(bk, p, cross, even, 0)
    b2e, *p = step(b1e, p, ring, even, 64)
    b1o, *p = step(b2e, p, ring, odd, 0)
    (b2o,) = step(b1o, p, ring, odd, 64, True)
    de, *p = call(
        k_dstart, [flags, even, a2e, a1o, a2o, bk, b1e, b2e, b1o, b2o, w, w2, ws, tb], [(3, 3, 64, 64)] + [pay] * 4
    )
    h = swap(p, here)
    x, loc = call(k_xbulk, [flags, de, q, v1, v2, vprev, tb], [(3, 3, 256, 128)] * 2, 3 * big)
    u1, d, *p = call(
        k_xpost, [flags, x, loc, *h, *h1, *h2, vh, vprev, ta, tb], [st, st] + [pay] * 4,
        scratch=[(3, 3, 128, 128), (3, 3, 64, 64), (3, 3, 256, 128)],
    )
    h = swap(p, here)
    (loc,) = call(k_bulk1, [u1, tb], [st], big)
    (out,) = call(k_last, [flags, u1, d, loc, *h, tb], [st])
    return out.reshape(initial.shape)


def solution(mesh):
    return jax.shard_map(
        shards,
        mesh=mesh,
        in_specs=(P("tm", None, "space", None, None, None),),
        out_specs=P("tm", None, "space", None, None, None),
        check_vma=False,
    )
```

```python
import functools

import jax
import jax.numpy as jnp
import ml_dtypes
import numpy as np
from jax import lax
from jax.experimental import pallas as pl
from jax.experimental.pallas import tpu as pltpu
from jax.sharding import PartitionSpec as P

H = 0.001
NU = 0.05
W0 = (5.0 / 24.0, 1.0 / 3.0, -1.0 / 24.0)
W1 = (-1.0 / 24.0, 1.0 / 3.0, 5.0 / 24.0)
F32 = jnp.float32
BF = jnp.bfloat16
AX = ("tm", "space")


def cheb_tables(count):
    index = np.arange(count)
    points = -np.cos(np.pi * index / (count - 1))
    weights = (-1.0) ** index
    weights[0] = weights[0] * 0.5
    weights[-1] = weights[-1] * 0.5
    return points, weights


def diff_matrix(points, weights):
    count = points.shape[0]
    ident = np.eye(count)
    gaps = points[:, None] - points[None, :] + ident
    matrix = weights[None, :] / weights[:, None] / gaps
    matrix = matrix * (1.0 - ident)
    return matrix - ident * matrix.sum(axis=1)[:, None]


def interp_matrix(points, weights, targets):
    gaps = targets[:, None] - points[None, :]
    exact_hit = np.abs(gaps) < 1e-12
    safe_gaps = np.where(exact_hit, 1.0, gaps)
    terms = weights[None, :] / safe_gaps
    matrix = terms / terms.sum(axis=1, keepdims=True)
    any_hit = exact_hit.any(axis=1)
    return np.where(any_hit[:, None], np.where(exact_hit, 1.0, 0.0), matrix)


def lifted_matrix(count, length, periodic):
    points, weights = cheb_tables(count)
    matrix = np.kron(np.eye(length // count), diff_matrix(points, weights))
    lift = (count - 1) ** 2 / 2.0
    for place in range(length):
        if place % count == 0:
            matrix[place, place] += lift
            if place > 0:
                matrix[place, place - 1] -= lift
            elif periodic:
                matrix[place, length - 1] -= lift
        if place % count == count - 1:
            matrix[place, place] -= lift
            if place < length - 1:
                matrix[place, place + 1] += lift
            elif periodic:
                matrix[place, 0] += lift
    return matrix


def hilo(matrix):
    hi = matrix.astype(ml_dtypes.bfloat16)
    lo = (matrix - hi.astype(np.float64)).astype(ml_dtypes.bfloat16)
    return hi, lo


def left_pieces(matrix):
    h, l = hilo(matrix)
    if matrix.shape[1] <= 64:
        return [np.concatenate([h, l, h], 1)]
    if matrix.shape[1] <= 128:
        return [np.concatenate([h, h], 1), l]
    return [h, l]


def right_pieces(matrix):
    h, l = hilo(matrix)
    return [np.concatenate([h, h], 0), l]


def level_ops(n, zlen):
    m = lifted_matrix(n, n, False)
    c = (n - 1) ** 2 / 2.0
    eye = np.eye(n)
    e0, e1 = eye[:, :1], eye[:, -1:]
    mm = m @ m - c * c * (e0 @ e0.T + e1 @ e1.T)
    a = np.concatenate([np.kron(m, eye), np.kron(eye, m), NU * (np.kron(mm, eye) + np.kron(eye, mm))])
    zero = np.zeros((n, 1))
    gb, ga = -c * e0, c * e1
    lb = [-c * NU * m[:, :1], -c * NU * e0]
    la = [c * NU * m[:, -1:], c * NU * e1]

    def bx(col):
        return np.kron(col, eye)

    def by(col):
        return np.kron(eye, col)

    hx = np.concatenate([bx(gb), bx(zero), bx(ga), bx(zero), by(zero), by(zero), by(zero), by(zero)], 1)
    hy = np.concatenate([bx(zero), bx(zero), bx(zero), bx(zero), by(gb), by(zero), by(ga), by(zero)], 1)
    hl = np.concatenate([bx(lb[0]), bx(lb[1]), bx(la[0]), bx(la[1]), by(lb[0]), by(lb[1]), by(la[0]), by(la[1])], 1)
    h = np.concatenate([hx, hy, hl])
    z = lifted_matrix(n, zlen, True)
    return m, a, h, z.T, NU * (z @ z).T


def faces_matrix(rows_val, rows_par, n_in):
    eye = np.eye(n_in)
    out = []
    for side in (0, 1):
        out += [np.kron(rows_val[side][None], eye), np.kron(rows_par[side][None], eye)]
    for side in (0, 1):
        out += [np.kron(eye, rows_val[side][None]), np.kron(eye, rows_par[side][None])]
    return np.concatenate(out)


def tables():
    fp, fw = cheb_tables(16)
    cp, cw = cheb_tables(8)
    r = interp_matrix(fp, fw, cp)
    p = interp_matrix(cp, cw, fp)
    t = {}
    m, a, h, zg, zl = level_ops(16, 128)
    t["fa"] = a
    t["fh"] = h[256:]
    t["fz"] = np.concatenate([zg, zl], 1)
    part = faces_matrix((m[0] * 0, m[0] * 0), (m[0], m[-1]), 16)
    t["fe"] = np.concatenate([part[16:32], part[48:64], part[80:96], part[112:128]])
    mc, ac, hc, zgc, zlc = level_ops(8, 64)
    t["ca"] = np.concatenate([ac, hc], 1)
    two = np.eye(2)
    t["cz"] = np.concatenate([np.kron(two, zgc), np.kron(two, zlc)], 1)
    e8 = np.eye(8)
    t["cf"] = faces_matrix((e8[0], e8[-1]), (mc[0], mc[-1]), 8)
    mp = m @ p
    t["xf"] = faces_matrix((p[0], p[-1]), (mp[0], mp[-1]), 8)
    t["rxy"] = np.kron(r, r)
    t["rz"] = np.kron(np.eye(8), r).T
    t["pxy"] = np.kron(p, p)
    t["pz"] = np.kron(np.eye(8), p).T
    t["ph"] = np.kron(np.eye(8), p)
    return t


def packed(names, table):
    where, rows, at = {}, [], 0
    for name in names:
        for i, piece in enumerate((right_pieces if name in RIGHT else left_pieces)(table[name])):
            n, k = piece.shape
            where[name, i] = (at, n, k)
            full = np.zeros((-(-n // 16) * 16, 256), ml_dtypes.bfloat16)
            full[:n, :k] = piece
            rows.append(full)
            at += full.shape[0]
    return np.concatenate(rows), where


RIGHT = ("fz", "cz", "rz", "pz")
TABLES = tables()
PACK_A, WHERE = packed(["fe"], TABLES)
PACK_B, WHERE_B = packed([n for n in TABLES if n != "fe"], TABLES)
WHERE.update(WHERE_B)


def split(x):
    hi = x.astype(BF)
    lo = (x - hi.astype(F32)).astype(BF)
    return hi, lo


def mm(a, b):
    return jnp.dot(a, b, preferred_element_type=F32)


def piece(t, name, i):
    at, n, k = WHERE[name, i]
    return t[at : at + n, :k]


def ldot(t, name, x):
    xh, xl = split(x)
    if x.shape[0] <= 64:
        return mm(piece(t, name, 0), jnp.concatenate([xh, xh, xl], axis=0))
    if x.shape[0] <= 128:
        return mm(piece(t, name, 0), jnp.concatenate([xh, xl], axis=0)) + mm(piece(t, name, 1), xh)
    th = piece(t, name, 0)
    return mm(th, xh) + (mm(piece(t, name, 1), xh) + mm(th, xl))


def rdot(x, t, name):
    xh, xl = split(x)
    return mm(jnp.concatenate([xh, xl], axis=1), piece(t, name, 0)) + mm(xh, piece(t, name, 1))


def cat3(v):
    return jnp.concatenate([v[0], v[1], v[2]], axis=1)


def cut3(x, width=128):
    return [x[:, i * width : (i + 1) * width] for i in range(3)]


def fine_local(v, t):
    g = ldot(t, "fa", cat3(v))
    z = rdot(jnp.concatenate(v, axis=0), t, "fz")
    out = []
    for c in range(3):
        s = slice(128 * c, 128 * c + 128)
        zc = z[256 * c : 256 * c + 256]
        adv = v[0] * g[0:256, s] + v[1] * g[256:512, s] + v[2] * zc[:, :128]
        out.append(g[512:768, s] + zc[:, 128:] - adv)
    return out


def fine_halo(v, halo, t):
    k = ldot(t, "fh", cat3(halo))
    c = 112.5
    out = []
    for i in range(3):
        s = slice(128 * i, 128 * i + 128)
        r = k[256:512, s] - v[1] * k[0:256, s]
        first = r[0:16] + c * v[0][0:16] * halo[i][0:16]
        last = r[240:256] - c * v[0][240:256] * halo[i][32:48]
        out.append(jnp.concatenate([first, r[16:240], last], axis=0))
    return out


def halo_of(flags, h, c, lo, hi):
    p1, p2, c1, c2 = [r[c, lo:hi] for r in h]
    rodd, codd = flags[1] == 1, flags[2] == 1
    return jnp.concatenate(
        [jnp.where(rodd, p1, p2), jnp.where(rodd, p2, p1), jnp.where(codd, c1, c2), jnp.where(codd, c2, c1)], axis=0
    )


def send_faces(flags, outs, c, rows, xlo, xhi, ylo, yhi):
    rodd, codd = flags[1] == 1, flags[2] == 1
    outs[0][c, rows] = jnp.where(rodd, xlo, xhi)
    outs[1][c, rows] = jnp.where(rodd, xhi, xlo)
    outs[2][c, rows] = jnp.where(codd, ylo, yhi)
    outs[3][c, rows] = jnp.where(codd, yhi, ylo)


def fine_faces(flags, outs, vref, t):
    v = [vref[c] for c in range(3)]
    part = ldot(t, "fe", cat3(v))
    for c in range(3):
        pc = part[:, 128 * c : 128 * c + 128]
        send_faces(
            flags, outs, c, slice(0, 16),
            v[c][0:16], v[c][240:256],
            vref[c, pl.ds(0, 16, stride=16), :], vref[c, pl.ds(15, 16, stride=16), :],
        )
        send_faces(flags, outs, c, slice(16, 32), pc[0:16], pc[16:32], pc[32:48], pc[48:64])


def coarse_faces(flags, outs, rows, e, t):
    for c in range(3):
        f = ldot(t, "cf", e[c])
        send_faces(flags, outs, c, rows, f[0:16], f[16:32], f[32:48], f[48:64])


def coarse_rate(w, halo, t):
    g = cut3(ldot(t, "ca", jnp.concatenate([cat3(w), cat3(halo)], axis=0)))
    z = rdot(jnp.concatenate(w, axis=0), t, "cz")
    out = []
    for c in range(3):
        s = slice(64 * c, 64 * c + 64)
        adv = w[0] * g[c][0:64] + w[1] * g[c][64:128] + w[2] * z[s, :128]
        out.append(g[c][128:192] + z[s, 128:] - adv)
    return out


def restrict(v, t):
    s = ldot(t, "rxy", cat3(v))
    r = rdot(jnp.concatenate(cut3(s), axis=0), t, "rz")
    return [r[64 * c : 64 * c + 64] for c in range(3)]


def prolong(e, t):
    s = rdot(jnp.concatenate(e, axis=0), t, "pz")
    return cut3(ldot(t, "pxy", jnp.concatenate([s[0:64], s[64:128], s[128:192]], axis=1)))


def wide(x):
    return jnp.concatenate([x, x], axis=1)


def load3(r):
    return [r[c] for c in range(3)]


def store3(r, v):
    for c in range(3):
        r[c] = v[c]


def k_start(flags, v, ta, *outs):
    fine_faces(flags, outs, v, ta)


def k_bulk1(v, t, out):
    store3(out, fine_local(load3(v), t))


def k_post1(flags, v, loc, h1, h2, h3, h4, ta, t, f0, v1, *outs):
    h = (h1, h2, h3, h4)
    halo = [halo_of(flags, h, c, 0, 32) for c in range(3)]
    vv = load3(v)
    add = fine_halo(vv, halo, t)
    for c in range(3):
        f = loc[c] + add[c]
        f0[c] = f
        v1[c] = vv[c] + (H / 2.0) * f
    fine_faces(flags, outs, v1, ta)


def k_bulk2(flags, v, q, t, out, w, *outs):
    vv = load3(v)
    store3(out, fine_local(vv, t))
    w0 = restrict(load3(q), t)
    w1 = restrict(vv, t)
    both = [jnp.concatenate([w0[c], w1[c]], axis=1) for c in range(3)]
    store3(w, both)
    coarse_faces(flags, outs, slice(0, 16), both, t)


def k_post2(flags, v, loc, h1, h2, h3, h4, d1, d2, d3, d4, ta, t, b1, v2, *outs):
    h = (h1, h2, h3, h4)
    halo = [halo_of(flags, h, c, 0, 32) for c in range(3)]
    vv = load3(v)
    add = fine_halo(vv, halo, t)
    for c in range(3):
        f = loc[c] + add[c]
        b1[c] = f
        v2[c] = vv[c] + (H / 2.0) * f
    fine_faces(flags, outs, v2, ta)
    for o, d in zip(outs, (d1, d2, d3, d4)):
        for c in range(3):
            o[c, 32:48] = d[c]


def k_bulk3(v, f0, b1, t, out, w2, fa, fb):
    vv = load3(v)
    store3(out, fine_local(vv, t))
    store3(w2, restrict(vv, t))
    rf = restrict(load3(f0), t)
    rb = restrict(load3(b1), t)
    for c in range(3):
        fa[c] = (H * W0[0]) * rf[c] + (H * W0[1]) * rb[c]
        fb[c] = (H * W1[0]) * rf[c] + (H * W1[1]) * rb[c]


def k_post3(flags, v, loc, h1, h2, h3, h4, w, fa, fb, t, a, vh):
    h = (h1, h2, h3, h4)
    halo = [halo_of(flags, h, c, 0, 32) for c in range(3)]
    vv = load3(v)
    add = fine_halo(vv, halo, t)
    b2 = [loc[c] + add[c] for c in range(3)]
    rb = restrict(b2, t)
    ww = load3(w)
    chalo = [halo_of(flags, h, c, 32, 48) for c in range(3)]
    cr = coarse_rate(ww, chalo, t)
    for c in range(3):
        t0 = fa[c] + (H * W0[2]) * rb[c]
        t1 = fb[c] + (H * W1[2]) * rb[c]
        start = jnp.where(flags[0] == 1, ww[c][:, :64], (-H / 2.0) * cr[c][:, :64])
        a[c] = jnp.concatenate([start + t0, t1 - (H / 2.0) * cr[c][:, 64:]], axis=1)
        vh[c, 0:256] = vv[c]
        vh[c, 256:384] = halo[c]


def pair_faces(e, t, out, up, down, left, right):
    for c in range(3):
        out[c, 0:64] = e[c]
        f = ldot(t, "cf", e[c])
        up[c] = f[0:16, :64]
        down[c] = f[16:32, 64:]
        left[c] = f[32:48]
        right[c] = f[48:64]
        out[c, 64:80] = jnp.concatenate([f[0:16, 64:], f[16:32, :64]], axis=1)


def k_begin(flags, own, far, own2, far2, t, even, odd, *outs):
    low, second = flags[1] == 1, flags[3] == 1

    def pair(c, mine, other):
        a = jnp.where(low, other[c], mine[c])
        b = jnp.where(low, mine[c], other[c])
        return jnp.concatenate([
            jnp.concatenate([a[:, :64], b[:, :64]], axis=1), jnp.concatenate([a[:, 64:], b[:, 64:]], axis=1)
        ], axis=0)

    e = []
    for c in range(3):
        p, q = pair(c, own, far), pair(c, own2, far2)
        even[c] = jnp.where(second, q, p)
        odd[c] = jnp.where(second, p, q)
        e.append(even[c, 0:64])
    pair_faces(e, t, *outs)


def pair_step(e, up, down, left, right, r, t, rows):
    ee = [e[c, 0:64] for c in range(3)]
    halo = []
    for c in range(3):
        i = e[c, 64:80]
        halo.append(jnp.concatenate([
            jnp.concatenate([up[c], i[:, 64:]], axis=1), jnp.concatenate([i[:, :64], down[c]], axis=1), left[c], right[c]
        ], axis=0))
    rate = coarse_rate(ee, halo, t)
    return [ee[c] + (H / 2.0) * rate[c] + r[c, rows : rows + 64] for c in range(3)]


def k_chain(e, up, down, left, right, r, t, *outs, rows):
    pair_faces(pair_step(e, up, down, left, right, r, t, rows), t, *outs)


def mine(flags, x):
    return jnp.where(flags[1] == 1, x[:, 64:], x[:, :64])


def k_x0(flags, a2e, b2e, bk, ws, q, vh, t, d, x, loc):
    first, second, late = flags[0] == 1, flags[3] == 1, flags[4] == 1
    for c in range(3):
        k = jnp.where(second, jnp.where(late, b2e[c, 0:64], a2e[c, 0:64]), bk[c, 0:64])
        d[c] = jnp.where(first, 0.0, mine(flags, k) - ws[c])
    pr = prolong(load3(d), t)
    xs = [jnp.where(first, q[c], vh[c, 0:256]) + pr[c] for c in range(3)]
    store3(x, xs)
    store3(loc, fine_local(xs, t))


def k_x1(flags, even, a1o, b1e, b1o, w, v1, t, d, x, loc):
    second, late = flags[3] == 1, flags[4] == 1
    for c in range(3):
        e1 = jnp.where(
            late, jnp.where(second, b1o[c, 0:64], b1e[c, 0:64]), jnp.where(second, a1o[c, 0:64], even[c, 0:64])
        )
        d[c] = mine(flags, e1) - w[c][:, 64:]
    pr = prolong(load3(d), t)
    xs = [v1[c] + pr[c] for c in range(3)]
    store3(x, xs)
    store3(loc, fine_local(xs, t))


def k_dstart(flags, e, up, down, left, right, r, a2e, a2o, b2e, d0, d1, w2, t, d2, *outs):
    second, late = flags[3] == 1, flags[4] == 1
    b2o = pair_step(e, up, down, left, right, r, t, 64)
    for c in range(3):
        e2 = jnp.where(
            late, jnp.where(second, b2o[c], b2e[c, 0:64]), jnp.where(second, a2o[c, 0:64], a2e[c, 0:64])
        )
        d = mine(flags, e2) - w2[c]
        d2[c] = d
        f = ldot(t, "xf", jnp.concatenate([d0[c], d1[c]], axis=1))
        g = ldot(t, "xf", d)
        send_faces(flags, outs, c, slice(0, 16), f[0:16], f[16:32], f[32:48], f[48:64])
        send_faces(flags, outs, c, slice(16, 32), *[wide(g[16 * i : 16 * i + 16]) for i in range(4)])


def k_x2(d, v2, t, x, loc):
    pr = prolong(load3(d), t)
    xs = [v2[c] + pr[c] for c in range(3)]
    store3(x, xs)
    store3(loc, fine_local(xs, t))


def k_ws(vh, t, ws):
    store3(ws, restrict([vh[c, 0:256] for c in range(3)], t))


def k_xpost(flags, x0, x1, x2, l0, l1, l2, h1, h2, h3, h4, a1, a2, a3, a4, b1, b2, b3, b4, v2h, vh, ta, t, u1, d, *outs):
    first = flags[0] == 1
    h = (h1, h2, h3, h4)
    lo = [halo_of(flags, h, c, 0, 16) for c in range(3)]
    hi = [halo_of(flags, h, c, 16, 32) for c in range(3)]
    g = []
    for m, (x, loc) in enumerate(((x0, l0), (x1, l1), (x2, l2))):
        co = [lo[c][:, :64] if m == 0 else lo[c][:, 64:] if m == 1 else hi[c][:, :64] for c in range(3)]
        s = rdot(jnp.concatenate(co, axis=0), t, "pz")
        fine = cut3(ldot(t, "ph", jnp.concatenate([s[0:64], s[64:128], s[128:192]], axis=1)))
        halo = []
        for c in range(3):
            if m == 0:
                base = jnp.where(first, halo_of(flags, (a1, a2, a3, a4), c, 0, 32), vh[c, 256:384])
            elif m == 1:
                base = halo_of(flags, (b1, b2, b3, b4), c, 0, 32)
            else:
                base = v2h[c, 256:384]
            halo.append(base + fine[c])
        add = fine_halo(load3(x), halo, t)
        g.append([loc[c] + add[c] for c in range(3)])
    for c in range(3):
        u = x0[c] + H * (W0[0] * g[0][c] + W0[1] * g[1][c] + W0[2] * g[2][c])
        u1[c] = u
        d[c] = u + H * (W1[0] * g[0][c] + (W1[1] - 0.5) * g[1][c] + W1[2] * g[2][c])
    fine_faces(flags, outs, u1, ta)


def k_last(flags, v, d, loc, h1, h2, h3, h4, t, out):
    h = (h1, h2, h3, h4)
    halo = [halo_of(flags, h, c, 0, 32) for c in range(3)]
    add = fine_halo(load3(v), halo, t)
    for c in range(3):
        out[c] = d[c] + (H / 2.0) * (loc[c] + add[c])


def call(kernel, args, outs, cost=0, scratch=()):
    flat = args
    specs = [
        pl.BlockSpec(memory_space=pltpu.SMEM if a.dtype == jnp.int32 else pltpu.VMEM) for a in flat
    ]
    shapes = [jax.ShapeDtypeStruct(s, F32) for s in outs]
    size = sum(int(np.prod(a.shape)) * a.dtype.itemsize for a in flat) + sum(int(np.prod(s)) * 4 for s in outs)
    return pl.pallas_call(
        kernel,
        out_shape=shapes,
        in_specs=specs,
        out_specs=[pl.BlockSpec(memory_space=pltpu.VMEM) for _ in outs],
        scratch_shapes=[pltpu.VMEM(s, F32) for s in scratch],
        cost_estimate=pl.CostEstimate(flops=cost, bytes_accessed=size, transcendentals=0),
        compiler_params=pltpu.CompilerParams(vmem_limit_bytes=48 * 1024 * 1024),
    )(*flat)


def routes(shift):
    def dev(t, r, c):
        return t * 64 + (r % 16) * 4 + c % 4

    out = []
    for kind in range(4):
        pairs = []
        for t in range(4):
            if not 0 <= t + shift < 4:
                continue
            for r in range(16):
                for c in range(4):
                    if kind == 0:
                        to = (r ^ 1, c)
                    elif kind == 1:
                        to = (r + 1 if r & 1 else r - 1, c)
                    elif kind == 2:
                        to = (r, c ^ 1)
                    else:
                        to = (r, c + 1 if c & 1 else c - 1)
                    pairs.append((dev(t, r, c), dev(t + shift, *to)))
        out.append(pairs)
    return out


def ring_routes(late):
    out = []
    for dk, dz in ((-1, 0), (1, 0), (0, -1), (0, 1)):
        pairs = []
        for t in range(4):
            to = t ^ (2 * late)
            for k in range(8):
                for z in range(8):
                    pairs.append((t * 64 + k * 8 + z, to * 64 + ((k + dk) % 8) * 8 + (z + dz) % 8))
        out.append(pairs)
    return out


def shards(initial):
    ta, tb = jnp.asarray(PACK_A), jnp.asarray(PACK_B)
    space, tm = lax.axis_index("space"), lax.axis_index("tm")
    flags = jnp.stack([(tm == 0).astype(jnp.int32), (space // 4) % 2, space % 2, tm % 2, tm // 2]).astype(jnp.int32)
    here = routes(0)
    ring, cross = ring_routes(0), ring_routes(1)
    after = [(t * 64 + b, (t + 1) % 4 * 64 + b) for t in range(4) for b in range(64)]
    two_on = [(t * 64 + b, (t ^ 2) * 64 + b) for t in range(4) for b in range(64)]
    partner = [(t * 64 + b, (t ^ 1) * 64 + b) for t in range(4) for b in range(64)]

    def swap(pieces, way, order=(1, 0, 3, 2)):
        got = {i: lax.ppermute(pieces[i], AX, way[i]) for i in order}
        return [got[i] for i in range(4)]

    st, pay, co, duo = (3, 256, 128), (3, 32, 128), (3, 64, 64), (3, 64, 128)
    c2pay, bpay = (3, 16, 128), (3, 48, 128)
    faces = [(3, 80, 128), (3, 16, 64), (3, 16, 64), (3, 16, 128), (3, 16, 128)]
    q = initial.reshape(st)
    big = 2_000_000_000
    p = call(k_start, [flags, q, ta], [pay] * 4)
    h1 = swap(p, here)
    (loc,) = call(k_bulk1, [q, tb], [st], big)
    f0, v1, *p = call(k_post1, [flags, q, loc, *h1, ta, tb], [st, st] + [pay] * 4)
    h2 = swap(p, here)
    loc, w, *cp = call(k_bulk2, [flags, v1, q, tb], [st, duo] + [c2pay] * 4, big)
    b1, v2, *p = call(k_post2, [flags, v1, loc, *h2, *cp, ta, tb], [st, st] + [bpay] * 4)
    h3 = swap(p, here)
    loc, w2, fa, fb = call(k_bulk3, [v2, f0, b1, tb], [st, co, co, co], big)
    a, vh = call(k_post3, [flags, v2, loc, *h3, w, fa, fb, tb], [duo, (3, 384, 128)])
    far = lax.ppermute(a, AX, here[0])
    own2, far2 = lax.ppermute(a, AX, partner), lax.ppermute(far, AX, partner)
    even, odd, e, *p = call(k_begin, [flags, a, far, own2, far2, tb], [(3, 128, 128)] * 2 + faces)

    def trade(p, way):
        below, above, right, left = swap(p, way, (0, 1, 2, 3))
        return above, below, left, right

    def step(e, p, way, r, rows):
        return call(functools.partial(k_chain, rows=rows), [e, *trade(p, way), r, tb], faces)

    a2e, *p = step(e, p, ring, even, 64)
    a2e, vh = lax.optimization_barrier((a2e, vh))
    vprev = lax.ppermute(vh, AX, after)
    a1o, *p = step(a2e, p, ring, odd, 0)
    a2o, *p = step(a1o, p, ring, odd, 64)
    (ws,) = call(k_ws, [vprev, tb], [co])
    bk = lax.ppermute(a2o, AX, two_on)
    bk, ws = lax.optimization_barrier((bk, ws))
    b1e, *p = step(bk, p, cross, even, 0)
    b2e, *p = step(b1e, p, ring, even, 64)
    d0, x0, l0 = call(k_x0, [flags, a2e, b2e, bk, ws, q, vprev, tb], [co, st, st], big)
    b1o, *p = step(b2e, p, ring, odd, 0)
    d1, x1, l1 = call(k_x1, [flags, even, a1o, b1e, b1o, w, v1, tb], [co, st, st], big)
    d2, *p = call(
        k_dstart, [flags, b1o, *trade(p, ring), odd, a2e, a2o, b2e, d0, d1, w2, tb], [co] + [pay] * 4
    )
    h = swap(p, here)
    x2, l2 = call(k_x2, [d2, v2, tb], [st, st], big)
    u1, d, *p = call(
        k_xpost, [flags, x0, x1, x2, l0, l1, l2, *h, *h1, *h2, vh, vprev, ta, tb], [st, st] + [pay] * 4
    )
    h = swap(p, here)
    (loc,) = call(k_bulk1, [u1, tb], [st], big)
    (out,) = call(k_last, [flags, u1, d, loc, *h, tb], [st])
    return out.reshape(initial.shape)


def solution(mesh):
    return jax.shard_map(
        shards,
        mesh=mesh,
        in_specs=(P("tm", None, "space", None, None, None),),
        out_specs=P("tm", None, "space", None, None, None),
        check_vma=False,
    )
```

```python
import functools

import jax
import jax.numpy as jnp
import ml_dtypes
import numpy as np
from jax import lax
from jax.experimental import pallas as pl
from jax.experimental.pallas import tpu as pltpu
from jax.sharding import PartitionSpec as P


H = 0.001
NU = 0.05
W0 = (5.0 / 24.0, 1.0 / 3.0, -1.0 / 24.0)
W1 = (-1.0 / 24.0, 1.0 / 3.0, 5.0 / 24.0)
F32 = jnp.float32
BF = jnp.bfloat16
AX = ("tm", "space")


def cheb_tables(count):
    index = np.arange(count)
    points = -np.cos(np.pi * index / (count - 1))
    weights = (-1.0) ** index
    weights[0] = weights[0] * 0.5
    weights[-1] = weights[-1] * 0.5
    return points, weights


def diff_matrix(points, weights):
    count = points.shape[0]
    ident = np.eye(count)
    gaps = points[:, None] - points[None, :] + ident
    matrix = weights[None, :] / weights[:, None] / gaps
    matrix = matrix * (1.0 - ident)
    return matrix - ident * matrix.sum(axis=1)[:, None]


def interp_matrix(points, weights, targets):
    gaps = targets[:, None] - points[None, :]
    exact_hit = np.abs(gaps) < 1e-12
    safe_gaps = np.where(exact_hit, 1.0, gaps)
    terms = weights[None, :] / safe_gaps
    matrix = terms / terms.sum(axis=1, keepdims=True)
    any_hit = exact_hit.any(axis=1)
    return np.where(any_hit[:, None], np.where(exact_hit, 1.0, 0.0), matrix)


def lifted_matrix(count, length, periodic):
    points, weights = cheb_tables(count)
    matrix = np.kron(np.eye(length // count), diff_matrix(points, weights))
    lift = (count - 1) ** 2 / 2.0
    for place in range(length):
        if place % count == 0:
            matrix[place, place] += lift
            if place > 0:
                matrix[place, place - 1] -= lift
            elif periodic:
                matrix[place, length - 1] -= lift
        if place % count == count - 1:
            matrix[place, place] -= lift
            if place < length - 1:
                matrix[place, place + 1] += lift
            elif periodic:
                matrix[place, 0] += lift
    return matrix


def hilo(matrix):
    hi = matrix.astype(ml_dtypes.bfloat16)
    lo = (matrix - hi.astype(np.float64)).astype(ml_dtypes.bfloat16)
    return hi, lo


def left_pieces(matrix):
    h, l = hilo(matrix)
    if matrix.shape[1] <= 64:
        return [np.concatenate([h, l, h], 1)]
    if matrix.shape[1] <= 128:
        return [np.concatenate([h, h], 1), l]
    return [h, l]


def right_pieces(matrix):
    h, l = hilo(matrix)
    return [np.concatenate([h, h], 0), l]


def level_ops(n, zlen):
    m = lifted_matrix(n, n, False)
    c = (n - 1) ** 2 / 2.0
    eye = np.eye(n)
    e0, e1 = eye[:, :1], eye[:, -1:]
    mm = m @ m - c * c * (e0 @ e0.T + e1 @ e1.T)
    a = np.concatenate([np.kron(m, eye), np.kron(eye, m), NU * (np.kron(mm, eye) + np.kron(eye, mm))])
    zero = np.zeros((n, 1))
    gb, ga = -c * e0, c * e1
    lb = [-c * NU * m[:, :1], -c * NU * e0]
    la = [c * NU * m[:, -1:], c * NU * e1]

    def bx(col):
        return np.kron(col, eye)

    def by(col):
        return np.kron(eye, col)

    hx = np.concatenate([bx(gb), bx(zero), bx(ga), bx(zero), by(zero), by(zero), by(zero), by(zero)], 1)
    hy = np.concatenate([bx(zero), bx(zero), bx(zero), bx(zero), by(gb), by(zero), by(ga), by(zero)], 1)
    hl = np.concatenate([bx(lb[0]), bx(lb[1]), bx(la[0]), bx(la[1]), by(lb[0]), by(lb[1]), by(la[0]), by(la[1])], 1)
    h = np.concatenate([hx, hy, hl])
    z = lifted_matrix(n, zlen, True)
    return m, a, h, z.T, NU * (z @ z).T


def faces_matrix(rows_val, rows_par, n_in):
    eye = np.eye(n_in)
    out = []
    for side in (0, 1):
        out += [np.kron(rows_val[side][None], eye), np.kron(rows_par[side][None], eye)]
    for side in (0, 1):
        out += [np.kron(eye, rows_val[side][None]), np.kron(eye, rows_par[side][None])]
    return np.concatenate(out)


def tables():
    fp, fw = cheb_tables(16)
    cp, cw = cheb_tables(8)
    r = interp_matrix(fp, fw, cp)
    p = interp_matrix(cp, cw, fp)
    t = {}
    m, a, h, zg, zl = level_ops(16, 128)
    t["fa"] = a
    t["fh"] = h[512:]
    t["fz"] = np.concatenate([zg, zl], 1)
    part = faces_matrix((m[0] * 0, m[0] * 0), (m[0], m[-1]), 16)
    t["fe"] = np.concatenate([part[16:32], part[48:64], part[80:96], part[112:128]])
    mc, ac, hc, zgc, zlc = level_ops(8, 64)
    t["ca"] = np.concatenate([ac, hc], 1)
    two = np.eye(2)
    t["cz"] = np.concatenate([np.kron(two, zgc), np.kron(two, zlc)], 1)
    e8 = np.eye(8)
    t["cf"] = faces_matrix((e8[0], e8[-1]), (mc[0], mc[-1]), 8)
    mp = m @ p
    t["xf"] = faces_matrix((p[0], p[-1]), (mp[0], mp[-1]), 8)
    t["rxy"] = np.kron(r, r)
    t["rz"] = np.kron(np.eye(8), r).T
    t["pxy"] = np.kron(p, p)
    t["pz"] = np.kron(np.eye(8), p).T
    t["ph"] = np.kron(np.eye(8), p)
    return t


def packed(names, table):
    where, rows, at = {}, [], 0
    for name in names:
        for i, piece in enumerate((right_pieces if name in RIGHT else left_pieces)(table[name])):
            n, k = piece.shape
            where[name, i] = (at, n, k)
            full = np.zeros((-(-n // 16) * 16, 256), ml_dtypes.bfloat16)
            full[:n, :k] = piece
            rows.append(full)
            at += full.shape[0]
    return np.concatenate(rows), where


RIGHT = ("fz", "cz", "rz", "pz")
TABLES = tables()
EDGE = lifted_matrix(16, 16, False)
PACK_A, WHERE = packed(["fe"], TABLES)
PACK_B, WHERE_B = packed([n for n in TABLES if n != "fe"], TABLES)
WHERE.update(WHERE_B)


def split(x):
    hi = x.astype(BF)
    lo = (x - hi.astype(F32)).astype(BF)
    return hi, lo


def mm(a, b):
    return jnp.dot(a, b, preferred_element_type=F32)


def piece(t, name, i):
    at, n, k = WHERE[name, i]
    return t[at : at + n, :k]


def ldot(t, name, x):
    xh, xl = split(x)
    if x.shape[0] <= 64:
        return mm(piece(t, name, 0), jnp.concatenate([xh, xh, xl], axis=0))
    if x.shape[0] <= 128:
        return mm(piece(t, name, 0), jnp.concatenate([xh, xl], axis=0)) + mm(piece(t, name, 1), xh)
    th = piece(t, name, 0)
    return mm(th, xh) + (mm(piece(t, name, 1), xh) + mm(th, xl))


def rdot(x, t, name):
    xh, xl = split(x)
    return mm(jnp.concatenate([xh, xl], axis=1), piece(t, name, 0)) + mm(xh, piece(t, name, 1))


def cat3(v):
    return jnp.concatenate([v[0], v[1], v[2]], axis=1)


def cut3(x, width=128):
    return [x[:, i * width : (i + 1) * width] for i in range(3)]


def fine_local(v, t):
    g = ldot(t, "fa", cat3(v))
    z = rdot(jnp.concatenate(v, axis=0), t, "fz")
    out = []
    for c in range(3):
        s = slice(128 * c, 128 * c + 128)
        zc = z[256 * c : 256 * c + 256]
        adv = v[0] * g[0:256, s] + v[1] * g[256:512, s] + v[2] * zc[:, :128]
        out.append(g[512:768, s] + zc[:, 128:] - adv)
    return out


def fine_rate(v, loc, halo, t, acc):
    k = ldot(t, "fh", cat3(halo))
    c = 112.5
    low, high = pl.ds(0, 16, stride=16), pl.ds(15, 16, stride=16)
    vlow, vhigh = v[1, low, :], v[1, high, :]
    for i in range(3):
        r = loc[i] + k[:, 128 * i : 128 * i + 128]
        acc[i, 16:240] = r[16:240]
        acc[i, 0:16] = r[0:16] + c * v[0, 0:16] * halo[i][0:16]
        acc[i, 240:256] = r[240:256] - c * v[0, 240:256] * halo[i][32:48]
        acc[i, low, :] = acc[i, low, :] + c * vlow * halo[i][64:80]
        acc[i, high, :] = acc[i, high, :] - c * vhigh * halo[i][96:112]


def halo_of(flags, h, c, lo, hi):
    p2, p1, c1, c2 = [r[c, lo:hi] for r in h]
    rodd, codd = flags[1] == 1, flags[2] == 1
    return jnp.concatenate(
        [jnp.where(rodd, p1, p2), jnp.where(rodd, p2, p1), jnp.where(codd, c1, c2), jnp.where(codd, c2, c1)], axis=0
    )


def send_faces(flags, outs, c, rows, xlo, xhi, ylo, yhi):
    rodd, codd = flags[1] == 1, flags[2] == 1
    outs[0][c, rows] = jnp.where(rodd, xhi, xlo)
    outs[1][c, rows] = jnp.where(rodd, xlo, xhi)
    outs[2][c, rows] = jnp.where(codd, ylo, yhi)
    outs[3][c, rows] = jnp.where(codd, yhi, ylo)


def fine_faces(flags, outs, vref, t):
    v = [vref[c] for c in range(3)]
    part = ldot(t, "fe", cat3(v))
    for c in range(3):
        pc = part[:, 128 * c : 128 * c + 128]
        send_faces(
            flags, outs, c, slice(0, 16),
            v[c][0:16], v[c][240:256],
            vref[c, pl.ds(0, 16, stride=16), :], vref[c, pl.ds(15, 16, stride=16), :],
        )
        send_faces(flags, outs, c, slice(16, 32), pc[0:16], pc[16:32], pc[32:48], pc[48:64])


def coarse_faces(flags, outs, rows, e, t):
    for c in range(3):
        f = ldot(t, "cf", e[c])
        send_faces(flags, outs, c, rows, f[0:16], f[16:32], f[32:48], f[48:64])


def coarse_rate(w, halo, t):
    g = cut3(ldot(t, "ca", jnp.concatenate([cat3(w), cat3(halo)], axis=0)))
    z = rdot(jnp.concatenate(w, axis=0), t, "cz")
    out = []
    for c in range(3):
        s = slice(64 * c, 64 * c + 64)
        adv = w[0] * g[c][0:64] + w[1] * g[c][64:128] + w[2] * z[s, :128]
        out.append(g[c][128:192] + z[s, 128:] - adv)
    return out


def restrict(v, t):
    s = ldot(t, "rxy", cat3(v))
    r = rdot(jnp.concatenate(cut3(s), axis=0), t, "rz")
    return [r[64 * c : 64 * c + 64] for c in range(3)]


def prolong(e, t):
    s = rdot(jnp.concatenate(e, axis=0), t, "pz")
    return cut3(ldot(t, "pxy", jnp.concatenate([s[0:64], s[64:128], s[128:192]], axis=1)))


def wide(x):
    return jnp.concatenate([x, x], axis=1)


def load3(r):
    return [r[c] for c in range(3)]


def store3(r, v):
    for c in range(3):
        r[c] = v[c]


def k_start(flags, v, *outs):
    for c in range(3):
        px = [v[c, 16 * j : 16 * j + 16] for j in range(16)]
        py = [v[c, pl.ds(j, 16, stride=16), :] for j in range(16)]
        send_faces(flags, outs, c, slice(0, 16), px[0], px[15], py[0], py[15])
        parts = []
        for plane in (px, py):
            for row in (EDGE[0], EDGE[15]):
                total = float(row[0]) * plane[0]
                for j in range(1, 16):
                    total = total + float(row[j]) * plane[j]
                parts.append(total)
        send_faces(flags, outs, c, slice(16, 32), *parts)


def k_bulk1(v, t, out):
    store3(out, fine_local(load3(v), t))


def k_post1(flags, v, loc, h1, h2, h3, h4, ta, t, f0, v1, *outs):
    h = (h1, h2, h3, h4)
    halo = [halo_of(flags, h, c, 0, 32) for c in range(3)]
    fine_rate(v, loc, halo, t, f0)
    for c in range(3):
        v1[c] = v[c] + (H / 2.0) * f0[c]
    fine_faces(flags, outs, v1, ta)


def k_bulk2(flags, v, q, t, out, w, *outs):
    vv = load3(v)
    store3(out, fine_local(vv, t))
    w0 = restrict(load3(q), t)
    w1 = restrict(vv, t)
    both = [jnp.concatenate([w0[c], w1[c]], axis=1) for c in range(3)]
    store3(w, both)
    coarse_faces(flags, outs, slice(0, 16), both, t)


def k_post2(flags, v, loc, h1, h2, h3, h4, d1, d2, d3, d4, ta, t, b1, v2, *outs):
    h = (h1, h2, h3, h4)
    halo = [halo_of(flags, h, c, 0, 32) for c in range(3)]
    fine_rate(v, loc, halo, t, b1)
    for c in range(3):
        v2[c] = v[c] + (H / 2.0) * b1[c]
    fine_faces(flags, outs, v2, ta)
    for o, d in zip(outs, (d1, d2, d3, d4)):
        for c in range(3):
            o[c, 32:48] = d[c]


def k_bulk3(v, f0, b1, t, out, w2, fa, fb):
    vv = load3(v)
    store3(out, fine_local(vv, t))
    store3(w2, restrict(vv, t))
    rf = restrict(load3(f0), t)
    rb = restrict(load3(b1), t)
    for c in range(3):
        fa[c] = (H * W0[0]) * rf[c] + (H * W0[1]) * rb[c]
        fb[c] = (H * W1[0]) * rf[c] + (H * W1[1]) * rb[c]


def k_post3(flags, v, loc, h1, h2, h3, h4, w, fa, fb, t, a, vh, b2):
    h = (h1, h2, h3, h4)
    halo = [halo_of(flags, h, c, 0, 32) for c in range(3)]
    fine_rate(v, loc, halo, t, b2)
    rb = restrict(load3(b2), t)
    ww = load3(w)
    chalo = [halo_of(flags, h, c, 32, 48) for c in range(3)]
    cr = coarse_rate(ww, chalo, t)
    for c in range(3):
        t0 = fa[c] + (H * W0[2]) * rb[c]
        t1 = fb[c] + (H * W1[2]) * rb[c]
        start = jnp.where(flags[0] == 1, ww[c][:, :64], (-H / 2.0) * cr[c][:, :64])
        a[c] = jnp.concatenate([start + t0, t1 - (H / 2.0) * cr[c][:, 64:]], axis=1)
        vh[c, 0:256] = v[c]
        vh[c, 256:384] = halo[c]


def pair_faces(e, t, out, up, down, left, right):
    for c in range(3):
        out[c, 0:64] = e[c]
        f = ldot(t, "cf", e[c])
        up[c] = f[0:16, :64]
        down[c] = f[16:32, 64:]
        left[c] = f[32:48]
        right[c] = f[48:64]
        out[c, 64:80] = jnp.concatenate([f[0:16, 64:], f[16:32, :64]], axis=1)


def k_begin(flags, own, far, own2, far2, t, even, odd, *outs):
    low, second = flags[1] == 1, flags[3] == 1

    def pair(c, mine, other):
        a = jnp.where(low, other[c], mine[c])
        b = jnp.where(low, mine[c], other[c])
        return jnp.concatenate([
            jnp.concatenate([a[:, :64], b[:, :64]], axis=1), jnp.concatenate([a[:, 64:], b[:, 64:]], axis=1)
        ], axis=0)

    e = []
    for c in range(3):
        p, q = pair(c, own, far), pair(c, own2, far2)
        even[c] = jnp.where(second, q, p)
        odd[c] = jnp.where(second, p, q)
        e.append(even[c, 0:64])
    pair_faces(e, t, *outs)


def pair_step(e, up, down, left, right, r, t, rows):
    ee = [e[c, 0:64] for c in range(3)]
    halo = []
    for c in range(3):
        i = e[c, 64:80]
        halo.append(jnp.concatenate([
            jnp.concatenate([up[c], i[:, 64:]], axis=1), jnp.concatenate([i[:, :64], down[c]], axis=1), left[c], right[c]
        ], axis=0))
    rate = coarse_rate(ee, halo, t)
    return [ee[c] + (H / 2.0) * rate[c] + r[c, rows : rows + 64] for c in range(3)]


def k_chain(e, up, down, left, right, r, t, *outs, rows):
    pair_faces(pair_step(e, up, down, left, right, r, t, rows), t, *outs)


def mine(flags, x):
    return jnp.where(flags[1] == 1, x[:, 64:], x[:, :64])


def k_x0(flags, a2e, b2e, bk, ws, q, vh, t, d, x, loc):
    first, second, late = flags[0] == 1, flags[3] == 1, flags[4] == 1
    for c in range(3):
        k = jnp.where(second, jnp.where(late, b2e[c, 0:64], a2e[c, 0:64]), bk[c, 0:64])
        d[c] = jnp.where(first, 0.0, mine(flags, k) - ws[c])
    pr = prolong(load3(d), t)
    xs = [jnp.where(first, q[c], vh[c, 0:256]) + pr[c] for c in range(3)]
    store3(x, xs)
    store3(loc, fine_local(xs, t))


def k_x1(flags, even, a1o, b1e, b1o, w, v1, t, d, x, loc):
    second, late = flags[3] == 1, flags[4] == 1
    for c in range(3):
        e1 = jnp.where(
            late, jnp.where(second, b1o[c, 0:64], b1e[c, 0:64]), jnp.where(second, a1o[c, 0:64], even[c, 0:64])
        )
        d[c] = mine(flags, e1) - w[c][:, 64:]
    pr = prolong(load3(d), t)
    xs = [v1[c] + pr[c] for c in range(3)]
    store3(x, xs)
    store3(loc, fine_local(xs, t))


def k_dstart(flags, e, up, down, left, right, r, a2e, a2o, b2e, d0, d1, w2, t, d2, *outs):
    second, late = flags[3] == 1, flags[4] == 1
    b2o = pair_step(e, up, down, left, right, r, t, 64)
    for c in range(3):
        e2 = jnp.where(
            late, jnp.where(second, b2o[c], b2e[c, 0:64]), jnp.where(second, a2o[c, 0:64], a2e[c, 0:64])
        )
        d = mine(flags, e2) - w2[c]
        d2[c] = d
        f = ldot(t, "xf", jnp.concatenate([d0[c], d1[c]], axis=1))
        g = ldot(t, "xf", d)
        send_faces(flags, outs, c, slice(0, 16), f[0:16], f[16:32], f[32:48], f[48:64])
        send_faces(flags, outs, c, slice(16, 32), *[wide(g[16 * i : 16 * i + 16]) for i in range(4)])


def k_x2(d, v2, t, x, loc):
    pr = prolong(load3(d), t)
    xs = [v2[c] + pr[c] for c in range(3)]
    store3(x, xs)
    store3(loc, fine_local(xs, t))


def k_ws(vh, t, ws):
    store3(ws, restrict([vh[c, 0:256] for c in range(3)], t))


def k_xpost(flags, x0, x1, x2, l0, l1, l2, h1, h2, h3, h4, a1, a2, a3, a4, b1, b2, b3, b4, v2h, vh, ta, t, u1, d, o1, o2, o3, o4, g0, g1, g2):
    first = flags[0] == 1
    h = (h1, h2, h3, h4)
    lo = [halo_of(flags, h, c, 0, 16) for c in range(3)]
    hi = [halo_of(flags, h, c, 16, 32) for c in range(3)]
    g = (g0, g1, g2)
    for m, (x, loc) in enumerate(((x0, l0), (x1, l1), (x2, l2))):
        co = [lo[c][:, :64] if m == 0 else lo[c][:, 64:] if m == 1 else hi[c][:, :64] for c in range(3)]
        s = rdot(jnp.concatenate(co, axis=0), t, "pz")
        fine = cut3(ldot(t, "ph", jnp.concatenate([s[0:64], s[64:128], s[128:192]], axis=1)))
        halo = []
        for c in range(3):
            if m == 0:
                base = jnp.where(first, halo_of(flags, (a1, a2, a3, a4), c, 0, 32), vh[c, 256:384])
            elif m == 1:
                base = halo_of(flags, (b1, b2, b3, b4), c, 0, 32)
            else:
                base = v2h[c, 256:384]
            halo.append(base + fine[c])
        fine_rate(x, loc, halo, t, g[m])
    for c in range(3):
        u = x0[c] + H * (W0[0] * g[0][c] + W0[1] * g[1][c] + W0[2] * g[2][c])
        u1[c] = u
        d[c] = u + H * (W1[0] * g[0][c] + (W1[1] - 0.5) * g[1][c] + W1[2] * g[2][c])
    fine_faces(flags, (o1, o2, o3, o4), u1, ta)


def k_last(flags, v, d, loc, h1, h2, h3, h4, t, out, acc):
    h = (h1, h2, h3, h4)
    halo = [halo_of(flags, h, c, 0, 32) for c in range(3)]
    fine_rate(v, loc, halo, t, acc)
    for c in range(3):
        out[c] = d[c] + (H / 2.0) * acc[c]


def call(kernel, args, outs, cost=0, scratch=()):
    flat = args
    specs = [
        pl.BlockSpec(memory_space=pltpu.SMEM if a.dtype == jnp.int32 else pltpu.VMEM) for a in flat
    ]
    shapes = [jax.ShapeDtypeStruct(s, F32) for s in outs]
    size = sum(int(np.prod(a.shape)) * a.dtype.itemsize for a in flat) + sum(int(np.prod(s)) * 4 for s in outs)
    return pl.pallas_call(
        kernel,
        out_shape=shapes,
        in_specs=specs,
        out_specs=[pl.BlockSpec(memory_space=pltpu.VMEM) for _ in outs],
        scratch_shapes=[pltpu.VMEM(s, F32) for s in scratch],
        cost_estimate=pl.CostEstimate(flops=cost, bytes_accessed=size, transcendentals=0),
        compiler_params=pltpu.CompilerParams(vmem_limit_bytes=48 * 1024 * 1024),
    )(*flat)


def routes(shift):
    def dev(t, r, c):
        return t * 64 + (r % 16) * 4 + c % 4

    out = []
    for kind in range(4):
        pairs = []
        for t in range(4):
            if not 0 <= t + shift < 4:
                continue
            for r in range(16):
                for c in range(4):
                    if kind == 0:
                        to = (r + 1 if r & 1 else r - 1, c)
                    elif kind == 1:
                        to = (r ^ 1, c)
                    elif kind == 2:
                        to = (r, c ^ 1)
                    else:
                        to = (r, c + 1 if c & 1 else c - 1)
                    pairs.append((dev(t, r, c), dev(t + shift, *to)))
        out.append(pairs)
    return out


def ring_routes(late):
    out = []
    for dk, dz in ((-1, 0), (1, 0), (0, -1), (0, 1)):
        pairs = []
        for t in range(4):
            to = t ^ (2 * late)
            for k in range(8):
                for z in range(8):
                    pairs.append((t * 64 + k * 8 + z, to * 64 + ((k + dk) % 8) * 8 + (z + dz) % 8))
        out.append(pairs)
    return out


def shards(initial):
    ta, tb = jnp.asarray(PACK_A), jnp.asarray(PACK_B)
    space, tm = lax.axis_index("space"), lax.axis_index("tm")
    flags = jnp.stack([(tm == 0).astype(jnp.int32), (space // 4) % 2, space % 2, tm % 2, tm // 2]).astype(jnp.int32)
    here = routes(0)
    ring, cross = ring_routes(0), ring_routes(1)
    after = [(t * 64 + b, (t + 1) % 4 * 64 + b) for t in range(4) for b in range(64)]
    two_on = [(t * 64 + b, (t ^ 2) * 64 + b) for t in range(4) for b in range(64)]
    partner = [(t * 64 + b, (t ^ 1) * 64 + b) for t in range(4) for b in range(64)]

    def swap(pieces, way, order=(0, 1, 2, 3)):
        got = {i: lax.ppermute(pieces[i], AX, way[i]) for i in order}
        return [got[i] for i in range(4)]

    st, pay, co, duo = (3, 256, 128), (3, 32, 128), (3, 64, 64), (3, 64, 128)
    c2pay, bpay = (3, 16, 128), (3, 48, 128)
    faces = [(3, 80, 128), (3, 16, 64), (3, 16, 64), (3, 16, 128), (3, 16, 128)]
    q = initial.reshape(st)
    big = 2_000_000_000
    p = call(k_start, [flags, q], [pay] * 4)
    h1 = swap(p, here)
    (loc,) = call(k_bulk1, [q, tb], [st], big)
    f0, v1, *p = call(k_post1, [flags, q, loc, *h1, ta, tb], [st, st] + [pay] * 4)
    h2 = swap(p, here)
    loc, w, *cp = call(k_bulk2, [flags, v1, q, tb], [st, duo] + [c2pay] * 4, big)
    b1, v2, *p = call(k_post2, [flags, v1, loc, *h2, *cp, ta, tb], [st, st] + [bpay] * 4)
    h3 = swap(p, here)
    loc, w2, fa, fb = call(k_bulk3, [v2, f0, b1, tb], [st, co, co, co], big)
    a, vh = call(k_post3, [flags, v2, loc, *h3, w, fa, fb, tb], [duo, (3, 384, 128)], scratch=[st])
    far = lax.ppermute(a, AX, here[1])
    own2 = lax.ppermute(a, AX, partner)
    vprev = lax.ppermute(vh, AX, after)
    far2 = lax.ppermute(far, AX, partner)
    even, odd, e, *p = call(k_begin, [flags, a, far, own2, far2, tb], [(3, 128, 128)] * 2 + faces)

    def trade(p, way):
        below, above, right, left = swap(p, way, (0, 1, 2, 3))
        return above, below, left, right

    def step(e, p, way, r, rows):
        return call(functools.partial(k_chain, rows=rows), [e, *trade(p, way), r, tb], faces)

    a2e, *p = step(e, p, ring, even, 64)
    a1o, *p = step(a2e, p, ring, odd, 0)
    a2o, *p = step(a1o, p, ring, odd, 64)
    (ws,) = call(k_ws, [vprev, tb], [co])
    bk = lax.ppermute(a2o, AX, two_on)
    bk, ws = lax.optimization_barrier((bk, ws))
    b1e, *p = step(bk, p, cross, even, 0)
    b2e, *p = step(b1e, p, ring, even, 64)
    d0, x0, l0 = call(k_x0, [flags, a2e, b2e, bk, ws, q, vprev, tb], [co, st, st], big)
    b1o, *p = step(b2e, p, ring, odd, 0)
    d1, x1, l1 = call(k_x1, [flags, even, a1o, b1e, b1o, w, v1, tb], [co, st, st], big)
    d2, *p = call(
        k_dstart, [flags, b1o, *trade(p, ring), odd, a2e, a2o, b2e, d0, d1, w2, tb], [co] + [pay] * 4
    )
    h = swap(p, here)
    x2, l2 = call(k_x2, [d2, v2, tb], [st, st], big)
    u1, d, *p = call(
        k_xpost, [flags, x0, x1, x2, l0, l1, l2, *h, *h1, *h2, vh, vprev, ta, tb], [st, st] + [pay] * 4,
        scratch=[st] * 3,
    )
    h = swap(p, here)
    (loc,) = call(k_bulk1, [u1, tb], [st], big)
    (out,) = call(k_last, [flags, u1, d, loc, *h, tb], [st], scratch=[st])
    return out.reshape(initial.shape)


def solution(mesh):
    return jax.shard_map(
        shards,
        mesh=mesh,
        in_specs=(P("tm", None, "space", None, None, None),),
        out_specs=P("tm", None, "space", None, None, None),
        check_vma=False,
    )
```

```python
import functools

import jax
import jax.numpy as jnp
import ml_dtypes
import numpy as np
from jax import lax
from jax.experimental import pallas as pl
from jax.experimental.pallas import tpu as pltpu
from jax.sharding import PartitionSpec as P


H = 0.001
NU = 0.05
W0 = (5.0 / 24.0, 1.0 / 3.0, -1.0 / 24.0)
W1 = (-1.0 / 24.0, 1.0 / 3.0, 5.0 / 24.0)
F32 = jnp.float32
BF = jnp.bfloat16
AX = ("tm", "space")


def cheb_tables(count):
    index = np.arange(count)
    points = -np.cos(np.pi * index / (count - 1))
    weights = (-1.0) ** index
    weights[0] = weights[0] * 0.5
    weights[-1] = weights[-1] * 0.5
    return points, weights


def diff_matrix(points, weights):
    count = points.shape[0]
    ident = np.eye(count)
    gaps = points[:, None] - points[None, :] + ident
    matrix = weights[None, :] / weights[:, None] / gaps
    matrix = matrix * (1.0 - ident)
    return matrix - ident * matrix.sum(axis=1)[:, None]


def interp_matrix(points, weights, targets):
    gaps = targets[:, None] - points[None, :]
    exact_hit = np.abs(gaps) < 1e-12
    safe_gaps = np.where(exact_hit, 1.0, gaps)
    terms = weights[None, :] / safe_gaps
    matrix = terms / terms.sum(axis=1, keepdims=True)
    any_hit = exact_hit.any(axis=1)
    return np.where(any_hit[:, None], np.where(exact_hit, 1.0, 0.0), matrix)


def lifted_matrix(count, length, periodic):
    points, weights = cheb_tables(count)
    matrix = np.kron(np.eye(length // count), diff_matrix(points, weights))
    lift = (count - 1) ** 2 / 2.0
    for place in range(length):
        if place % count == 0:
            matrix[place, place] += lift
            if place > 0:
                matrix[place, place - 1] -= lift
            elif periodic:
                matrix[place, length - 1] -= lift
        if place % count == count - 1:
            matrix[place, place] -= lift
            if place < length - 1:
                matrix[place, place + 1] += lift
            elif periodic:
                matrix[place, 0] += lift
    return matrix


def hilo(matrix):
    hi = matrix.astype(ml_dtypes.bfloat16)
    lo = (matrix - hi.astype(np.float64)).astype(ml_dtypes.bfloat16)
    return hi, lo


def left_pieces(matrix):
    h, l = hilo(matrix)
    if matrix.shape[1] <= 64:
        return [np.concatenate([h, l, h], 1)]
    if matrix.shape[1] <= 128:
        return [np.concatenate([h, h], 1), l]
    return [h, l]


def right_pieces(matrix):
    h, l = hilo(matrix)
    return [np.concatenate([h, h], 0), l]


def level_ops(n, zlen):
    m = lifted_matrix(n, n, False)
    c = (n - 1) ** 2 / 2.0
    eye = np.eye(n)
    e0, e1 = eye[:, :1], eye[:, -1:]
    mm = m @ m - c * c * (e0 @ e0.T + e1 @ e1.T)
    a = np.concatenate([np.kron(m, eye), np.kron(eye, m), NU * (np.kron(mm, eye) + np.kron(eye, mm))])
    zero = np.zeros((n, 1))
    gb, ga = -c * e0, c * e1
    lb = [-c * NU * m[:, :1], -c * NU * e0]
    la = [c * NU * m[:, -1:], c * NU * e1]

    def bx(col):
        return np.kron(col, eye)

    def by(col):
        return np.kron(eye, col)

    hx = np.concatenate([bx(gb), bx(zero), bx(ga), bx(zero), by(zero), by(zero), by(zero), by(zero)], 1)
    hy = np.concatenate([bx(zero), bx(zero), bx(zero), bx(zero), by(gb), by(zero), by(ga), by(zero)], 1)
    hl = np.concatenate([bx(lb[0]), bx(lb[1]), bx(la[0]), bx(la[1]), by(lb[0]), by(lb[1]), by(la[0]), by(la[1])], 1)
    h = np.concatenate([hx, hy, hl])
    z = lifted_matrix(n, zlen, True)
    return m, a, h, z.T, NU * (z @ z).T


def faces_matrix(rows_val, rows_par, n_in):
    eye = np.eye(n_in)
    out = []
    for side in (0, 1):
        out += [np.kron(rows_val[side][None], eye), np.kron(rows_par[side][None], eye)]
    for side in (0, 1):
        out += [np.kron(eye, rows_val[side][None]), np.kron(eye, rows_par[side][None])]
    return np.concatenate(out)


def tables():
    fp, fw = cheb_tables(16)
    cp, cw = cheb_tables(8)
    r = interp_matrix(fp, fw, cp)
    p = interp_matrix(cp, cw, fp)
    t = {}
    m, a, h, zg, zl = level_ops(16, 128)
    t["fa"] = a
    t["fh"] = h[512:]
    t["fz"] = np.concatenate([zg, zl], 1)
    part = faces_matrix((m[0] * 0, m[0] * 0), (m[0], m[-1]), 16)
    t["fe"] = np.concatenate([part[16:32], part[48:64], part[80:96], part[112:128]])
    pr = p @ r
    proj = faces_matrix((m[0] * 0, m[0] * 0), (m[0] @ pr, m[-1] @ pr), 16)
    t["fp"] = np.concatenate([proj[16:32], proj[48:64], proj[80:96], proj[112:128]])
    t["pl"] = np.kron(np.eye(8), pr)
    t["zr"] = np.kron(np.eye(8), pr).T
    mc, ac, hc, zgc, zlc = level_ops(8, 64)
    t["ca"] = np.concatenate([ac, hc], 1)
    two = np.eye(2)
    t["cz"] = np.concatenate([np.kron(two, zgc), np.kron(two, zlc)], 1)
    e8 = np.eye(8)
    t["cf"] = faces_matrix((e8[0], e8[-1]), (mc[0], mc[-1]), 8)
    mp = m @ p
    t["xf"] = faces_matrix((p[0], p[-1]), (mp[0], mp[-1]), 8)
    t["rxy"] = np.kron(r, r)
    t["rz"] = np.kron(np.eye(8), r).T
    t["pxy"] = np.kron(p, p)
    t["pz"] = np.kron(np.eye(8), p).T
    t["ph"] = np.kron(np.eye(8), p)
    return t


def packed(names, table):
    where, rows, at = {}, [], 0
    for name in names:
        for i, piece in enumerate((right_pieces if name in RIGHT else left_pieces)(table[name])):
            n, k = piece.shape
            where[name, i] = (at, n, k)
            full = np.zeros((-(-n // 16) * 16, 256), ml_dtypes.bfloat16)
            full[:n, :k] = piece
            rows.append(full)
            at += full.shape[0]
    return np.concatenate(rows), where


RIGHT = ("fz", "cz", "rz", "pz", "zr")
TABLES = tables()
EDGE = lifted_matrix(16, 16, False)
PACK_A, WHERE = packed(["fe", "fp"], TABLES)
PACK_B, WHERE_B = packed([n for n in TABLES if n not in ("fe", "fp")], TABLES)
WHERE.update(WHERE_B)


def split(x):
    hi = x.astype(BF)
    lo = (x - hi.astype(F32)).astype(BF)
    return hi, lo


def mm(a, b):
    return jnp.dot(a, b, preferred_element_type=F32)


def piece(t, name, i):
    at, n, k = WHERE[name, i]
    return t[at : at + n, :k]


def ldot(t, name, x):
    xh, xl = split(x)
    if x.shape[0] <= 64:
        return mm(piece(t, name, 0), jnp.concatenate([xh, xh, xl], axis=0))
    if x.shape[0] <= 128:
        return mm(piece(t, name, 0), jnp.concatenate([xh, xl], axis=0)) + mm(piece(t, name, 1), xh)
    th = piece(t, name, 0)
    return mm(th, xh) + (mm(piece(t, name, 1), xh) + mm(th, xl))


def rdot(x, t, name):
    xh, xl = split(x)
    return mm(jnp.concatenate([xh, xl], axis=1), piece(t, name, 0)) + mm(xh, piece(t, name, 1))


def cat3(v):
    return jnp.concatenate([v[0], v[1], v[2]], axis=1)


def cut3(x, width=128):
    return [x[:, i * width : (i + 1) * width] for i in range(3)]


def fine_local(v, t):
    g = ldot(t, "fa", cat3(v))
    z = rdot(jnp.concatenate(v, axis=0), t, "fz")
    out = []
    for c in range(3):
        s = slice(128 * c, 128 * c + 128)
        zc = z[256 * c : 256 * c + 256]
        adv = v[0] * g[0:256, s] + v[1] * g[256:512, s] + v[2] * zc[:, :128]
        out.append(g[512:768, s] + zc[:, 128:] - adv)
    return out


def fine_rate(v, loc, halo, t, acc):
    k = ldot(t, "fh", cat3(halo))
    c = 112.5
    low, high = pl.ds(0, 16, stride=16), pl.ds(15, 16, stride=16)
    vlow, vhigh = v[1, low, :], v[1, high, :]
    for i in range(3):
        r = loc[i] + k[:, 128 * i : 128 * i + 128]
        acc[i, 16:240] = r[16:240]
        acc[i, 0:16] = r[0:16] + c * v[0, 0:16] * halo[i][0:16]
        acc[i, 240:256] = r[240:256] - c * v[0, 240:256] * halo[i][32:48]
        acc[i, low, :] = acc[i, low, :] + c * vlow * halo[i][64:80]
        acc[i, high, :] = acc[i, high, :] - c * vhigh * halo[i][96:112]


def halo_of(flags, h, c, lo, hi):
    p2, p1, c1, c2 = [r[c, lo:hi] for r in h]
    rodd, codd = flags[1] == 1, flags[2] == 1
    return jnp.concatenate(
        [jnp.where(rodd, p1, p2), jnp.where(rodd, p2, p1), jnp.where(codd, c1, c2), jnp.where(codd, c2, c1)], axis=0
    )


def send_faces(flags, outs, c, rows, xlo, xhi, ylo, yhi):
    rodd, codd = flags[1] == 1, flags[2] == 1
    outs[0][c, rows] = jnp.where(rodd, xhi, xlo)
    outs[1][c, rows] = jnp.where(rodd, xlo, xhi)
    outs[2][c, rows] = jnp.where(codd, ylo, yhi)
    outs[3][c, rows] = jnp.where(codd, yhi, ylo)


def fine_faces(flags, outs, vref, t, proj=0):
    v = [vref[c] for c in range(3)]
    part = ldot(t, "fe", cat3(v))
    for c in range(3):
        pc = part[:, 128 * c : 128 * c + 128]
        send_faces(
            flags, outs, c, slice(0, 16),
            v[c][0:16], v[c][240:256],
            vref[c, pl.ds(0, 16, stride=16), :], vref[c, pl.ds(15, 16, stride=16), :],
        )
        send_faces(flags, outs, c, slice(16, 32), pc[0:16], pc[16:32], pc[32:48], pc[48:64])
    if proj:
        part = ldot(t, "fp", cat3(v))
        for c in range(3):
            pc = part[:, 128 * c : 128 * c + 128]
            send_faces(flags, outs, c, slice(proj, proj + 16), pc[0:16], pc[16:32], pc[32:48], pc[48:64])


def coarse_faces(flags, outs, rows, e, t):
    for c in range(3):
        f = ldot(t, "cf", e[c])
        send_faces(flags, outs, c, rows, f[0:16], f[16:32], f[32:48], f[48:64])


def coarse_rate(w, halo, t):
    g = cut3(ldot(t, "ca", jnp.concatenate([cat3(w), cat3(halo)], axis=0)))
    z = rdot(jnp.concatenate(w, axis=0), t, "cz")
    out = []
    for c in range(3):
        s = slice(64 * c, 64 * c + 64)
        adv = w[0] * g[c][0:64] + w[1] * g[c][64:128] + w[2] * z[s, :128]
        out.append(g[c][128:192] + z[s, 128:] - adv)
    return out


def restrict(v, t):
    s = ldot(t, "rxy", cat3(v))
    r = rdot(jnp.concatenate(cut3(s), axis=0), t, "rz")
    return [r[64 * c : 64 * c + 64] for c in range(3)]


def prolong(e, t):
    s = rdot(jnp.concatenate(e, axis=0), t, "pz")
    return cut3(ldot(t, "pxy", jnp.concatenate([s[0:64], s[64:128], s[128:192]], axis=1)))


def load3(r):
    return [r[c] for c in range(3)]


def store3(r, v):
    for c in range(3):
        r[c] = v[c]


def k_start(flags, v, *outs):
    for c in range(3):
        px = [v[c, 16 * j : 16 * j + 16] for j in range(16)]
        py = [v[c, pl.ds(j, 16, stride=16), :] for j in range(16)]
        send_faces(flags, outs, c, slice(0, 16), px[0], px[15], py[0], py[15])
        parts = []
        for plane in (px, py):
            for row in (EDGE[0], EDGE[15]):
                total = float(row[0]) * plane[0]
                for j in range(1, 16):
                    total = total + float(row[j]) * plane[j]
                parts.append(total)
        send_faces(flags, outs, c, slice(16, 32), *parts)


def k_bulk1(v, t, out):
    store3(out, fine_local(load3(v), t))


def k_post1(flags, v, loc, h1, h2, h3, h4, ta, t, f0, v1, *outs):
    h = (h1, h2, h3, h4)
    halo = [halo_of(flags, h, c, 0, 32) for c in range(3)]
    fine_rate(v, loc, halo, t, f0)
    for c in range(3):
        v1[c] = v[c] + (H / 2.0) * f0[c]
    fine_faces(flags, outs, v1, ta, 32)


def k_bulk2(flags, v, q, t, out, w, *outs):
    vv = load3(v)
    store3(out, fine_local(vv, t))
    w0 = restrict(load3(q), t)
    w1 = restrict(vv, t)
    both = [jnp.concatenate([w0[c], w1[c]], axis=1) for c in range(3)]
    store3(w, both)
    coarse_faces(flags, outs, slice(0, 16), both, t)


def k_post2(flags, v, loc, h1, h2, h3, h4, d1, d2, d3, d4, ta, t, b1, v2, *outs):
    h = (h1, h2, h3, h4)
    halo = [halo_of(flags, h, c, 0, 32) for c in range(3)]
    fine_rate(v, loc, halo, t, b1)
    for c in range(3):
        v2[c] = v[c] + (H / 2.0) * b1[c]
    fine_faces(flags, outs, v2, ta, 48)
    for o, d in zip(outs, (d1, d2, d3, d4)):
        for c in range(3):
            o[c, 32:48] = d[c]


def k_bulk3(v, f0, b1, t, out, w2, fa, fb):
    vv = load3(v)
    store3(out, fine_local(vv, t))
    store3(w2, restrict(vv, t))
    rf = restrict(load3(f0), t)
    rb = restrict(load3(b1), t)
    for c in range(3):
        fa[c] = (H * W0[0]) * rf[c] + (H * W0[1]) * rb[c]
        fb[c] = (H * W1[0]) * rf[c] + (H * W1[1]) * rb[c]


def k_post3(flags, v, loc, h1, h2, h3, h4, w, fa, fb, t, a, b2):
    h = (h1, h2, h3, h4)
    halo = [halo_of(flags, h, c, 0, 32) for c in range(3)]
    fine_rate(v, loc, halo, t, b2)
    rb = restrict(load3(b2), t)
    ww = load3(w)
    chalo = [halo_of(flags, h, c, 32, 48) for c in range(3)]
    cr = coarse_rate(ww, chalo, t)
    for c in range(3):
        t0 = fa[c] + (H * W0[2]) * rb[c]
        t1 = fb[c] + (H * W1[2]) * rb[c]
        start = jnp.where(flags[0] == 1, ww[c][:, :64], (-H / 2.0) * cr[c][:, :64])
        a[c] = jnp.concatenate([start + t0, t1 - (H / 2.0) * cr[c][:, 64:]], axis=1)


def base_halo(flags, h, at, t):
    own = [halo_of(flags, h, c, 0, 32) for c in range(3)]
    parts = [halo_of(flags, h, c, at, at + 16) for c in range(3)]
    rows = []
    for c in range(3):
        rows.append(jnp.concatenate(
            [x for d in range(4) for x in (own[c][32 * d : 32 * d + 16], parts[c][16 * d : 16 * d + 16])], axis=0
        ))
    z = rdot(jnp.concatenate(cut3(ldot(t, "pl", cat3(rows))), axis=0), t, "zr")
    return [own[c] - z[128 * c : 128 * c + 128] for c in range(3)]


def k_base1(flags, h1, h2, h3, h4, t, out):
    store3(out, base_halo(flags, (h1, h2, h3, h4), 32, t))


def k_base2(flags, v, h1, h2, h3, h4, t, vh):
    base = base_halo(flags, (h1, h2, h3, h4), 48, t)
    for c in range(3):
        vh[c, 0:256] = v[c]
        vh[c, 256:384] = base[c]


def pair_faces(e, t, out, up, down, left, right):
    for c in range(3):
        out[c, 0:64] = e[c]
        f = ldot(t, "cf", e[c])
        up[c] = f[0:16, :64]
        down[c] = f[16:32, 64:]
        left[c] = f[32:48]
        right[c] = f[48:64]
        out[c, 64:80] = jnp.concatenate([f[0:16, 64:], f[16:32, :64]], axis=1)


def k_begin(flags, own, far, own2, far2, t, even, odd, *outs):
    low, second = flags[1] == 1, flags[3] == 1

    def pair(c, mine, other):
        a = jnp.where(low, other[c], mine[c])
        b = jnp.where(low, mine[c], other[c])
        return jnp.concatenate([
            jnp.concatenate([a[:, :64], b[:, :64]], axis=1), jnp.concatenate([a[:, 64:], b[:, 64:]], axis=1)
        ], axis=0)

    e = []
    for c in range(3):
        p, q = pair(c, own, far), pair(c, own2, far2)
        even[c] = jnp.where(second, q, p)
        odd[c] = jnp.where(second, p, q)
        e.append(even[c, 0:64])
    pair_faces(e, t, *outs)


def pair_step(e, up, down, left, right, r, t, rows):
    ee = [e[c, 0:64] for c in range(3)]
    halo = []
    for c in range(3):
        i = e[c, 64:80]
        halo.append(jnp.concatenate([
            jnp.concatenate([up[c], i[:, 64:]], axis=1), jnp.concatenate([i[:, :64], down[c]], axis=1), left[c], right[c]
        ], axis=0))
    rate = coarse_rate(ee, halo, t)
    return [ee[c] + (H / 2.0) * rate[c] + r[c, rows : rows + 64] for c in range(3)]


def k_chain(e, up, down, left, right, r, t, *outs, rows):
    pair_faces(pair_step(e, up, down, left, right, r, t, rows), t, *outs)


def mine(flags, x):
    return jnp.where(flags[1] == 1, x[:, 64:], x[:, :64])


def k_x0(flags, a2e, b2e, bk, ws, q, vh, t, kp, x, loc):
    first, second, late = flags[0] == 1, flags[3] == 1, flags[4] == 1
    d = []
    for c in range(3):
        k = jnp.where(second, jnp.where(late, b2e[c, 0:64], a2e[c, 0:64]), bk[c, 0:64])
        kp[c] = k
        d.append(jnp.where(first, 0.0, mine(flags, k) - ws[c]))
    pr = prolong(d, t)
    xs = [jnp.where(first, q[c], vh[c, 0:256]) + pr[c] for c in range(3)]
    store3(x, xs)
    store3(loc, fine_local(xs, t))


def k_x1(flags, even, a1o, b1e, b1o, w, v1, t, ep, x, loc):
    second, late = flags[3] == 1, flags[4] == 1
    d = []
    for c in range(3):
        e1 = jnp.where(
            late, jnp.where(second, b1o[c, 0:64], b1e[c, 0:64]), jnp.where(second, a1o[c, 0:64], even[c, 0:64])
        )
        ep[c] = e1
        d.append(mine(flags, e1) - w[c][:, 64:])
    pr = prolong(d, t)
    xs = [v1[c] + pr[c] for c in range(3)]
    store3(x, xs)
    store3(loc, fine_local(xs, t))


def k_dstart(flags, e, up, down, left, right, r, a2e, a2o, b2e, kp, ep, w2, t, d2, row, inner, toleft, toright):
    odd, second, late = flags[1] == 1, flags[3] == 1, flags[4] == 1
    b2o = pair_step(e, up, down, left, right, r, t, 64)
    for c in range(3):
        e2 = jnp.where(
            late, jnp.where(second, b2o[c], b2e[c, 0:64]), jnp.where(second, a2o[c, 0:64], a2e[c, 0:64])
        )
        d2[c] = mine(flags, e2) - w2[c]
        f = ldot(t, "xf", jnp.concatenate([kp[c], ep[c], e2], axis=1))
        lows = [f[:, 128 * m : 128 * m + 64] for m in range(3)]
        highs = [f[:, 128 * m + 64 : 128 * m + 128] for m in range(3)]

        def put(out, cond, rows, lo, hi):
            n = [jnp.where(cond, hi[m][rows[1]], lo[m][rows[0]]) for m in range(3)]
            out[c, 0:16] = jnp.concatenate([n[0], n[1]], axis=1)
            out[c, 16:32] = jnp.concatenate([n[2], n[2]], axis=1)

        xlo, xhi, ylo, yhi = slice(0, 16), slice(16, 32), slice(32, 48), slice(48, 64)
        put(row, odd, (xhi, xlo), highs, lows)
        put(inner, odd, (xlo, xhi), highs, lows)
        put(toleft, flags[5] == 1, (ylo, ylo), lows, highs)
        put(toright, flags[6] == 1, (yhi, yhi), lows, highs)


def k_x2(d, v2, t, x, loc):
    pr = prolong(load3(d), t)
    xs = [v2[c] + pr[c] for c in range(3)]
    store3(x, xs)
    store3(loc, fine_local(xs, t))


def k_ws(vh, t, ws):
    store3(ws, restrict([vh[c, 0:256] for c in range(3)], t))


def k_xpost(flags, x0, x1, x2, l0, l1, l2, inner, row, left, right, a1, a2, a3, a4, base1, v2h, vh, ta, t,
            u1, d, o1, o2, o3, o4, g0, g1, g2):
    first, odd = flags[0] == 1, flags[1] == 1

    def around(c, rows):
        i, r = inner[c, rows], row[c, rows]
        return jnp.concatenate([jnp.where(odd, i, r), jnp.where(odd, r, i), left[c, rows], right[c, rows]], axis=0)

    lo = [around(c, slice(0, 16)) for c in range(3)]
    hi = [around(c, slice(16, 32)) for c in range(3)]
    g = (g0, g1, g2)
    for m, (x, loc) in enumerate(((x0, l0), (x1, l1), (x2, l2))):
        co = [
            jnp.where(first, 0.0, lo[c][:, :64]) if m == 0 else lo[c][:, 64:] if m == 1 else hi[c][:, :64]
            for c in range(3)
        ]
        s = rdot(jnp.concatenate(co, axis=0), t, "pz")
        fine = cut3(ldot(t, "ph", jnp.concatenate([s[0:64], s[64:128], s[128:192]], axis=1)))
        halo = []
        for c in range(3):
            if m == 0:
                base = jnp.where(first, halo_of(flags, (a1, a2, a3, a4), c, 0, 32), vh[c, 256:384])
            elif m == 1:
                base = base1[c]
            else:
                base = v2h[c, 256:384]
            halo.append(base + fine[c])
        fine_rate(x, loc, halo, t, g[m])
    for c in range(3):
        u = x0[c] + H * (W0[0] * g[0][c] + W0[1] * g[1][c] + W0[2] * g[2][c])
        u1[c] = u
        d[c] = u + H * (W1[0] * g[0][c] + (W1[1] - 0.5) * g[1][c] + W1[2] * g[2][c])
    fine_faces(flags, (o1, o2, o3, o4), u1, ta)


def k_last(flags, v, d, loc, h1, h2, h3, h4, t, out, acc):
    h = (h1, h2, h3, h4)
    halo = [halo_of(flags, h, c, 0, 32) for c in range(3)]
    fine_rate(v, loc, halo, t, acc)
    for c in range(3):
        out[c] = d[c] + (H / 2.0) * acc[c]


def call(kernel, args, outs, cost=0, scratch=()):
    flat = args
    specs = [
        pl.BlockSpec(memory_space=pltpu.SMEM if a.dtype == jnp.int32 else pltpu.VMEM) for a in flat
    ]
    shapes = [jax.ShapeDtypeStruct(s, F32) for s in outs]
    size = sum(int(np.prod(a.shape)) * a.dtype.itemsize for a in flat) + sum(int(np.prod(s)) * 4 for s in outs)
    return pl.pallas_call(
        kernel,
        out_shape=shapes,
        in_specs=specs,
        out_specs=[pl.BlockSpec(memory_space=pltpu.VMEM) for _ in outs],
        scratch_shapes=[pltpu.VMEM(s, F32) for s in scratch],
        cost_estimate=pl.CostEstimate(flops=cost, bytes_accessed=size, transcendentals=0),
        compiler_params=pltpu.CompilerParams(vmem_limit_bytes=48 * 1024 * 1024),
    )(*flat)


def routes(shift):
    def dev(t, r, c):
        return t * 64 + (r % 16) * 4 + c % 4

    out = []
    for kind in range(4):
        pairs = []
        for t in range(4):
            if not 0 <= t + shift < 4:
                continue
            for r in range(16):
                for c in range(4):
                    if kind == 0:
                        to = (r + 1 if r & 1 else r - 1, c)
                    elif kind == 1:
                        to = (r ^ 1, c)
                    elif kind == 2:
                        to = (r, c ^ 1)
                    else:
                        to = (r, c + 1 if c & 1 else c - 1)
                    pairs.append((dev(t, r, c), dev(t + shift, *to)))
        out.append(pairs)
    return out


def ring_routes(late):
    out = []
    for dk, dz in ((-1, 0), (1, 0), (0, -1), (0, 1)):
        pairs = []
        for t in range(4):
            to = t ^ (2 * late)
            for k in range(8):
                for z in range(8):
                    pairs.append((t * 64 + k * 8 + z, to * 64 + ((k + dk) % 8) * 8 + (z + dz) % 8))
        out.append(pairs)
    return out


def shards(initial):
    ta, tb = jnp.asarray(PACK_A), jnp.asarray(PACK_B)
    space, tm = lax.axis_index("space"), lax.axis_index("tm")
    flags = jnp.stack([(tm == 0).astype(jnp.int32), (space // 4) % 2, space % 2, tm % 2, tm // 2, (space + 7) % 8 // 4, (space + 1) % 8 // 4]).astype(jnp.int32)
    here = routes(0)
    ring, cross = ring_routes(0), ring_routes(1)
    pair_row = [(i, i // 64 * 64 + (i % 64 + (8 if i % 8 < 4 else 56)) % 64) for i in range(256)]
    after = [(t * 64 + b, (t + 1) % 4 * 64 + b) for t in range(4) for b in range(64)]
    two_on = [(t * 64 + b, (t ^ 2) * 64 + b) for t in range(4) for b in range(64)]
    partner = [(t * 64 + b, (t ^ 1) * 64 + b) for t in range(4) for b in range(64)]

    def swap(pieces, way, order=(0, 1, 2, 3)):
        got = {i: lax.ppermute(pieces[i], AX, way[i]) for i in order}
        return [got[i] for i in range(4)]

    st, pay, co, duo = (3, 256, 128), (3, 32, 128), (3, 64, 64), (3, 64, 128)
    c2pay, bpay, lpay = (3, 16, 128), (3, 48, 128), (3, 64, 128)
    faces = [(3, 80, 128), (3, 16, 64), (3, 16, 64), (3, 16, 128), (3, 16, 128)]
    q = initial.reshape(st)
    big = 2_000_000_000
    p = call(k_start, [flags, q], [pay] * 4)
    h1 = swap(p, here)
    (loc,) = call(k_bulk1, [q, tb], [st], big)
    f0, v1, *p = call(k_post1, [flags, q, loc, *h1, ta, tb], [st, st] + [bpay] * 4)
    h2 = swap(p, here)
    loc, w, *cp = call(k_bulk2, [flags, v1, q, tb], [st, duo] + [c2pay] * 4, big)
    b1, v2, *p = call(k_post2, [flags, v1, loc, *h2, *cp, ta, tb], [st, st] + [lpay] * 4)
    h3 = swap(p, here)
    loc, w2, fa, fb = call(k_bulk3, [v2, f0, b1, tb], [st, co, co, co], big)
    (a,) = call(k_post3, [flags, v2, loc, *h3, w, fa, fb, tb], [duo], scratch=[st])
    (base1,) = call(k_base1, [flags, *h2, tb], [(3, 128, 128)], big)
    far = lax.ppermute(a, AX, here[1])
    own2 = lax.ppermute(a, AX, partner)
    own2, v2late = lax.optimization_barrier((own2, v2))
    (vh,) = call(k_base2, [flags, v2late, *h3, tb], [(3, 384, 128)], big)
    vprev = lax.ppermute(vh, AX, after)
    far2 = lax.ppermute(far, AX, partner)
    even, odd, e, *p = call(k_begin, [flags, a, far, own2, far2, tb], [(3, 128, 128)] * 2 + faces)

    def trade(p, way):
        below, above, right, left = swap(p, way, (0, 1, 2, 3))
        return above, below, left, right

    def step(e, p, way, r, rows):
        return call(functools.partial(k_chain, rows=rows), [e, *trade(p, way), r, tb], faces)

    a2e, *p = step(e, p, ring, even, 64)
    a1o, *p = step(a2e, p, ring, odd, 0)
    a2o, *p = step(a1o, p, ring, odd, 64)
    (ws,) = call(k_ws, [vprev, tb], [co])
    bk = lax.ppermute(a2o, AX, two_on)
    bk, ws = lax.optimization_barrier((bk, ws))
    b1e, *p = step(bk, p, cross, even, 0)
    b2e, *p = step(b1e, p, ring, even, 64)
    kp, x0, l0 = call(k_x0, [flags, a2e, b2e, bk, ws, q, vprev, tb], [duo, st, st], big)
    b1o, *p = step(b2e, p, ring, odd, 0)
    ep, x1, l1 = call(k_x1, [flags, even, a1o, b1e, b1o, w, v1, tb], [duo, st, st], big)
    d2, row, inner, toleft, toright = call(
        k_dstart, [flags, b1o, *trade(p, ring), odd, a2e, a2o, b2e, kp, ep, w2, tb], [co] + [pay] * 4
    )
    row, right, left = (lax.ppermute(x, AX, w) for x, w in ((row, pair_row), (toleft, ring[2]), (toright, ring[3])))
    x2, l2 = call(k_x2, [d2, v2, tb], [st, st], big)
    u1, d, *p = call(
        k_xpost, [flags, x0, x1, x2, l0, l1, l2, inner, row, left, right, *h1, base1, vh, vprev, ta, tb], [st, st] + [pay] * 4,
        scratch=[st] * 3,
    )
    h = swap(p, here)
    (loc,) = call(k_bulk1, [u1, tb], [st], big)
    (out,) = call(k_last, [flags, u1, d, loc, *h, tb], [st], scratch=[st])
    return out.reshape(initial.shape)


def solution(mesh):
    return jax.shard_map(
        shards,
        mesh=mesh,
        in_specs=(P("tm", None, "space", None, None, None),),
        out_specs=P("tm", None, "space", None, None, None),
        check_vma=False,
    )
```

```python
import functools

import jax
import jax.numpy as jnp
import ml_dtypes
import numpy as np
from jax import lax
from jax.experimental import pallas as pl
from jax.experimental.pallas import tpu as pltpu
from jax.sharding import PartitionSpec as P


H = 0.001
NU = 0.05
W0 = (5.0 / 24.0, 1.0 / 3.0, -1.0 / 24.0)
W1 = (-1.0 / 24.0, 1.0 / 3.0, 5.0 / 24.0)
F32 = jnp.float32
BF = jnp.bfloat16
AX = ("tm", "space")


def cheb_tables(count):
    index = np.arange(count)
    points = -np.cos(np.pi * index / (count - 1))
    weights = (-1.0) ** index
    weights[0] = weights[0] * 0.5
    weights[-1] = weights[-1] * 0.5
    return points, weights


def diff_matrix(points, weights):
    count = points.shape[0]
    ident = np.eye(count)
    gaps = points[:, None] - points[None, :] + ident
    matrix = weights[None, :] / weights[:, None] / gaps
    matrix = matrix * (1.0 - ident)
    return matrix - ident * matrix.sum(axis=1)[:, None]


def interp_matrix(points, weights, targets):
    gaps = targets[:, None] - points[None, :]
    exact_hit = np.abs(gaps) < 1e-12
    safe_gaps = np.where(exact_hit, 1.0, gaps)
    terms = weights[None, :] / safe_gaps
    matrix = terms / terms.sum(axis=1, keepdims=True)
    any_hit = exact_hit.any(axis=1)
    return np.where(any_hit[:, None], np.where(exact_hit, 1.0, 0.0), matrix)


def lifted_matrix(count, length, periodic):
    points, weights = cheb_tables(count)
    matrix = np.kron(np.eye(length // count), diff_matrix(points, weights))
    lift = (count - 1) ** 2 / 2.0
    for place in range(length):
        if place % count == 0:
            matrix[place, place] += lift
            if place > 0:
                matrix[place, place - 1] -= lift
            elif periodic:
                matrix[place, length - 1] -= lift
        if place % count == count - 1:
            matrix[place, place] -= lift
            if place < length - 1:
                matrix[place, place + 1] += lift
            elif periodic:
                matrix[place, 0] += lift
    return matrix


def hilo(matrix):
    hi = matrix.astype(ml_dtypes.bfloat16)
    lo = (matrix - hi.astype(np.float64)).astype(ml_dtypes.bfloat16)
    return hi, lo


def left_pieces(matrix):
    h, l = hilo(matrix)
    if matrix.shape[1] <= 64:
        return [np.concatenate([h, l, h], 1)]
    if matrix.shape[1] <= 128:
        return [np.concatenate([h, h], 1), l]
    return [h, l]


def right_pieces(matrix):
    h, l = hilo(matrix)
    return [np.concatenate([h, h], 0), l]


def level_ops(n, zlen):
    m = lifted_matrix(n, n, False)
    c = (n - 1) ** 2 / 2.0
    eye = np.eye(n)
    e0, e1 = eye[:, :1], eye[:, -1:]
    mm = m @ m - c * c * (e0 @ e0.T + e1 @ e1.T)
    a = np.concatenate([np.kron(m, eye), np.kron(eye, m), NU * (np.kron(mm, eye) + np.kron(eye, mm))])
    zero = np.zeros((n, 1))
    gb, ga = -c * e0, c * e1
    lb = [-c * NU * m[:, :1], -c * NU * e0]
    la = [c * NU * m[:, -1:], c * NU * e1]

    def bx(col):
        return np.kron(col, eye)

    def by(col):
        return np.kron(eye, col)

    hx = np.concatenate([bx(gb), bx(zero), bx(ga), bx(zero), by(zero), by(zero), by(zero), by(zero)], 1)
    hy = np.concatenate([bx(zero), bx(zero), bx(zero), bx(zero), by(gb), by(zero), by(ga), by(zero)], 1)
    hl = np.concatenate([bx(lb[0]), bx(lb[1]), bx(la[0]), bx(la[1]), by(lb[0]), by(lb[1]), by(la[0]), by(la[1])], 1)
    h = np.concatenate([hx, hy, hl])
    z = lifted_matrix(n, zlen, True)
    return m, a, h, z.T, NU * (z @ z).T


def faces_matrix(rows_val, rows_par, n_in):
    eye = np.eye(n_in)
    out = []
    for side in (0, 1):
        out += [np.kron(rows_val[side][None], eye), np.kron(rows_par[side][None], eye)]
    for side in (0, 1):
        out += [np.kron(eye, rows_val[side][None]), np.kron(eye, rows_par[side][None])]
    return np.concatenate(out)


def tables():
    fp, fw = cheb_tables(16)
    cp, cw = cheb_tables(8)
    r = interp_matrix(fp, fw, cp)
    p = interp_matrix(cp, cw, fp)
    t = {}
    m, a, h, zg, zl = level_ops(16, 128)
    t["fa"] = a
    t["fh"] = h[512:]
    t["fz"] = np.concatenate([zg, zl], 1)
    part = faces_matrix((m[0] * 0, m[0] * 0), (m[0], m[-1]), 16)
    t["fe"] = np.concatenate([part[16:32], part[48:64], part[80:96], part[112:128]])
    pr = p @ r
    proj = faces_matrix((m[0] * 0, m[0] * 0), (m[0] @ pr, m[-1] @ pr), 16)
    t["r4"] = np.kron(np.eye(4), r)
    t["fp"] = t["r4"] @ np.concatenate([proj[16:32], proj[48:64], proj[80:96], proj[112:128]])
    mc, ac, hc, zgc, zlc = level_ops(8, 64)
    t["ca"] = np.concatenate([ac, hc], 1)
    two = np.eye(2)
    t["cz"] = np.concatenate([np.kron(two, zgc), np.kron(two, zlc)], 1)
    e8 = np.eye(8)
    t["cf"] = faces_matrix((e8[0], e8[-1]), (mc[0], mc[-1]), 8)
    mp = m @ p
    t["xf"] = faces_matrix((p[0], p[-1]), (mp[0], mp[-1]), 8)
    t["rxy"] = np.kron(r, r)
    t["rz"] = np.kron(np.eye(8), r).T
    t["pxy"] = np.kron(p, p)
    t["pz"] = np.kron(np.eye(8), p).T
    t["ph"] = np.kron(np.eye(8), p)
    return t


def packed(names, table):
    where, rows, at = {}, [], 0
    for name in names:
        for i, piece in enumerate((right_pieces if name in RIGHT else left_pieces)(table[name])):
            n, k = piece.shape
            where[name, i] = (at, n, k)
            full = np.zeros((-(-n // 16) * 16, 256), ml_dtypes.bfloat16)
            full[:n, :k] = piece
            rows.append(full)
            at += full.shape[0]
    return np.concatenate(rows), where


RIGHT = ("fz", "cz", "rz", "pz")
TABLES = tables()
EDGE = lifted_matrix(16, 16, False)
PACK_A, WHERE = packed(["fe", "fp"], TABLES)
PACK_B, WHERE_B = packed([n for n in TABLES if n not in ("fe", "fp")], TABLES)
WHERE.update(WHERE_B)


def split(x):
    hi = x.astype(BF)
    lo = (x - hi.astype(F32)).astype(BF)
    return hi, lo


def mm(a, b):
    return jnp.dot(a, b, preferred_element_type=F32)


def piece(t, name, i):
    at, n, k = WHERE[name, i]
    return t[at : at + n, :k]


def ldot(t, name, x):
    xh, xl = split(x)
    if x.shape[0] <= 64:
        return mm(piece(t, name, 0), jnp.concatenate([xh, xh, xl], axis=0))
    if x.shape[0] <= 128:
        return mm(piece(t, name, 0), jnp.concatenate([xh, xl], axis=0)) + mm(piece(t, name, 1), xh)
    th = piece(t, name, 0)
    return mm(th, xh) + (mm(piece(t, name, 1), xh) + mm(th, xl))


def rdot(x, t, name):
    xh, xl = split(x)
    return mm(jnp.concatenate([xh, xl], axis=1), piece(t, name, 0)) + mm(xh, piece(t, name, 1))


def cat3(v):
    return jnp.concatenate([v[0], v[1], v[2]], axis=1)


def cut3(x, width=128):
    return [x[:, i * width : (i + 1) * width] for i in range(3)]


def fine_local(v, t):
    g = ldot(t, "fa", cat3(v))
    z = rdot(jnp.concatenate(v, axis=0), t, "fz")
    out = []
    for c in range(3):
        s = slice(128 * c, 128 * c + 128)
        zc = z[256 * c : 256 * c + 256]
        adv = v[0] * g[0:256, s] + v[1] * g[256:512, s] + v[2] * zc[:, :128]
        out.append(g[512:768, s] + zc[:, 128:] - adv)
    return out


def fine_rate(v, loc, halo, t, acc):
    k = ldot(t, "fh", cat3(halo))
    c = 112.5
    low, high = pl.ds(0, 16, stride=16), pl.ds(15, 16, stride=16)
    vlow, vhigh = v[1, low, :], v[1, high, :]
    for i in range(3):
        r = loc[i] + k[:, 128 * i : 128 * i + 128]
        acc[i, 16:240] = r[16:240]
        acc[i, 0:16] = r[0:16] + c * v[0, 0:16] * halo[i][0:16]
        acc[i, 240:256] = r[240:256] - c * v[0, 240:256] * halo[i][32:48]
        acc[i, low, :] = acc[i, low, :] + c * vlow * halo[i][64:80]
        acc[i, high, :] = acc[i, high, :] - c * vhigh * halo[i][96:112]


def halo_of(flags, h, c, lo, hi):
    p2, p1, c1, c2 = [r[c, lo:hi] for r in h]
    rodd, codd = flags[1] == 1, flags[2] == 1
    return jnp.concatenate(
        [jnp.where(rodd, p1, p2), jnp.where(rodd, p2, p1), jnp.where(codd, c1, c2), jnp.where(codd, c2, c1)], axis=0
    )


def send_faces(flags, outs, c, rows, xlo, xhi, ylo, yhi):
    rodd, codd = flags[1] == 1, flags[2] == 1
    outs[0][c, rows] = jnp.where(rodd, xhi, xlo)
    outs[1][c, rows] = jnp.where(rodd, xlo, xhi)
    outs[2][c, rows] = jnp.where(codd, ylo, yhi)
    outs[3][c, rows] = jnp.where(codd, yhi, ylo)


def fine_faces(flags, outs, vref, t):
    v = [vref[c] for c in range(3)]
    part = ldot(t, "fe", cat3(v))
    for c in range(3):
        pc = part[:, 128 * c : 128 * c + 128]
        send_faces(
            flags, outs, c, slice(0, 16),
            v[c][0:16], v[c][240:256],
            vref[c, pl.ds(0, 16, stride=16), :], vref[c, pl.ds(15, 16, stride=16), :],
        )
        send_faces(flags, outs, c, slice(16, 32), pc[0:16], pc[16:32], pc[32:48], pc[48:64])


def beside(f):
    return jnp.concatenate([f[0:8], f[8:16]], axis=1)


def coarse_faces(flags, outs, c, f):
    send_faces(flags, outs, c, slice(0, 8), *[beside(f[16 * d : 16 * d + 16]) for d in range(4)])


def coarse_rate(w, halo, t):
    g = cut3(ldot(t, "ca", jnp.concatenate([cat3(w), cat3(halo)], axis=0)))
    z = rdot(jnp.concatenate(w, axis=0), t, "cz")
    out = []
    for c in range(3):
        s = slice(64 * c, 64 * c + 64)
        adv = w[0] * g[c][0:64] + w[1] * g[c][64:128] + w[2] * z[s, :128]
        out.append(g[c][128:192] + z[s, 128:] - adv)
    return out


def restrict(v, t):
    s = ldot(t, "rxy", cat3(v))
    r = rdot(jnp.concatenate(cut3(s), axis=0), t, "rz")
    return [r[64 * c : 64 * c + 64] for c in range(3)]


def prolong(e, t):
    s = rdot(jnp.concatenate(e, axis=0), t, "pz")
    return cut3(ldot(t, "pxy", jnp.concatenate([s[0:64], s[64:128], s[128:192]], axis=1)))


def wide(x):
    return jnp.concatenate([x, x], axis=1)


def load3(r):
    return [r[c] for c in range(3)]


def store3(r, v):
    for c in range(3):
        r[c] = v[c]


def k_start(flags, v, *outs):
    for c in range(3):
        px = [v[c, 16 * j : 16 * j + 16] for j in range(16)]
        py = [v[c, pl.ds(j, 16, stride=16), :] for j in range(16)]
        send_faces(flags, outs, c, slice(0, 16), px[0], px[15], py[0], py[15])
        parts = []
        for plane in (px, py):
            for row in (EDGE[0], EDGE[15]):
                total = float(row[0]) * plane[0]
                for j in range(1, 16):
                    total = total + float(row[j]) * plane[j]
                parts.append(total)
        send_faces(flags, outs, c, slice(16, 32), *parts)


def k_bulk1(v, t, out):
    store3(out, fine_local(load3(v), t))


def k_bulkq(flags, q, t, out, w0, *outs):
    qq = load3(q)
    store3(out, fine_local(qq, t))
    w = restrict(qq, t)
    store3(w0, w)
    for c in range(3):
        coarse_faces(flags, outs, c, ldot(t, "cf", w[c]))


def k_post1(flags, v, loc, h1, h2, h3, h4, d1, d2, d3, d4, ta, t, f0, v1, *outs):
    h = (h1, h2, h3, h4)
    halo = [halo_of(flags, h, c, 0, 32) for c in range(3)]
    fine_rate(v, loc, halo, t, f0)
    for c in range(3):
        v1[c] = v[c] + (H / 2.0) * f0[c]
    fine_faces(flags, outs, v1, ta)
    for o, d in zip(outs, (d1, d2, d3, d4)):
        for c in range(3):
            o[c, 32:40] = d[c]


def k_bulk2(flags, v, w0, t, out, w, *outs):
    vv = load3(v)
    store3(out, fine_local(vv, t))
    w1 = restrict(vv, t)
    for c in range(3):
        w[c] = jnp.concatenate([w0[c], w1[c]], axis=1)
        coarse_faces(flags, outs, c, ldot(t, "cf", w1[c]))
        f = ldot(t, "xf", w1[c])
        send_faces(flags, outs, c, slice(8, 16), *[wide(f[16 * d + 8 : 16 * d + 16]) for d in range(4)])


def k_post2(flags, v, loc, h1, h2, h3, h4, d1, d2, d3, d4, ta, t, b1, v2, *outs):
    h = (h1, h2, h3, h4)
    halo = [halo_of(flags, h, c, 0, 32) for c in range(3)]
    fine_rate(v, loc, halo, t, b1)
    for c in range(3):
        v2[c] = v[c] + (H / 2.0) * b1[c]
    fine_faces(flags, outs, v2, ta)
    part = rdot(jnp.concatenate(cut3(ldot(ta, "fp", cat3(load3(v2)))), axis=0), t, "rz")
    for c in range(3):
        send_faces(flags, outs, c, slice(40, 48), *[wide(part[32 * c + 8 * d : 32 * c + 8 * d + 8]) for d in range(4)])
    left = lax.broadcasted_iota(jnp.int32, (8, 128), 1) < 64
    for o, d in zip(outs, (d1, d2, d3, d4)):
        for c in range(3):
            o[c, 32:40] = d[c, 0:8]
            o[c, 40:48] = jnp.where(left, d[c, 8:16], o[c, 40:48])


def k_bulk3(v, f0, b1, t, out, w2, fa, fb):
    vv = load3(v)
    store3(out, fine_local(vv, t))
    store3(w2, restrict(vv, t))
    rf = restrict(load3(f0), t)
    rb = restrict(load3(b1), t)
    for c in range(3):
        fa[c] = (H * W0[0]) * rf[c] + (H * W0[1]) * rb[c]
        fb[c] = (H * W1[0]) * rf[c] + (H * W1[1]) * rb[c]


def k_post3(flags, v, loc, h1, h2, h3, h4, e1, e2, e3, e4, w, fa, fb, t, a, b2):
    h = (h1, h2, h3, h4)
    halo = [halo_of(flags, h, c, 0, 32) for c in range(3)]
    fine_rate(v, loc, halo, t, b2)
    rb = restrict(load3(b2), t)
    ww = load3(w)
    chalo = []
    for c in range(3):
        m0, m1 = halo_of(flags, (e1, e2, e3, e4), c, 32, 40), halo_of(flags, h, c, 32, 40)
        val = jnp.concatenate([m0[:, :64], m1[:, :64]], axis=1)
        par = jnp.concatenate([m0[:, 64:], m1[:, 64:]], axis=1)
        chalo.append(jnp.concatenate(
            [x[8 * d : 8 * d + 8] for d in range(4) for x in (val, par)], axis=0
        ))
    cr = coarse_rate(ww, chalo, t)
    for c in range(3):
        t0 = fa[c] + (H * W0[2]) * rb[c]
        t1 = fb[c] + (H * W1[2]) * rb[c]
        start = jnp.where(flags[0] == 1, ww[c][:, :64], (-H / 2.0) * cr[c][:, :64])
        a[c] = jnp.concatenate([start + t0, t1 - (H / 2.0) * cr[c][:, 64:]], axis=1)


def k_base(flags, v, e1, e2, e3, e4, h1, h2, h3, h4, t, base1, vh):
    e, h = (e1, e2, e3, e4), (h1, h2, h3, h4)
    own1 = [halo_of(flags, e, c, 0, 32) for c in range(3)]
    own2 = [halo_of(flags, h, c, 0, 32) for c in range(3)]
    val1 = [halo_of(flags, h, c, 32, 40) for c in range(3)]
    par = [halo_of(flags, h, c, 40, 48) for c in range(3)]
    faces = [jnp.concatenate([own2[c][32 * d : 32 * d + 16] for d in range(4)], axis=0) for c in range(3)]
    val2 = rdot(jnp.concatenate(cut3(ldot(t, "r4", cat3(faces))), axis=0), t, "rz")

    def weave(a, b):
        return jnp.concatenate([x[8 * d : 8 * d + 8] for d in range(4) for x in (a, b)], axis=0)

    co = [weave(val1[c][:, :64], par[c][:, :64]) for c in range(3)]
    co += [weave(val2[32 * c : 32 * c + 32], par[c][:, 64:]) for c in range(3)]
    s = rdot(jnp.concatenate(co, axis=0), t, "pz")
    fine = ldot(t, "ph", jnp.concatenate([s[64 * i : 64 * i + 64] for i in range(6)], axis=1))
    for c in range(3):
        base1[c] = own1[c] - fine[:, 128 * c : 128 * c + 128]
        vh[c, 0:256] = v[c]
        vh[c, 256:384] = own2[c] - fine[:, 384 + 128 * c : 512 + 128 * c]


def pair_faces(e, t, out, up, down, left, right):
    for c in range(3):
        out[c, 0:64] = e[c]
        f = ldot(t, "cf", e[c])
        up[c] = f[0:16, :64]
        down[c] = f[16:32, 64:]
        left[c] = f[32:48]
        right[c] = f[48:64]
        out[c, 64:80] = jnp.concatenate([f[0:16, 64:], f[16:32, :64]], axis=1)


def k_begin(flags, own, far, own2, far2, t, even, odd, *outs):
    low, second = flags[1] == 1, flags[3] == 1

    def pair(c, mine, other):
        a = jnp.where(low, other[c], mine[c])
        b = jnp.where(low, mine[c], other[c])
        return jnp.concatenate([
            jnp.concatenate([a[:, :64], b[:, :64]], axis=1), jnp.concatenate([a[:, 64:], b[:, 64:]], axis=1)
        ], axis=0)

    e = []
    for c in range(3):
        p, q = pair(c, own, far), pair(c, own2, far2)
        even[c] = jnp.where(second, q, p)
        odd[c] = jnp.where(second, p, q)
        e.append(even[c, 0:64])
    pair_faces(e, t, *outs)


def pair_step(e, up, down, left, right, r, t, rows):
    ee = [e[c, 0:64] for c in range(3)]
    halo = []
    for c in range(3):
        i = e[c, 64:80]
        halo.append(jnp.concatenate([
            jnp.concatenate([up[c], i[:, 64:]], axis=1), jnp.concatenate([i[:, :64], down[c]], axis=1), left[c], right[c]
        ], axis=0))
    rate = coarse_rate(ee, halo, t)
    return [ee[c] + (H / 2.0) * rate[c] + r[c, rows : rows + 64] for c in range(3)]


def k_chain(e, up, down, left, right, r, t, *outs, rows):
    pair_faces(pair_step(e, up, down, left, right, r, t, rows), t, *outs)


def mine(flags, x):
    return jnp.where(flags[1] == 1, x[:, 64:], x[:, :64])


def k_x0(flags, a2e, b2e, bk, ws, q, vh, t, kp, x, loc):
    first, second, late = flags[0] == 1, flags[3] == 1, flags[4] == 1
    d = []
    for c in range(3):
        k = jnp.where(second, jnp.where(late, b2e[c, 0:64], a2e[c, 0:64]), bk[c, 0:64])
        kp[c] = k
        d.append(jnp.where(first, 0.0, mine(flags, k) - ws[c]))
    pr = prolong(d, t)
    xs = [jnp.where(first, q[c], vh[c, 0:256]) + pr[c] for c in range(3)]
    store3(x, xs)
    store3(loc, fine_local(xs, t))


def k_x1(flags, even, a1o, b1e, b1o, w, v1, t, ep, x, loc):
    second, late = flags[3] == 1, flags[4] == 1
    d = []
    for c in range(3):
        e1 = jnp.where(
            late, jnp.where(second, b1o[c, 0:64], b1e[c, 0:64]), jnp.where(second, a1o[c, 0:64], even[c, 0:64])
        )
        ep[c] = e1
        d.append(mine(flags, e1) - w[c][:, 64:])
    pr = prolong(d, t)
    xs = [v1[c] + pr[c] for c in range(3)]
    store3(x, xs)
    store3(loc, fine_local(xs, t))


def k_dstart(flags, e, up, down, left, right, r, a2e, a2o, b2e, kp, ep, w2, t, d2, row, inner, toleft, toright):
    odd, second, late = flags[1] == 1, flags[3] == 1, flags[4] == 1
    b2o = pair_step(e, up, down, left, right, r, t, 64)
    for c in range(3):
        e2 = jnp.where(
            late, jnp.where(second, b2o[c], b2e[c, 0:64]), jnp.where(second, a2o[c, 0:64], a2e[c, 0:64])
        )
        d2[c] = mine(flags, e2) - w2[c]
        f = ldot(t, "xf", jnp.concatenate([kp[c], ep[c], e2], axis=1))
        lows = [f[:, 128 * m : 128 * m + 64] for m in range(3)]
        highs = [f[:, 128 * m + 64 : 128 * m + 128] for m in range(3)]

        def put(out, cond, rows, lo, hi):
            n = [jnp.where(cond, hi[m][rows[1]], lo[m][rows[0]]) for m in range(3)]
            out[c, 0:16] = jnp.concatenate([n[0], n[1]], axis=1)
            out[c, 16:32] = jnp.concatenate([n[2], n[2]], axis=1)

        xlo, xhi, ylo, yhi = slice(0, 16), slice(16, 32), slice(32, 48), slice(48, 64)
        put(row, odd, (xhi, xlo), highs, lows)
        put(inner, odd, (xlo, xhi), highs, lows)
        put(toleft, flags[5] == 1, (ylo, ylo), lows, highs)
        put(toright, flags[6] == 1, (yhi, yhi), lows, highs)


def k_x2(d, v2, t, x, loc):
    pr = prolong(load3(d), t)
    xs = [v2[c] + pr[c] for c in range(3)]
    store3(x, xs)
    store3(loc, fine_local(xs, t))


def k_ws(vh, t, ws):
    store3(ws, restrict([vh[c, 0:256] for c in range(3)], t))


def k_xpost(flags, x0, x1, x2, l0, l1, l2, inner, row, left, right, a1, a2, a3, a4, base1, v2h, vh, ta, t,
            u1, d, o1, o2, o3, o4, g0, g1, g2):
    first, odd = flags[0] == 1, flags[1] == 1

    def around(c, rows):
        i, r = inner[c, rows], row[c, rows]
        return jnp.concatenate([jnp.where(odd, i, r), jnp.where(odd, r, i), left[c, rows], right[c, rows]], axis=0)

    lo = [around(c, slice(0, 16)) for c in range(3)]
    hi = [around(c, slice(16, 32)) for c in range(3)]
    g = (g0, g1, g2)
    for m, (x, loc) in enumerate(((x0, l0), (x1, l1), (x2, l2))):
        co = [
            jnp.where(first, 0.0, lo[c][:, :64]) if m == 0 else lo[c][:, 64:] if m == 1 else hi[c][:, :64]
            for c in range(3)
        ]
        s = rdot(jnp.concatenate(co, axis=0), t, "pz")
        fine = cut3(ldot(t, "ph", jnp.concatenate([s[0:64], s[64:128], s[128:192]], axis=1)))
        halo = []
        for c in range(3):
            if m == 0:
                base = jnp.where(first, halo_of(flags, (a1, a2, a3, a4), c, 0, 32), vh[c, 256:384])
            elif m == 1:
                base = base1[c]
            else:
                base = v2h[c, 256:384]
            halo.append(base + fine[c])
        fine_rate(x, loc, halo, t, g[m])
    for c in range(3):
        u = x0[c] + H * (W0[0] * g[0][c] + W0[1] * g[1][c] + W0[2] * g[2][c])
        u1[c] = u
        d[c] = u + H * (W1[0] * g[0][c] + (W1[1] - 0.5) * g[1][c] + W1[2] * g[2][c])
    fine_faces(flags, (o1, o2, o3, o4), u1, ta)


def k_last(flags, v, d, loc, h1, h2, h3, h4, t, out, acc):
    h = (h1, h2, h3, h4)
    halo = [halo_of(flags, h, c, 0, 32) for c in range(3)]
    fine_rate(v, loc, halo, t, acc)
    for c in range(3):
        out[c] = d[c] + (H / 2.0) * acc[c]


def call(kernel, args, outs, cost=0, scratch=()):
    flat = args
    specs = [
        pl.BlockSpec(memory_space=pltpu.SMEM if a.dtype == jnp.int32 else pltpu.VMEM) for a in flat
    ]
    shapes = [jax.ShapeDtypeStruct(s, F32) for s in outs]
    size = sum(int(np.prod(a.shape)) * a.dtype.itemsize for a in flat) + sum(int(np.prod(s)) * 4 for s in outs)
    return pl.pallas_call(
        kernel,
        out_shape=shapes,
        in_specs=specs,
        out_specs=[pl.BlockSpec(memory_space=pltpu.VMEM) for _ in outs],
        scratch_shapes=[pltpu.VMEM(s, F32) for s in scratch],
        cost_estimate=pl.CostEstimate(flops=cost, bytes_accessed=size, transcendentals=0),
        compiler_params=pltpu.CompilerParams(vmem_limit_bytes=48 * 1024 * 1024),
    )(*flat)


def routes(shift):
    def dev(t, r, c):
        return t * 64 + (r % 16) * 4 + c % 4

    out = []
    for kind in range(4):
        pairs = []
        for t in range(4):
            if not 0 <= t + shift < 4:
                continue
            for r in range(16):
                for c in range(4):
                    if kind == 0:
                        to = (r + 1 if r & 1 else r - 1, c)
                    elif kind == 1:
                        to = (r ^ 1, c)
                    elif kind == 2:
                        to = (r, c ^ 1)
                    else:
                        to = (r, c + 1 if c & 1 else c - 1)
                    pairs.append((dev(t, r, c), dev(t + shift, *to)))
        out.append(pairs)
    return out


def ring_routes(late):
    out = []
    for dk, dz in ((-1, 0), (1, 0), (0, -1), (0, 1)):
        pairs = []
        for t in range(4):
            to = t ^ (2 * late)
            for k in range(8):
                for z in range(8):
                    pairs.append((t * 64 + k * 8 + z, to * 64 + ((k + dk) % 8) * 8 + (z + dz) % 8))
        out.append(pairs)
    return out


def shards(initial):
    ta, tb = jnp.asarray(PACK_A), jnp.asarray(PACK_B)
    space, tm = lax.axis_index("space"), lax.axis_index("tm")
    flags = jnp.stack([(tm == 0).astype(jnp.int32), (space // 4) % 2, space % 2, tm % 2, tm // 2, (space + 7) % 8 // 4, (space + 1) % 8 // 4]).astype(jnp.int32)
    here = routes(0)
    ring, cross = ring_routes(0), ring_routes(1)
    pair_row = [(i, i // 64 * 64 + (i % 64 + (8 if i % 8 < 4 else 56)) % 64) for i in range(256)]
    after = [(t * 64 + b, (t + 1) % 4 * 64 + b) for t in range(4) for b in range(64)]
    two_on = [(t * 64 + b, (t ^ 2) * 64 + b) for t in range(4) for b in range(64)]
    partner = [(t * 64 + b, (t ^ 1) * 64 + b) for t in range(4) for b in range(64)]

    def swap(pieces, way, order=(0, 1, 2, 3)):
        got = {i: lax.ppermute(pieces[i], AX, way[i]) for i in order}
        return [got[i] for i in range(4)]

    st, pay, co, duo = (3, 256, 128), (3, 32, 128), (3, 64, 64), (3, 64, 128)
    c2pay, bpay = (3, 16, 128), (3, 48, 128)
    faces = [(3, 80, 128), (3, 16, 64), (3, 16, 64), (3, 16, 128), (3, 16, 128)]
    q = initial.reshape(st)
    big = 2_000_000_000
    p = call(k_start, [flags, q], [pay] * 4)
    h1 = swap(p, here)
    loc, w0, *cp = call(k_bulkq, [flags, q, tb], [st, co] + [(3, 8, 128)] * 4, big)
    f0, v1, *p = call(k_post1, [flags, q, loc, *h1, *cp, ta, tb], [st, st] + [(3, 40, 128)] * 4)
    h2 = swap(p, here)
    loc, w, *cp = call(k_bulk2, [flags, v1, w0, tb], [st, duo] + [c2pay] * 4, big)
    b1, v2, *p = call(k_post2, [flags, v1, loc, *h2, *cp, ta, tb], [st, st] + [bpay] * 4)
    h3 = swap(p, here)
    loc, w2, fa, fb = call(k_bulk3, [v2, f0, b1, tb], [st, co, co, co], big)
    (a,) = call(k_post3, [flags, v2, loc, *h3, *h2, w, fa, fb, tb], [duo], scratch=[st])
    far = lax.ppermute(a, AX, here[1])
    own2 = lax.ppermute(a, AX, partner)
    own2, v2late = lax.optimization_barrier((own2, v2))
    base1, vh = call(k_base, [flags, v2late, *h2, *h3, tb], [(3, 128, 128), (3, 384, 128)], big)
    vprev = lax.ppermute(vh, AX, after)
    far2 = lax.ppermute(far, AX, partner)
    even, odd, e, *p = call(k_begin, [flags, a, far, own2, far2, tb], [(3, 128, 128)] * 2 + faces)

    def trade(p, way):
        below, above, right, left = swap(p, way, (0, 1, 2, 3))
        return above, below, left, right

    def step(e, p, way, r, rows):
        return call(functools.partial(k_chain, rows=rows), [e, *trade(p, way), r, tb], faces)

    a2e, *p = step(e, p, ring, even, 64)
    a1o, *p = step(a2e, p, ring, odd, 0)
    a2o, *p = step(a1o, p, ring, odd, 64)
    (ws,) = call(k_ws, [vprev, tb], [co])
    bk = lax.ppermute(a2o, AX, two_on)
    bk, ws = lax.optimization_barrier((bk, ws))
    b1e, *p = step(bk, p, cross, even, 0)
    b2e, *p = step(b1e, p, ring, even, 64)
    kp, x0, l0 = call(k_x0, [flags, a2e, b2e, bk, ws, q, vprev, tb], [duo, st, st], big)
    b1o, *p = step(b2e, p, ring, odd, 0)
    ep, x1, l1 = call(k_x1, [flags, even, a1o, b1e, b1o, w, v1, tb], [duo, st, st], big)
    d2, row, inner, toleft, toright = call(
        k_dstart, [flags, b1o, *trade(p, ring), odd, a2e, a2o, b2e, kp, ep, w2, tb], [co] + [pay] * 4
    )
    row, right, left = (lax.ppermute(x, AX, w) for x, w in ((row, pair_row), (toleft, ring[2]), (toright, ring[3])))
    x2, l2 = call(k_x2, [d2, v2, tb], [st, st], big)
    u1, d, *p = call(
        k_xpost, [flags, x0, x1, x2, l0, l1, l2, inner, row, left, right, *h1, base1, vh, vprev, ta, tb], [st, st] + [pay] * 4,
        scratch=[st] * 3,
    )
    h = swap(p, here)
    (loc,) = call(k_bulk1, [u1, tb], [st], big)
    (out,) = call(k_last, [flags, u1, d, loc, *h, tb], [st], scratch=[st])
    return out.reshape(initial.shape)


def solution(mesh):
    return jax.shard_map(
        shards,
        mesh=mesh,
        in_specs=(P("tm", None, "space", None, None, None),),
        out_specs=P("tm", None, "space", None, None, None),
        check_vma=False,
    )
```

```python
import functools

import jax
import jax.numpy as jnp
import ml_dtypes
import numpy as np
from jax import lax
from jax.experimental import pallas as pl
from jax.experimental.pallas import tpu as pltpu
from jax.sharding import PartitionSpec as P


H = 0.001
NU = 0.05
W0 = (5.0 / 24.0, 1.0 / 3.0, -1.0 / 24.0)
W1 = (-1.0 / 24.0, 1.0 / 3.0, 5.0 / 24.0)
F32 = jnp.float32
BF = jnp.bfloat16
AX = ("tm", "space")


def cheb_tables(count):
    index = np.arange(count)
    points = -np.cos(np.pi * index / (count - 1))
    weights = (-1.0) ** index
    weights[0] = weights[0] * 0.5
    weights[-1] = weights[-1] * 0.5
    return points, weights


def diff_matrix(points, weights):
    count = points.shape[0]
    ident = np.eye(count)
    gaps = points[:, None] - points[None, :] + ident
    matrix = weights[None, :] / weights[:, None] / gaps
    matrix = matrix * (1.0 - ident)
    return matrix - ident * matrix.sum(axis=1)[:, None]


def interp_matrix(points, weights, targets):
    gaps = targets[:, None] - points[None, :]
    exact_hit = np.abs(gaps) < 1e-12
    safe_gaps = np.where(exact_hit, 1.0, gaps)
    terms = weights[None, :] / safe_gaps
    matrix = terms / terms.sum(axis=1, keepdims=True)
    any_hit = exact_hit.any(axis=1)
    return np.where(any_hit[:, None], np.where(exact_hit, 1.0, 0.0), matrix)


def lifted_matrix(count, length, periodic):
    points, weights = cheb_tables(count)
    matrix = np.kron(np.eye(length // count), diff_matrix(points, weights))
    lift = (count - 1) ** 2 / 2.0
    for place in range(length):
        if place % count == 0:
            matrix[place, place] += lift
            if place > 0:
                matrix[place, place - 1] -= lift
            elif periodic:
                matrix[place, length - 1] -= lift
        if place % count == count - 1:
            matrix[place, place] -= lift
            if place < length - 1:
                matrix[place, place + 1] += lift
            elif periodic:
                matrix[place, 0] += lift
    return matrix


def hilo(matrix):
    hi = matrix.astype(ml_dtypes.bfloat16)
    lo = (matrix - hi.astype(np.float64)).astype(ml_dtypes.bfloat16)
    return hi, lo


def left_pieces(matrix):
    h, l = hilo(matrix)
    if matrix.shape[1] <= 64:
        return [np.concatenate([h, l, h], 1)]
    if matrix.shape[1] <= 128:
        return [np.concatenate([h, h], 1), l]
    return [h, l]


def right_pieces(matrix):
    h, l = hilo(matrix)
    return [np.concatenate([h, h], 0), l]


def level_ops(n, zlen):
    m = lifted_matrix(n, n, False)
    c = (n - 1) ** 2 / 2.0
    eye = np.eye(n)
    e0, e1 = eye[:, :1], eye[:, -1:]
    mm = m @ m - c * c * (e0 @ e0.T + e1 @ e1.T)
    a = np.concatenate([np.kron(m, eye), np.kron(eye, m), NU * (np.kron(mm, eye) + np.kron(eye, mm))])
    zero = np.zeros((n, 1))
    gb, ga = -c * e0, c * e1
    lb = [-c * NU * m[:, :1], -c * NU * e0]
    la = [c * NU * m[:, -1:], c * NU * e1]

    def bx(col):
        return np.kron(col, eye)

    def by(col):
        return np.kron(eye, col)

    hx = np.concatenate([bx(gb), bx(zero), bx(ga), bx(zero), by(zero), by(zero), by(zero), by(zero)], 1)
    hy = np.concatenate([bx(zero), bx(zero), bx(zero), bx(zero), by(gb), by(zero), by(ga), by(zero)], 1)
    hl = np.concatenate([bx(lb[0]), bx(lb[1]), bx(la[0]), bx(la[1]), by(lb[0]), by(lb[1]), by(la[0]), by(la[1])], 1)
    h = np.concatenate([hx, hy, hl])
    z = lifted_matrix(n, zlen, True)
    return m, a, h, z.T, NU * (z @ z).T


def faces_matrix(rows_val, rows_par, n_in):
    eye = np.eye(n_in)
    out = []
    for side in (0, 1):
        out += [np.kron(rows_val[side][None], eye), np.kron(rows_par[side][None], eye)]
    for side in (0, 1):
        out += [np.kron(eye, rows_val[side][None]), np.kron(eye, rows_par[side][None])]
    return np.concatenate(out)


def tables():
    fp, fw = cheb_tables(16)
    cp, cw = cheb_tables(8)
    r = interp_matrix(fp, fw, cp)
    p = interp_matrix(cp, cw, fp)
    t = {}
    m, a, h, zg, zl = level_ops(16, 128)
    t["fa"] = a
    t["fh"] = h[512:]
    t["fz"] = np.concatenate([zg, zl], 1)
    part = faces_matrix((m[0] * 0, m[0] * 0), (m[0], m[-1]), 16)
    t["fe"] = np.concatenate([part[16:32], part[48:64], part[80:96], part[112:128]])
    pr = p @ r
    proj = faces_matrix((m[0] * 0, m[0] * 0), (m[0] @ pr, m[-1] @ pr), 16)
    t["r4"] = np.kron(np.eye(4), r)
    t["fp"] = t["r4"] @ np.concatenate([proj[16:32], proj[48:64], proj[80:96], proj[112:128]])
    mc, ac, hc, zgc, zlc = level_ops(8, 64)
    t["ca"] = np.concatenate([ac, hc], 1)
    two = np.eye(2)
    t["cz"] = np.concatenate([np.kron(two, zgc), np.kron(two, zlc)], 1)
    e8 = np.eye(8)
    t["cf"] = faces_matrix((e8[0], e8[-1]), (mc[0], mc[-1]), 8)
    mp = m @ p
    t["xf"] = faces_matrix((p[0], p[-1]), (mp[0], mp[-1]), 8)
    t["rxy"] = np.kron(r, r)
    t["rz"] = np.kron(np.eye(8), r).T
    t["pxy"] = np.kron(p, p)
    t["pz"] = np.kron(np.eye(8), p).T
    t["ph"] = np.kron(np.eye(8), p)
    t["pv"] = np.kron(np.eye(4), np.concatenate([p, 0.0 * p], 1))
    t["lp"] = t["fh"] @ t["ph"]
    return t


def packed(names, table):
    where, rows, at = {}, [], 0
    for name in names:
        for i, piece in enumerate((right_pieces if name in RIGHT else left_pieces)(table[name])):
            n, k = piece.shape
            where[name, i] = (at, n, k)
            full = np.zeros((-(-n // 16) * 16, 256), ml_dtypes.bfloat16)
            full[:n, :k] = piece
            rows.append(full)
            at += full.shape[0]
    return np.concatenate(rows), where


RIGHT = ("fz", "cz", "rz", "pz")
TABLES = tables()
EDGE = lifted_matrix(16, 16, False)
PACK_A, WHERE = packed(["fe", "fp"], TABLES)
PACK_B, WHERE_B = packed([n for n in TABLES if n not in ("fe", "fp")], TABLES)
WHERE.update(WHERE_B)


def split(x):
    hi = x.astype(BF)
    lo = (x - hi.astype(F32)).astype(BF)
    return hi, lo


def mm(a, b):
    return jnp.dot(a, b, preferred_element_type=F32)


def piece(t, name, i):
    at, n, k = WHERE[name, i]
    return t[at : at + n, :k]


def ldot(t, name, x):
    xh, xl = split(x)
    if x.shape[0] <= 64:
        return mm(piece(t, name, 0), jnp.concatenate([xh, xh, xl], axis=0))
    if x.shape[0] <= 128:
        return mm(piece(t, name, 0), jnp.concatenate([xh, xl], axis=0)) + mm(piece(t, name, 1), xh)
    th = piece(t, name, 0)
    return mm(th, xh) + (mm(piece(t, name, 1), xh) + mm(th, xl))


def rdot(x, t, name):
    xh, xl = split(x)
    return mm(jnp.concatenate([xh, xl], axis=1), piece(t, name, 0)) + mm(xh, piece(t, name, 1))


def cat3(v):
    return jnp.concatenate([v[0], v[1], v[2]], axis=1)


def cut3(x, width=128):
    return [x[:, i * width : (i + 1) * width] for i in range(3)]


def fine_local(v, t):
    g = ldot(t, "fa", cat3(v))
    z = rdot(jnp.concatenate(v, axis=0), t, "fz")
    out = []
    for c in range(3):
        s = slice(128 * c, 128 * c + 128)
        zc = z[256 * c : 256 * c + 256]
        adv = v[0] * g[0:256, s] + v[1] * g[256:512, s] + v[2] * zc[:, :128]
        out.append(g[512:768, s] + zc[:, 128:] - adv)
    return out


def fine_rate(v, loc, halo, t, acc):
    k = ldot(t, "fh", cat3(halo))
    c = 112.5
    low, high = pl.ds(0, 16, stride=16), pl.ds(15, 16, stride=16)
    vlow, vhigh = v[1, low, :], v[1, high, :]
    for i in range(3):
        r = loc[i] + k[:, 128 * i : 128 * i + 128]
        acc[i, 16:240] = r[16:240]
        acc[i, 0:16] = r[0:16] + c * v[0, 0:16] * halo[i][0:16]
        acc[i, 240:256] = r[240:256] - c * v[0, 240:256] * halo[i][32:48]
        acc[i, low, :] = acc[i, low, :] + c * vlow * halo[i][64:80]
        acc[i, high, :] = acc[i, high, :] - c * vhigh * halo[i][96:112]


def halo_of(flags, h, c, lo, hi):
    p2, p1, c1, c2 = [r[c, lo:hi] for r in h]
    rodd, codd = flags[1] == 1, flags[2] == 1
    return jnp.concatenate(
        [jnp.where(rodd, p1, p2), jnp.where(rodd, p2, p1), jnp.where(codd, c1, c2), jnp.where(codd, c2, c1)], axis=0
    )


def send_faces(flags, outs, c, rows, xlo, xhi, ylo, yhi):
    rodd, codd = flags[1] == 1, flags[2] == 1
    outs[0][c, rows] = jnp.where(rodd, xhi, xlo)
    outs[1][c, rows] = jnp.where(rodd, xlo, xhi)
    outs[2][c, rows] = jnp.where(codd, ylo, yhi)
    outs[3][c, rows] = jnp.where(codd, yhi, ylo)


def fine_faces(flags, outs, vref, t):
    v = [vref[c] for c in range(3)]
    part = ldot(t, "fe", cat3(v))
    for c in range(3):
        pc = part[:, 128 * c : 128 * c + 128]
        send_faces(
            flags, outs, c, slice(0, 16),
            v[c][0:16], v[c][240:256],
            vref[c, pl.ds(0, 16, stride=16), :], vref[c, pl.ds(15, 16, stride=16), :],
        )
        send_faces(flags, outs, c, slice(16, 32), pc[0:16], pc[16:32], pc[32:48], pc[48:64])


def beside(f):
    return jnp.concatenate([f[0:8], f[8:16]], axis=1)


def coarse_faces(flags, outs, c, f):
    send_faces(flags, outs, c, slice(0, 8), *[beside(f[16 * d : 16 * d + 16]) for d in range(4)])


def coarse_rate(w, halo, t):
    g = cut3(ldot(t, "ca", jnp.concatenate([cat3(w), cat3(halo)], axis=0)))
    z = rdot(jnp.concatenate(w, axis=0), t, "cz")
    out = []
    for c in range(3):
        s = slice(64 * c, 64 * c + 64)
        adv = w[0] * g[c][0:64] + w[1] * g[c][64:128] + w[2] * z[s, :128]
        out.append(g[c][128:192] + z[s, 128:] - adv)
    return out


def restrict(v, t):
    s = ldot(t, "rxy", cat3(v))
    r = rdot(jnp.concatenate(cut3(s), axis=0), t, "rz")
    return [r[64 * c : 64 * c + 64] for c in range(3)]


def prolong(e, t):
    s = rdot(jnp.concatenate(e, axis=0), t, "pz")
    return cut3(ldot(t, "pxy", jnp.concatenate([s[0:64], s[64:128], s[128:192]], axis=1)))


def wide(x):
    return jnp.concatenate([x, x], axis=1)


def load3(r):
    return [r[c] for c in range(3)]


def store3(r, v):
    for c in range(3):
        r[c] = v[c]


def k_start(flags, v, *outs):
    for c in range(3):
        px = [v[c, 16 * j : 16 * j + 16] for j in range(16)]
        py = [v[c, pl.ds(j, 16, stride=16), :] for j in range(16)]
        send_faces(flags, outs, c, slice(0, 16), px[0], px[15], py[0], py[15])
        parts = []
        for plane in (px, py):
            for row in (EDGE[0], EDGE[15]):
                total = float(row[0]) * plane[0]
                for j in range(1, 16):
                    total = total + float(row[j]) * plane[j]
                parts.append(total)
        send_faces(flags, outs, c, slice(16, 32), *parts)


def k_bulk1(v, t, out):
    store3(out, fine_local(load3(v), t))


def k_bulkq(flags, q, t, out, w0, *outs):
    qq = load3(q)
    store3(out, fine_local(qq, t))
    w = restrict(qq, t)
    store3(w0, w)
    for c in range(3):
        coarse_faces(flags, outs, c, ldot(t, "cf", w[c]))


def k_post1(flags, v, loc, h1, h2, h3, h4, d1, d2, d3, d4, ta, t, f0, v1, *outs):
    h = (h1, h2, h3, h4)
    halo = [halo_of(flags, h, c, 0, 32) for c in range(3)]
    fine_rate(v, loc, halo, t, f0)
    for c in range(3):
        v1[c] = v[c] + (H / 2.0) * f0[c]
    fine_faces(flags, outs, v1, ta)
    for o, d in zip(outs, (d1, d2, d3, d4)):
        for c in range(3):
            o[c, 32:40] = d[c]


def k_bulk2(flags, v, w0, t, out, w, *outs):
    vv = load3(v)
    store3(out, fine_local(vv, t))
    w1 = restrict(vv, t)
    for c in range(3):
        w[c] = jnp.concatenate([w0[c], w1[c]], axis=1)
        coarse_faces(flags, outs, c, ldot(t, "cf", w1[c]))
        f = ldot(t, "xf", w1[c])
        send_faces(flags, outs, c, slice(8, 16), *[wide(f[16 * d + 8 : 16 * d + 16]) for d in range(4)])


def k_post2(flags, v, loc, h1, h2, h3, h4, d1, d2, d3, d4, ta, t, b1, v2, *outs):
    h = (h1, h2, h3, h4)
    halo = [halo_of(flags, h, c, 0, 32) for c in range(3)]
    fine_rate(v, loc, halo, t, b1)
    for c in range(3):
        v2[c] = v[c] + (H / 2.0) * b1[c]
    fine_faces(flags, outs, v2, ta)
    part = rdot(jnp.concatenate(cut3(ldot(ta, "fp", cat3(load3(v2)))), axis=0), t, "rz")
    for c in range(3):
        send_faces(flags, outs, c, slice(40, 48), *[wide(part[32 * c + 8 * d : 32 * c + 8 * d + 8]) for d in range(4)])
    left = lax.broadcasted_iota(jnp.int32, (8, 128), 1) < 64
    for o, d in zip(outs, (d1, d2, d3, d4)):
        for c in range(3):
            o[c, 32:40] = d[c, 0:8]
            o[c, 40:48] = jnp.where(left, d[c, 8:16], o[c, 40:48])


def k_bulk3(v, f0, b1, t, out, w2, fa, fb):
    vv = load3(v)
    store3(out, fine_local(vv, t))
    store3(w2, restrict(vv, t))
    rf = restrict(load3(f0), t)
    rb = restrict(load3(b1), t)
    for c in range(3):
        fa[c] = (H * W0[0]) * rf[c] + (H * W0[1]) * rb[c]
        fb[c] = (H * W1[0]) * rf[c] + (H * W1[1]) * rb[c]


def k_post3(flags, v, loc, h1, h2, h3, h4, e1, e2, e3, e4, w, fa, fb, t, a, b2):
    h = (h1, h2, h3, h4)
    halo = [halo_of(flags, h, c, 0, 32) for c in range(3)]
    fine_rate(v, loc, halo, t, b2)
    rb = restrict(load3(b2), t)
    ww = load3(w)
    chalo = []
    for c in range(3):
        m0, m1 = halo_of(flags, (e1, e2, e3, e4), c, 32, 40), halo_of(flags, h, c, 32, 40)
        val = jnp.concatenate([m0[:, :64], m1[:, :64]], axis=1)
        par = jnp.concatenate([m0[:, 64:], m1[:, 64:]], axis=1)
        chalo.append(jnp.concatenate(
            [x[8 * d : 8 * d + 8] for d in range(4) for x in (val, par)], axis=0
        ))
    cr = coarse_rate(ww, chalo, t)
    for c in range(3):
        t0 = fa[c] + (H * W0[2]) * rb[c]
        t1 = fb[c] + (H * W1[2]) * rb[c]
        start = jnp.where(flags[0] == 1, ww[c][:, :64], (-H / 2.0) * cr[c][:, :64])
        a[c] = jnp.concatenate([start + t0, t1 - (H / 2.0) * cr[c][:, 64:]], axis=1)


def k_base(flags, v, e1, e2, e3, e4, h1, h2, h3, h4, t, base1, vh):
    e, h = (e1, e2, e3, e4), (h1, h2, h3, h4)
    own1 = [halo_of(flags, e, c, 0, 32) for c in range(3)]
    own2 = [halo_of(flags, h, c, 0, 32) for c in range(3)]
    val1 = [halo_of(flags, h, c, 32, 40) for c in range(3)]
    par = [halo_of(flags, h, c, 40, 48) for c in range(3)]
    faces = [jnp.concatenate([own2[c][32 * d : 32 * d + 16] for d in range(4)], axis=0) for c in range(3)]
    val2 = rdot(jnp.concatenate(cut3(ldot(t, "r4", cat3(faces))), axis=0), t, "rz")

    def weave(a, b):
        return jnp.concatenate([x[8 * d : 8 * d + 8] for d in range(4) for x in (a, b)], axis=0)

    co = [weave(val1[c][:, :64], par[c][:, :64]) for c in range(3)]
    co += [weave(val2[32 * c : 32 * c + 32], par[c][:, 64:]) for c in range(3)]
    s = rdot(jnp.concatenate(co, axis=0), t, "pz")
    fine = ldot(t, "ph", jnp.concatenate([s[64 * i : 64 * i + 64] for i in range(6)], axis=1))
    for c in range(3):
        base1[c] = own1[c] - fine[:, 128 * c : 128 * c + 128]
        vh[c, 0:256] = v[c]
        vh[c, 256:384] = own2[c] - fine[:, 384 + 128 * c : 512 + 128 * c]


def pair_faces(e, t, out, up, down, left, right):
    for c in range(3):
        out[c, 0:64] = e[c]
        f = ldot(t, "cf", e[c])
        up[c] = f[0:16, :64]
        down[c] = f[16:32, 64:]
        left[c] = f[32:48]
        right[c] = f[48:64]
        out[c, 64:80] = jnp.concatenate([f[0:16, 64:], f[16:32, :64]], axis=1)


def k_begin(flags, own, far, own2, far2, t, even, odd, *outs):
    low, second = flags[1] == 1, flags[3] == 1

    def pair(c, mine, other):
        a = jnp.where(low, other[c], mine[c])
        b = jnp.where(low, mine[c], other[c])
        return jnp.concatenate([
            jnp.concatenate([a[:, :64], b[:, :64]], axis=1), jnp.concatenate([a[:, 64:], b[:, 64:]], axis=1)
        ], axis=0)

    e = []
    for c in range(3):
        p, q = pair(c, own, far), pair(c, own2, far2)
        even[c] = jnp.where(second, q, p)
        odd[c] = jnp.where(second, p, q)
        e.append(even[c, 0:64])
    pair_faces(e, t, *outs)


def pair_step(e, up, down, left, right, r, t, rows):
    ee = [e[c, 0:64] for c in range(3)]
    halo = []
    for c in range(3):
        i = e[c, 64:80]
        halo.append(jnp.concatenate([
            jnp.concatenate([up[c], i[:, 64:]], axis=1), jnp.concatenate([i[:, :64], down[c]], axis=1), left[c], right[c]
        ], axis=0))
    rate = coarse_rate(ee, halo, t)
    return [ee[c] + (H / 2.0) * rate[c] + r[c, rows : rows + 64] for c in range(3)]


def k_chain(e, up, down, left, right, r, t, *outs, rows):
    pair_faces(pair_step(e, up, down, left, right, r, t, rows), t, *outs)


def mine(flags, x):
    return jnp.where(flags[1] == 1, x[:, 64:], x[:, :64])


def k_x0(flags, a2e, b2e, bk, ws, q, vh, t, kp, x, loc):
    first, second, late = flags[0] == 1, flags[3] == 1, flags[4] == 1
    d = []
    for c in range(3):
        k = jnp.where(second, jnp.where(late, b2e[c, 0:64], a2e[c, 0:64]), bk[c, 0:64])
        kp[c] = k
        d.append(jnp.where(first, 0.0, mine(flags, k) - ws[c]))
    pr = prolong(d, t)
    xs = [jnp.where(first, q[c], vh[c, 0:256]) + pr[c] for c in range(3)]
    store3(x, xs)
    store3(loc, fine_local(xs, t))


def k_x1(flags, even, a1o, b1e, b1o, w, v1, t, ep, x, loc):
    second, late = flags[3] == 1, flags[4] == 1
    d = []
    for c in range(3):
        e1 = jnp.where(
            late, jnp.where(second, b1o[c, 0:64], b1e[c, 0:64]), jnp.where(second, a1o[c, 0:64], even[c, 0:64])
        )
        ep[c] = e1
        d.append(mine(flags, e1) - w[c][:, 64:])
    pr = prolong(d, t)
    xs = [v1[c] + pr[c] for c in range(3)]
    store3(x, xs)
    store3(loc, fine_local(xs, t))


def k_dstart(flags, e, up, down, left, right, r, a2e, a2o, b2e, kp, ep, w2, t, d2, row, inner, toleft, toright):
    odd, second, late = flags[1] == 1, flags[3] == 1, flags[4] == 1
    b2o = pair_step(e, up, down, left, right, r, t, 64)
    for c in range(3):
        e2 = jnp.where(
            late, jnp.where(second, b2o[c], b2e[c, 0:64]), jnp.where(second, a2o[c, 0:64], a2e[c, 0:64])
        )
        d2[c] = mine(flags, e2) - w2[c]
        f = ldot(t, "xf", jnp.concatenate([kp[c], ep[c], e2], axis=1))
        lows = [f[:, 128 * m : 128 * m + 64] for m in range(3)]
        highs = [f[:, 128 * m + 64 : 128 * m + 128] for m in range(3)]

        def put(out, cond, rows, lo, hi):
            n = [jnp.where(cond, hi[m][rows[1]], lo[m][rows[0]]) for m in range(3)]
            out[c, 0:16] = jnp.concatenate([n[0], n[1]], axis=1)
            out[c, 16:32] = jnp.concatenate([n[2], n[2]], axis=1)

        xlo, xhi, ylo, yhi = slice(0, 16), slice(16, 32), slice(32, 48), slice(48, 64)
        put(row, odd, (xhi, xlo), highs, lows)
        put(inner, odd, (xlo, xhi), highs, lows)
        put(toleft, flags[5] == 1, (ylo, ylo), lows, highs)
        put(toright, flags[6] == 1, (yhi, yhi), lows, highs)


def k_x2(flags, d, v2, x0, l0, x1, l1, a1, a2, a3, a4, base1, v2h, vh, t, x2, g0, g1, g2):
    first = flags[0] == 1
    pr = prolong(load3(d), t)
    xs = [v2[c] + pr[c] for c in range(3)]
    store3(x2, xs)
    loc = fine_local(xs, t)
    base0 = [jnp.where(first, halo_of(flags, (a1, a2, a3, a4), c, 0, 32), vh[c, 256:384]) for c in range(3)]
    fine_rate(x0, l0, base0, t, g0)
    fine_rate(x1, l1, load3(base1), t, g1)
    fine_rate(x2, loc, [v2h[c, 256:384] for c in range(3)], t, g2)


def k_ws(vh, t, ws):
    store3(ws, restrict([vh[c, 0:256] for c in range(3)], t))


def k_xpost(flags, x0, x1, x2, g0, g1, g2, inner, row, left, right, ta, t, u1, d, o1, o2, o3, o4):
    first, odd = flags[0] == 1, flags[1] == 1

    def around(c, rows):
        i, r = inner[c, rows], row[c, rows]
        return jnp.concatenate([jnp.where(odd, i, r), jnp.where(odd, r, i), left[c, rows], right[c, rows]], axis=0)

    lo = [around(c, slice(0, 16)) for c in range(3)]
    hi = [around(c, slice(16, 32)) for c in range(3)]
    co = [jnp.where(first, 0.0, lo[c][:, :64]) for c in range(3)]
    co += [lo[c][:, 64:] for c in range(3)] + [hi[c][:, :64] for c in range(3)]
    s = rdot(jnp.concatenate(co, axis=0), t, "pz")
    s = [s[64 * i : 64 * i + 64] for i in range(9)]
    val = ldot(t, "pv", jnp.concatenate(s, axis=1))
    val = [val[:, 128 * i : 128 * i + 128] for i in range(9)]
    weights = (W0, (W1[0], W1[1] - 0.5, W1[2]))
    mixed = [w[0] * s[c] + w[1] * s[3 + c] + w[2] * s[6 + c] for w in weights for c in range(3)]
    lift = ldot(t, "lp", jnp.concatenate(mixed, axis=1))
    low, high = pl.ds(0, 16, stride=16), pl.ds(15, 16, stride=16)
    xs, gs = (x0, x1, x2), (g0, g1, g2)
    for i, (w, out) in enumerate(zip(weights, (u1, d))):
        for c in range(3):
            mix = w[0] * gs[0][c] + w[1] * gs[1][c] + w[2] * gs[2][c]
            before = x0[c] if i == 0 else u1[c]
            out[c] = before + H * (mix + lift[:, 384 * i + 128 * c : 384 * i + 128 * c + 128])
            edges = [0.0] * 4
            for m in range(3):
                f, k, x = val[3 * m + c], H * 112.5 * w[m], xs[m]
                edges[0] += k * (x[0, 0:16] * f[0:16])
                edges[1] -= k * (x[0, 240:256] * f[16:32])
                edges[2] += k * (x[1, low, :] * f[32:48])
                edges[3] -= k * (x[1, high, :] * f[48:64])
            out[c, 0:16] = out[c, 0:16] + edges[0]
            out[c, 240:256] = out[c, 240:256] + edges[1]
            out[c, low, :] = out[c, low, :] + edges[2]
            out[c, high, :] = out[c, high, :] + edges[3]
    fine_faces(flags, (o1, o2, o3, o4), u1, ta)


def k_last(flags, v, d, loc, h1, h2, h3, h4, t, out, acc):
    h = (h1, h2, h3, h4)
    halo = [halo_of(flags, h, c, 0, 32) for c in range(3)]
    fine_rate(v, loc, halo, t, acc)
    for c in range(3):
        out[c] = d[c] + (H / 2.0) * acc[c]


def call(kernel, args, outs, cost=0, scratch=()):
    flat = args
    specs = [
        pl.BlockSpec(memory_space=pltpu.SMEM if a.dtype == jnp.int32 else pltpu.VMEM) for a in flat
    ]
    shapes = [jax.ShapeDtypeStruct(s, F32) for s in outs]
    size = sum(int(np.prod(a.shape)) * a.dtype.itemsize for a in flat) + sum(int(np.prod(s)) * 4 for s in outs)
    return pl.pallas_call(
        kernel,
        out_shape=shapes,
        in_specs=specs,
        out_specs=[pl.BlockSpec(memory_space=pltpu.VMEM) for _ in outs],
        scratch_shapes=[pltpu.VMEM(s, F32) for s in scratch],
        cost_estimate=pl.CostEstimate(flops=cost, bytes_accessed=size, transcendentals=0),
        compiler_params=pltpu.CompilerParams(vmem_limit_bytes=48 * 1024 * 1024),
    )(*flat)


def routes(shift):
    def dev(t, r, c):
        return t * 64 + (r % 16) * 4 + c % 4

    out = []
    for kind in range(4):
        pairs = []
        for t in range(4):
            if not 0 <= t + shift < 4:
                continue
            for r in range(16):
                for c in range(4):
                    if kind == 0:
                        to = (r + 1 if r & 1 else r - 1, c)
                    elif kind == 1:
                        to = (r ^ 1, c)
                    elif kind == 2:
                        to = (r, c ^ 1)
                    else:
                        to = (r, c + 1 if c & 1 else c - 1)
                    pairs.append((dev(t, r, c), dev(t + shift, *to)))
        out.append(pairs)
    return out


def ring_routes(late):
    out = []
    for dk, dz in ((-1, 0), (1, 0), (0, -1), (0, 1)):
        pairs = []
        for t in range(4):
            to = t ^ (2 * late)
            for k in range(8):
                for z in range(8):
                    pairs.append((t * 64 + k * 8 + z, to * 64 + ((k + dk) % 8) * 8 + (z + dz) % 8))
        out.append(pairs)
    return out


def shards(initial):
    ta, tb = jnp.asarray(PACK_A), jnp.asarray(PACK_B)
    space, tm = lax.axis_index("space"), lax.axis_index("tm")
    flags = jnp.stack([(tm == 0).astype(jnp.int32), (space // 4) % 2, space % 2, tm % 2, tm // 2, (space + 7) % 8 // 4, (space + 1) % 8 // 4]).astype(jnp.int32)
    here = routes(0)
    ring, cross = ring_routes(0), ring_routes(1)
    pair_row = [(i, i // 64 * 64 + (i % 64 + (8 if i % 8 < 4 else 56)) % 64) for i in range(256)]
    after = [(t * 64 + b, (t + 1) % 4 * 64 + b) for t in range(4) for b in range(64)]
    two_on = [(t * 64 + b, (t ^ 2) * 64 + b) for t in range(4) for b in range(64)]
    partner = [(t * 64 + b, (t ^ 1) * 64 + b) for t in range(4) for b in range(64)]

    def swap(pieces, way, order=(0, 1, 2, 3)):
        got = {i: lax.ppermute(pieces[i], AX, way[i]) for i in order}
        return [got[i] for i in range(4)]

    st, pay, co, duo = (3, 256, 128), (3, 32, 128), (3, 64, 64), (3, 64, 128)
    c2pay, bpay = (3, 16, 128), (3, 48, 128)
    faces = [(3, 80, 128), (3, 16, 64), (3, 16, 64), (3, 16, 128), (3, 16, 128)]
    q = initial.reshape(st)
    big = 2_000_000_000
    p = call(k_start, [flags, q], [pay] * 4)
    h1 = swap(p, here)
    loc, w0, *cp = call(k_bulkq, [flags, q, tb], [st, co] + [(3, 8, 128)] * 4, big)
    f0, v1, *p = call(k_post1, [flags, q, loc, *h1, *cp, ta, tb], [st, st] + [(3, 40, 128)] * 4)
    h2 = swap(p, here)
    loc, w, *cp = call(k_bulk2, [flags, v1, w0, tb], [st, duo] + [c2pay] * 4, big)
    b1, v2, *p = call(k_post2, [flags, v1, loc, *h2, *cp, ta, tb], [st, st] + [bpay] * 4)
    h3 = swap(p, here)
    loc, w2, fa, fb = call(k_bulk3, [v2, f0, b1, tb], [st, co, co, co], big)
    (a,) = call(k_post3, [flags, v2, loc, *h3, *h2, w, fa, fb, tb], [duo], scratch=[st])
    far = lax.ppermute(a, AX, here[1])
    own2 = lax.ppermute(a, AX, partner)
    own2, v2late = lax.optimization_barrier((own2, v2))
    base1, vh = call(k_base, [flags, v2late, *h2, *h3, tb], [(3, 128, 128), (3, 384, 128)], big)
    vprev = lax.ppermute(vh, AX, after)
    far2 = lax.ppermute(far, AX, partner)
    even, odd, e, *p = call(k_begin, [flags, a, far, own2, far2, tb], [(3, 128, 128)] * 2 + faces)

    def trade(p, way):
        below, above, right, left = swap(p, way, (0, 1, 2, 3))
        return above, below, left, right

    def step(e, p, way, r, rows):
        return call(functools.partial(k_chain, rows=rows), [e, *trade(p, way), r, tb], faces)

    a2e, *p = step(e, p, ring, even, 64)
    a1o, *p = step(a2e, p, ring, odd, 0)
    a2o, *p = step(a1o, p, ring, odd, 64)
    (ws,) = call(k_ws, [vprev, tb], [co])
    bk = lax.ppermute(a2o, AX, two_on)
    bk, ws = lax.optimization_barrier((bk, ws))
    b1e, *p = step(bk, p, cross, even, 0)
    b2e, *p = step(b1e, p, ring, even, 64)
    kp, x0, l0 = call(k_x0, [flags, a2e, b2e, bk, ws, q, vprev, tb], [duo, st, st], big)
    b1o, *p = step(b2e, p, ring, odd, 0)
    ep, x1, l1 = call(k_x1, [flags, even, a1o, b1e, b1o, w, v1, tb], [duo, st, st], big)
    d2, row, inner, toleft, toright = call(
        k_dstart, [flags, b1o, *trade(p, ring), odd, a2e, a2o, b2e, kp, ep, w2, tb], [co] + [pay] * 4
    )
    row, right, left = (lax.ppermute(x, AX, w) for x, w in ((row, pair_row), (toleft, ring[2]), (toright, ring[3])))
    x2, g0, g1, g2 = call(
        k_x2, [flags, d2, v2, x0, l0, x1, l1, *h1, base1, vh, vprev, tb], [st] * 4, big
    )
    u1, d, *p = call(
        k_xpost, [flags, x0, x1, x2, g0, g1, g2, inner, row, left, right, ta, tb], [st, st] + [pay] * 4
    )
    h = swap(p, here)
    (loc,) = call(k_bulk1, [u1, tb], [st], big)
    (out,) = call(k_last, [flags, u1, d, loc, *h, tb], [st], scratch=[st])
    return out.reshape(initial.shape)


def solution(mesh):
    return jax.shard_map(
        shards,
        mesh=mesh,
        in_specs=(P("tm", None, "space", None, None, None),),
        out_specs=P("tm", None, "space", None, None, None),
        check_vma=False,
    )
```

```python
import functools

import jax
import jax.numpy as jnp
import ml_dtypes
import numpy as np
from jax import lax
from jax.experimental import pallas as pl
from jax.experimental.pallas import tpu as pltpu
from jax.sharding import PartitionSpec as P


H = 0.001
NU = 0.05
W0 = (5.0 / 24.0, 1.0 / 3.0, -1.0 / 24.0)
W1 = (-1.0 / 24.0, 1.0 / 3.0, 5.0 / 24.0)
F32 = jnp.float32
BF = jnp.bfloat16
AX = ("tm", "space")


def cheb_tables(count):
    index = np.arange(count)
    points = -np.cos(np.pi * index / (count - 1))
    weights = (-1.0) ** index
    weights[0] = weights[0] * 0.5
    weights[-1] = weights[-1] * 0.5
    return points, weights


def diff_matrix(points, weights):
    count = points.shape[0]
    ident = np.eye(count)
    gaps = points[:, None] - points[None, :] + ident
    matrix = weights[None, :] / weights[:, None] / gaps
    matrix = matrix * (1.0 - ident)
    return matrix - ident * matrix.sum(axis=1)[:, None]


def interp_matrix(points, weights, targets):
    gaps = targets[:, None] - points[None, :]
    exact_hit = np.abs(gaps) < 1e-12
    safe_gaps = np.where(exact_hit, 1.0, gaps)
    terms = weights[None, :] / safe_gaps
    matrix = terms / terms.sum(axis=1, keepdims=True)
    any_hit = exact_hit.any(axis=1)
    return np.where(any_hit[:, None], np.where(exact_hit, 1.0, 0.0), matrix)


def lifted_matrix(count, length, periodic):
    points, weights = cheb_tables(count)
    matrix = np.kron(np.eye(length // count), diff_matrix(points, weights))
    lift = (count - 1) ** 2 / 2.0
    for place in range(length):
        if place % count == 0:
            matrix[place, place] += lift
            if place > 0:
                matrix[place, place - 1] -= lift
            elif periodic:
                matrix[place, length - 1] -= lift
        if place % count == count - 1:
            matrix[place, place] -= lift
            if place < length - 1:
                matrix[place, place + 1] += lift
            elif periodic:
                matrix[place, 0] += lift
    return matrix


def hilo(matrix):
    hi = matrix.astype(ml_dtypes.bfloat16)
    lo = (matrix - hi.astype(np.float64)).astype(ml_dtypes.bfloat16)
    return hi, lo


def left_pieces(matrix):
    h, l = hilo(matrix)
    if matrix.shape[1] <= 64:
        return [np.concatenate([h, l, h], 1)]
    if matrix.shape[1] <= 128:
        return [np.concatenate([h, h], 1), l]
    return [h, l]


def right_pieces(matrix):
    h, l = hilo(matrix)
    return [np.concatenate([h, h], 0), l]


def level_ops(n, zlen):
    m = lifted_matrix(n, n, False)
    c = (n - 1) ** 2 / 2.0
    eye = np.eye(n)
    e0, e1 = eye[:, :1], eye[:, -1:]
    mm = m @ m - c * c * (e0 @ e0.T + e1 @ e1.T)
    a = np.concatenate([np.kron(m, eye), np.kron(eye, m), NU * (np.kron(mm, eye) + np.kron(eye, mm))])
    zero = np.zeros((n, 1))
    gb, ga = -c * e0, c * e1
    lb = [-c * NU * m[:, :1], -c * NU * e0]
    la = [c * NU * m[:, -1:], c * NU * e1]

    def bx(col):
        return np.kron(col, eye)

    def by(col):
        return np.kron(eye, col)

    hx = np.concatenate([bx(gb), bx(zero), bx(ga), bx(zero), by(zero), by(zero), by(zero), by(zero)], 1)
    hy = np.concatenate([bx(zero), bx(zero), bx(zero), bx(zero), by(gb), by(zero), by(ga), by(zero)], 1)
    hl = np.concatenate([bx(lb[0]), bx(lb[1]), bx(la[0]), bx(la[1]), by(lb[0]), by(lb[1]), by(la[0]), by(la[1])], 1)
    h = np.concatenate([hx, hy, hl])
    z = lifted_matrix(n, zlen, True)
    return m, a, h, z.T, NU * (z @ z).T


def faces_matrix(rows_val, rows_par, n_in):
    eye = np.eye(n_in)
    out = []
    for side in (0, 1):
        out += [np.kron(rows_val[side][None], eye), np.kron(rows_par[side][None], eye)]
    for side in (0, 1):
        out += [np.kron(eye, rows_val[side][None]), np.kron(eye, rows_par[side][None])]
    return np.concatenate(out)


def tables():
    fp, fw = cheb_tables(16)
    cp, cw = cheb_tables(8)
    r = interp_matrix(fp, fw, cp)
    p = interp_matrix(cp, cw, fp)
    t = {}
    m, a, h, zg, zl = level_ops(16, 128)
    t["fa"] = a
    t["fh"] = h[512:]
    t["fz"] = np.concatenate([zg, zl], 1)
    part = faces_matrix((m[0] * 0, m[0] * 0), (m[0], m[-1]), 16)
    t["fe"] = np.concatenate([part[16:32], part[48:64], part[80:96], part[112:128]])
    pr = p @ r
    proj = faces_matrix((m[0] * 0, m[0] * 0), (m[0] @ pr, m[-1] @ pr), 16)
    t["r4"] = np.kron(np.eye(4), r)
    t["fp"] = t["r4"] @ np.concatenate([proj[16:32], proj[48:64], proj[80:96], proj[112:128]])
    mc, ac, hc, zgc, zlc = level_ops(8, 64)
    t["ca"] = np.concatenate([ac, hc], 1)
    two = np.eye(2)
    t["cz"] = np.concatenate([np.kron(two, zgc), np.kron(two, zlc)], 1)
    e8 = np.eye(8)
    t["cf"] = faces_matrix((e8[0], e8[-1]), (mc[0], mc[-1]), 8)
    mp = m @ p
    t["xf"] = faces_matrix((p[0], p[-1]), (mp[0], mp[-1]), 8)
    t["rxy"] = np.kron(r, r)
    t["rz"] = np.kron(np.eye(8), r).T
    t["pxy"] = np.kron(p, p)
    t["pz"] = np.kron(np.eye(8), p).T
    t["ph"] = np.kron(np.eye(8), p)
    t["pv"] = np.kron(np.eye(4), np.concatenate([p, 0.0 * p], 1))
    t["lp"] = t["fh"] @ t["ph"]
    return t


def packed(names, table):
    where, rows, at = {}, [], 0
    for name in names:
        for i, piece in enumerate((right_pieces if name in RIGHT else left_pieces)(table[name])):
            n, k = piece.shape
            where[name, i] = (at, n, k)
            full = np.zeros((-(-n // 16) * 16, 256), ml_dtypes.bfloat16)
            full[:n, :k] = piece
            rows.append(full)
            at += full.shape[0]
    return np.concatenate(rows), where


RIGHT = ("fz", "cz", "rz", "pz")
TABLES = tables()
EDGE = lifted_matrix(16, 16, False)
PACK_A, WHERE = packed(["fe", "fp"], TABLES)
PACK_B, WHERE_B = packed([n for n in TABLES if n not in ("fe", "fp")], TABLES)
WHERE.update(WHERE_B)


def split(x):
    hi = x.astype(BF)
    lo = (x - hi.astype(F32)).astype(BF)
    return hi, lo


def mm(a, b):
    return jnp.dot(a, b, preferred_element_type=F32)


def piece(t, name, i):
    at, n, k = WHERE[name, i]
    return t[at : at + n, :k]


def ldot(t, name, x):
    xh, xl = split(x)
    if x.shape[0] <= 64:
        return mm(piece(t, name, 0), jnp.concatenate([xh, xh, xl], axis=0))
    if x.shape[0] <= 128:
        return mm(piece(t, name, 0), jnp.concatenate([xh, xl], axis=0)) + mm(piece(t, name, 1), xh)
    th = piece(t, name, 0)
    return mm(th, xh) + (mm(piece(t, name, 1), xh) + mm(th, xl))


def rdot(x, t, name):
    xh, xl = split(x)
    return mm(jnp.concatenate([xh, xl], axis=1), piece(t, name, 0)) + mm(xh, piece(t, name, 1))


def cat3(v):
    return jnp.concatenate([v[0], v[1], v[2]], axis=1)


def cut3(x, width=128):
    return [x[:, i * width : (i + 1) * width] for i in range(3)]


def fine_local(v, t):
    g = ldot(t, "fa", cat3(v))
    z = rdot(jnp.concatenate(v, axis=0), t, "fz")
    out = []
    for c in range(3):
        s = slice(128 * c, 128 * c + 128)
        zc = z[256 * c : 256 * c + 256]
        adv = v[0] * g[0:256, s] + v[1] * g[256:512, s] + v[2] * zc[:, :128]
        out.append(g[512:768, s] + zc[:, 128:] - adv)
    return out


def fine_rate(v, loc, halo, t, acc):
    k = ldot(t, "fh", cat3(halo))
    c = 112.5
    low, high = pl.ds(0, 16, stride=16), pl.ds(15, 16, stride=16)
    vlow, vhigh = v[1, low, :], v[1, high, :]
    for i in range(3):
        r = loc[i] + k[:, 128 * i : 128 * i + 128]
        acc[i, 16:240] = r[16:240]
        acc[i, 0:16] = r[0:16] + c * v[0, 0:16] * halo[i][0:16]
        acc[i, 240:256] = r[240:256] - c * v[0, 240:256] * halo[i][32:48]
        acc[i, low, :] = acc[i, low, :] + c * vlow * halo[i][64:80]
        acc[i, high, :] = acc[i, high, :] - c * vhigh * halo[i][96:112]


def halo_of(flags, h, c, lo, hi):
    p2, p1, c1, c2 = [r[c, lo:hi] for r in h]
    rodd, codd = flags[1] == 1, flags[2] == 1
    return jnp.concatenate(
        [jnp.where(rodd, p1, p2), jnp.where(rodd, p2, p1), jnp.where(codd, c1, c2), jnp.where(codd, c2, c1)], axis=0
    )


def send_faces(flags, outs, c, rows, xlo, xhi, ylo, yhi):
    rodd, codd = flags[1] == 1, flags[2] == 1
    outs[0][c, rows] = jnp.where(rodd, xhi, xlo)
    outs[1][c, rows] = jnp.where(rodd, xlo, xhi)
    outs[2][c, rows] = jnp.where(codd, ylo, yhi)
    outs[3][c, rows] = jnp.where(codd, yhi, ylo)


def fine_faces(flags, outs, vref, t):
    v = [vref[c] for c in range(3)]
    part = ldot(t, "fe", cat3(v))
    for c in range(3):
        pc = part[:, 128 * c : 128 * c + 128]
        send_faces(
            flags, outs, c, slice(0, 16),
            v[c][0:16], v[c][240:256],
            vref[c, pl.ds(0, 16, stride=16), :], vref[c, pl.ds(15, 16, stride=16), :],
        )
        send_faces(flags, outs, c, slice(16, 32), pc[0:16], pc[16:32], pc[32:48], pc[48:64])


def beside(f):
    return jnp.concatenate([f[0:8], f[8:16]], axis=1)


def coarse_faces(flags, outs, c, f):
    send_faces(flags, outs, c, slice(0, 8), *[beside(f[16 * d : 16 * d + 16]) for d in range(4)])


def coarse_rate(w, halo, t):
    g = cut3(ldot(t, "ca", jnp.concatenate([cat3(w), cat3(halo)], axis=0)))
    z = rdot(jnp.concatenate(w, axis=0), t, "cz")
    out = []
    for c in range(3):
        s = slice(64 * c, 64 * c + 64)
        adv = w[0] * g[c][0:64] + w[1] * g[c][64:128] + w[2] * z[s, :128]
        out.append(g[c][128:192] + z[s, 128:] - adv)
    return out


def restrict(v, t):
    s = ldot(t, "rxy", cat3(v))
    r = rdot(jnp.concatenate(cut3(s), axis=0), t, "rz")
    return [r[64 * c : 64 * c + 64] for c in range(3)]


def prolong(e, t):
    s = rdot(jnp.concatenate(e, axis=0), t, "pz")
    return cut3(ldot(t, "pxy", jnp.concatenate([s[0:64], s[64:128], s[128:192]], axis=1)))


def wide(x):
    return jnp.concatenate([x, x], axis=1)


def load3(r):
    return [r[c] for c in range(3)]


def store3(r, v):
    for c in range(3):
        r[c] = v[c]


def k_start(flags, v, *outs):
    for c in range(3):
        px = [v[c, 16 * j : 16 * j + 16] for j in range(16)]
        py = [v[c, pl.ds(j, 16, stride=16), :] for j in range(16)]
        send_faces(flags, outs, c, slice(0, 16), px[0], px[15], py[0], py[15])
        parts = []
        for plane in (px, py):
            for row in (EDGE[0], EDGE[15]):
                total = float(row[0]) * plane[0]
                for j in range(1, 16):
                    total = total + float(row[j]) * plane[j]
                parts.append(total)
        send_faces(flags, outs, c, slice(16, 32), *parts)


def k_bulk1(v, t, out):
    store3(out, fine_local(load3(v), t))


def k_bulkq(flags, q, t, out, w0, *outs):
    qq = load3(q)
    store3(out, fine_local(qq, t))
    w = restrict(qq, t)
    store3(w0, w)
    for c in range(3):
        coarse_faces(flags, outs, c, ldot(t, "cf", w[c]))


def k_post1(flags, v, loc, h1, h2, h3, h4, d1, d2, d3, d4, ta, t, f0, v1, *outs):
    h = (h1, h2, h3, h4)
    halo = [halo_of(flags, h, c, 0, 32) for c in range(3)]
    fine_rate(v, loc, halo, t, f0)
    for c in range(3):
        v1[c] = v[c] + (H / 2.0) * f0[c]
    fine_faces(flags, outs, v1, ta)
    for o, d in zip(outs, (d1, d2, d3, d4)):
        for c in range(3):
            o[c, 32:40] = d[c]


def k_bulk2(flags, v, w0, t, out, w, *outs):
    vv = load3(v)
    store3(out, fine_local(vv, t))
    w1 = restrict(vv, t)
    for c in range(3):
        w[c] = jnp.concatenate([w0[c], w1[c]], axis=1)
        coarse_faces(flags, outs, c, ldot(t, "cf", w1[c]))
        f = ldot(t, "xf", w1[c])
        send_faces(flags, outs, c, slice(8, 16), *[wide(f[16 * d + 8 : 16 * d + 16]) for d in range(4)])


def k_post2(flags, v, loc, h1, h2, h3, h4, d1, d2, d3, d4, ta, t, b1, v2, *outs):
    h = (h1, h2, h3, h4)
    halo = [halo_of(flags, h, c, 0, 32) for c in range(3)]
    fine_rate(v, loc, halo, t, b1)
    for c in range(3):
        v2[c] = v[c] + (H / 2.0) * b1[c]
    fine_faces(flags, outs, v2, ta)
    part = rdot(jnp.concatenate(cut3(ldot(ta, "fp", cat3(load3(v2)))), axis=0), t, "rz")
    for c in range(3):
        send_faces(flags, outs, c, slice(40, 48), *[wide(part[32 * c + 8 * d : 32 * c + 8 * d + 8]) for d in range(4)])
    left = lax.broadcasted_iota(jnp.int32, (8, 128), 1) < 64
    for o, d in zip(outs, (d1, d2, d3, d4)):
        for c in range(3):
            o[c, 32:40] = d[c, 0:8]
            o[c, 40:48] = jnp.where(left, d[c, 8:16], o[c, 40:48])


def k_bulk3(v, f0, b1, t, out, w2, fa, fb):
    vv = load3(v)
    store3(out, fine_local(vv, t))
    store3(w2, restrict(vv, t))
    rf = restrict(load3(f0), t)
    rb = restrict(load3(b1), t)
    for c in range(3):
        fa[c] = (H * W0[0]) * rf[c] + (H * W0[1]) * rb[c]
        fb[c] = (H * W1[0]) * rf[c] + (H * W1[1]) * rb[c]


def k_post3(flags, v, loc, h1, h2, h3, h4, e1, e2, e3, e4, w, fa, fb, t, a, b2):
    h = (h1, h2, h3, h4)
    halo = [halo_of(flags, h, c, 0, 32) for c in range(3)]
    fine_rate(v, loc, halo, t, b2)
    rb = restrict(load3(b2), t)
    ww = load3(w)
    chalo = []
    for c in range(3):
        m0, m1 = halo_of(flags, (e1, e2, e3, e4), c, 32, 40), halo_of(flags, h, c, 32, 40)
        val = jnp.concatenate([m0[:, :64], m1[:, :64]], axis=1)
        par = jnp.concatenate([m0[:, 64:], m1[:, 64:]], axis=1)
        chalo.append(jnp.concatenate(
            [x[8 * d : 8 * d + 8] for d in range(4) for x in (val, par)], axis=0
        ))
    cr = coarse_rate(ww, chalo, t)
    for c in range(3):
        t0 = fa[c] + (H * W0[2]) * rb[c]
        t1 = fb[c] + (H * W1[2]) * rb[c]
        start = jnp.where(flags[0] == 1, ww[c][:, :64], (-H / 2.0) * cr[c][:, :64])
        a[c] = jnp.concatenate([start + t0, t1 - (H / 2.0) * cr[c][:, 64:]], axis=1)


def k_base(flags, v, e1, e2, e3, e4, h1, h2, h3, h4, t, base1, vh):
    e, h = (e1, e2, e3, e4), (h1, h2, h3, h4)
    own1 = [halo_of(flags, e, c, 0, 32) for c in range(3)]
    own2 = [halo_of(flags, h, c, 0, 32) for c in range(3)]
    val1 = [halo_of(flags, h, c, 32, 40) for c in range(3)]
    par = [halo_of(flags, h, c, 40, 48) for c in range(3)]
    faces = [jnp.concatenate([own2[c][32 * d : 32 * d + 16] for d in range(4)], axis=0) for c in range(3)]
    val2 = rdot(jnp.concatenate(cut3(ldot(t, "r4", cat3(faces))), axis=0), t, "rz")

    def weave(a, b):
        return jnp.concatenate([x[8 * d : 8 * d + 8] for d in range(4) for x in (a, b)], axis=0)

    co = [weave(val1[c][:, :64], par[c][:, :64]) for c in range(3)]
    co += [weave(val2[32 * c : 32 * c + 32], par[c][:, 64:]) for c in range(3)]
    s = rdot(jnp.concatenate(co, axis=0), t, "pz")
    fine = ldot(t, "ph", jnp.concatenate([s[64 * i : 64 * i + 64] for i in range(6)], axis=1))
    for c in range(3):
        base1[c] = own1[c] - fine[:, 128 * c : 128 * c + 128]
        vh[c, 0:256] = v[c]
        vh[c, 256:384] = own2[c] - fine[:, 384 + 128 * c : 512 + 128 * c]


def pair_faces(e, t, out, up, down, left, right):
    for c in range(3):
        out[c, 0:64] = e[c]
        f = ldot(t, "cf", e[c])
        up[c] = f[0:16, :64]
        down[c] = f[16:32, 64:]
        left[c] = f[32:48]
        right[c] = f[48:64]
        out[c, 64:80] = jnp.concatenate([f[0:16, 64:], f[16:32, :64]], axis=1)


def k_begin(flags, own, far, own2, far2, t, even, odd, *outs):
    low, second = flags[1] == 1, flags[3] == 1

    def pair(c, mine, other):
        a = jnp.where(low, other[c], mine[c])
        b = jnp.where(low, mine[c], other[c])
        return jnp.concatenate([
            jnp.concatenate([a[:, :64], b[:, :64]], axis=1), jnp.concatenate([a[:, 64:], b[:, 64:]], axis=1)
        ], axis=0)

    e = []
    for c in range(3):
        p, q = pair(c, own, far), pair(c, own2, far2)
        even[c] = jnp.where(second, q, p)
        odd[c] = jnp.where(second, p, q)
        e.append(even[c, 0:64])
    pair_faces(e, t, *outs)


def pair_step(e, up, down, left, right, r, t, rows):
    ee = [e[c, 0:64] for c in range(3)]
    halo = []
    for c in range(3):
        i = e[c, 64:80]
        halo.append(jnp.concatenate([
            jnp.concatenate([up[c], i[:, 64:]], axis=1), jnp.concatenate([i[:, :64], down[c]], axis=1), left[c], right[c]
        ], axis=0))
    rate = coarse_rate(ee, halo, t)
    return [ee[c] + (H / 2.0) * rate[c] + r[c, rows : rows + 64] for c in range(3)]


def k_chain(e, up, down, left, right, r, t, *outs, rows):
    pair_faces(pair_step(e, up, down, left, right, r, t, rows), t, *outs)


def mine(flags, x):
    return jnp.where(flags[1] == 1, x[:, 64:], x[:, :64])


def k_x0(flags, a2e, b2e, bk, ws, q, vh, a1, a2, a3, a4, t, kp, x, g):
    first, second, late = flags[0] == 1, flags[3] == 1, flags[4] == 1
    d = []
    for c in range(3):
        k = jnp.where(second, jnp.where(late, b2e[c, 0:64], a2e[c, 0:64]), bk[c, 0:64])
        kp[c] = k
        d.append(jnp.where(first, 0.0, mine(flags, k) - ws[c]))
    pr = prolong(d, t)
    xs = [jnp.where(first, q[c], vh[c, 0:256]) + pr[c] for c in range(3)]
    store3(x, xs)
    base = [jnp.where(first, halo_of(flags, (a1, a2, a3, a4), c, 0, 32), vh[c, 256:384]) for c in range(3)]
    fine_rate(x, fine_local(xs, t), base, t, g)


def k_x1(flags, even, a1o, b1e, b1o, w, v1, base1, t, ep, x, g):
    second, late = flags[3] == 1, flags[4] == 1
    d = []
    for c in range(3):
        e1 = jnp.where(
            late, jnp.where(second, b1o[c, 0:64], b1e[c, 0:64]), jnp.where(second, a1o[c, 0:64], even[c, 0:64])
        )
        ep[c] = e1
        d.append(mine(flags, e1) - w[c][:, 64:])
    pr = prolong(d, t)
    xs = [v1[c] + pr[c] for c in range(3)]
    store3(x, xs)
    fine_rate(x, fine_local(xs, t), load3(base1), t, g)


def k_dstart(flags, e, up, down, left, right, r, a2e, a2o, b2e, kp, ep, w2, t, d2, row, inner, toleft, toright):
    odd, second, late = flags[1] == 1, flags[3] == 1, flags[4] == 1
    b2o = pair_step(e, up, down, left, right, r, t, 64)
    for c in range(3):
        e2 = jnp.where(
            late, jnp.where(second, b2o[c], b2e[c, 0:64]), jnp.where(second, a2o[c, 0:64], a2e[c, 0:64])
        )
        d2[c] = mine(flags, e2) - w2[c]
        f = ldot(t, "xf", jnp.concatenate([kp[c], ep[c], e2], axis=1))
        lows = [f[:, 128 * m : 128 * m + 64] for m in range(3)]
        highs = [f[:, 128 * m + 64 : 128 * m + 128] for m in range(3)]

        def put(out, cond, rows, lo, hi):
            n = [jnp.where(cond, hi[m][rows[1]], lo[m][rows[0]]) for m in range(3)]
            out[c, 0:16] = jnp.concatenate([n[0], n[1]], axis=1)
            out[c, 16:32] = jnp.concatenate([n[2], n[2]], axis=1)

        xlo, xhi, ylo, yhi = slice(0, 16), slice(16, 32), slice(32, 48), slice(48, 64)
        put(row, odd, (xhi, xlo), highs, lows)
        put(inner, odd, (xlo, xhi), highs, lows)
        put(toleft, flags[5] == 1, (ylo, ylo), lows, highs)
        put(toright, flags[6] == 1, (yhi, yhi), lows, highs)


def k_x2(d, v2, v2h, t, x, g):
    pr = prolong(load3(d), t)
    xs = [v2[c] + pr[c] for c in range(3)]
    store3(x, xs)
    fine_rate(x, fine_local(xs, t), [v2h[c, 256:384] for c in range(3)], t, g)


def k_ws(vh, t, ws):
    store3(ws, restrict([vh[c, 0:256] for c in range(3)], t))


def k_xpost(flags, x0, x1, x2, g0, g1, g2, inner, row, left, right, ta, t, u1, d, o1, o2, o3, o4):
    first, odd = flags[0] == 1, flags[1] == 1

    def around(c, rows):
        i, r = inner[c, rows], row[c, rows]
        return jnp.concatenate([jnp.where(odd, i, r), jnp.where(odd, r, i), left[c, rows], right[c, rows]], axis=0)

    lo = [around(c, slice(0, 16)) for c in range(3)]
    hi = [around(c, slice(16, 32)) for c in range(3)]
    co = [jnp.where(first, 0.0, lo[c][:, :64]) for c in range(3)]
    co += [lo[c][:, 64:] for c in range(3)] + [hi[c][:, :64] for c in range(3)]
    s = rdot(jnp.concatenate(co, axis=0), t, "pz")
    s = [s[64 * i : 64 * i + 64] for i in range(9)]
    val = ldot(t, "pv", jnp.concatenate(s, axis=1))
    val = [val[:, 128 * i : 128 * i + 128] for i in range(9)]
    weights = (W0, (W1[0], W1[1] - 0.5, W1[2]))
    mixed = [w[0] * s[c] + w[1] * s[3 + c] + w[2] * s[6 + c] for w in weights for c in range(3)]
    lift = ldot(t, "lp", jnp.concatenate(mixed, axis=1))
    low, high = pl.ds(0, 16, stride=16), pl.ds(15, 16, stride=16)
    xs, gs = (x0, x1, x2), (g0, g1, g2)
    for i, (w, out) in enumerate(zip(weights, (u1, d))):
        for c in range(3):
            mix = w[0] * gs[0][c] + w[1] * gs[1][c] + w[2] * gs[2][c]
            before = x0[c] if i == 0 else u1[c]
            out[c] = before + H * (mix + lift[:, 384 * i + 128 * c : 384 * i + 128 * c + 128])
            edges = [0.0] * 4
            for m in range(3):
                f, k, x = val[3 * m + c], H * 112.5 * w[m], xs[m]
                edges[0] += k * (x[0, 0:16] * f[0:16])
                edges[1] -= k * (x[0, 240:256] * f[16:32])
                edges[2] += k * (x[1, low, :] * f[32:48])
                edges[3] -= k * (x[1, high, :] * f[48:64])
            out[c, 0:16] = out[c, 0:16] + edges[0]
            out[c, 240:256] = out[c, 240:256] + edges[1]
            out[c, low, :] = out[c, low, :] + edges[2]
            out[c, high, :] = out[c, high, :] + edges[3]
    fine_faces(flags, (o1, o2, o3, o4), u1, ta)


def k_last(flags, v, d, loc, h1, h2, h3, h4, t, out, acc):
    h = (h1, h2, h3, h4)
    halo = [halo_of(flags, h, c, 0, 32) for c in range(3)]
    fine_rate(v, loc, halo, t, acc)
    for c in range(3):
        out[c] = d[c] + (H / 2.0) * acc[c]


def call(kernel, args, outs, cost=0, scratch=()):
    flat = args
    specs = [
        pl.BlockSpec(memory_space=pltpu.SMEM if a.dtype == jnp.int32 else pltpu.VMEM) for a in flat
    ]
    shapes = [jax.ShapeDtypeStruct(s, F32) for s in outs]
    size = sum(int(np.prod(a.shape)) * a.dtype.itemsize for a in flat) + sum(int(np.prod(s)) * 4 for s in outs)
    return pl.pallas_call(
        kernel,
        out_shape=shapes,
        in_specs=specs,
        out_specs=[pl.BlockSpec(memory_space=pltpu.VMEM) for _ in outs],
        scratch_shapes=[pltpu.VMEM(s, F32) for s in scratch],
        cost_estimate=pl.CostEstimate(flops=cost, bytes_accessed=size, transcendentals=0),
        compiler_params=pltpu.CompilerParams(vmem_limit_bytes=48 * 1024 * 1024),
    )(*flat)


def routes(shift):
    def dev(t, r, c):
        return t * 64 + (r % 16) * 4 + c % 4

    out = []
    for kind in range(4):
        pairs = []
        for t in range(4):
            if not 0 <= t + shift < 4:
                continue
            for r in range(16):
                for c in range(4):
                    if kind == 0:
                        to = (r + 1 if r & 1 else r - 1, c)
                    elif kind == 1:
                        to = (r ^ 1, c)
                    elif kind == 2:
                        to = (r, c ^ 1)
                    else:
                        to = (r, c + 1 if c & 1 else c - 1)
                    pairs.append((dev(t, r, c), dev(t + shift, *to)))
        out.append(pairs)
    return out


def ring_routes(late):
    out = []
    for dk, dz in ((-1, 0), (1, 0), (0, -1), (0, 1)):
        pairs = []
        for t in range(4):
            to = t ^ (2 * late)
            for k in range(8):
                for z in range(8):
                    pairs.append((t * 64 + k * 8 + z, to * 64 + ((k + dk) % 8) * 8 + (z + dz) % 8))
        out.append(pairs)
    return out


def shards(initial):
    ta, tb = jnp.asarray(PACK_A), jnp.asarray(PACK_B)
    space, tm = lax.axis_index("space"), lax.axis_index("tm")
    flags = jnp.stack([(tm == 0).astype(jnp.int32), (space // 4) % 2, space % 2, tm % 2, tm // 2, (space + 7) % 8 // 4, (space + 1) % 8 // 4]).astype(jnp.int32)
    here = routes(0)
    ring, cross = ring_routes(0), ring_routes(1)
    pair_row = [(i, i // 64 * 64 + (i % 64 + (8 if i % 8 < 4 else 56)) % 64) for i in range(256)]
    after = [(t * 64 + b, (t + 1) % 4 * 64 + b) for t in range(4) for b in range(64)]
    two_on = [(t * 64 + b, (t ^ 2) * 64 + b) for t in range(4) for b in range(64)]
    partner = [(t * 64 + b, (t ^ 1) * 64 + b) for t in range(4) for b in range(64)]

    def swap(pieces, way, order=(0, 1, 2, 3)):
        got = {i: lax.ppermute(pieces[i], AX, way[i]) for i in order}
        return [got[i] for i in range(4)]

    st, pay, co, duo = (3, 256, 128), (3, 32, 128), (3, 64, 64), (3, 64, 128)
    c2pay, bpay = (3, 16, 128), (3, 48, 128)
    faces = [(3, 80, 128), (3, 16, 64), (3, 16, 64), (3, 16, 128), (3, 16, 128)]
    q = initial.reshape(st)
    big = 2_000_000_000
    p = call(k_start, [flags, q], [pay] * 4)
    h1 = swap(p, here)
    loc, w0, *cp = call(k_bulkq, [flags, q, tb], [st, co] + [(3, 8, 128)] * 4, big)
    f0, v1, *p = call(k_post1, [flags, q, loc, *h1, *cp, ta, tb], [st, st] + [(3, 40, 128)] * 4)
    h2 = swap(p, here)
    loc, w, *cp = call(k_bulk2, [flags, v1, w0, tb], [st, duo] + [c2pay] * 4, big)
    b1, v2, *p = call(k_post2, [flags, v1, loc, *h2, *cp, ta, tb], [st, st] + [bpay] * 4)
    h3 = swap(p, here)
    loc, w2, fa, fb = call(k_bulk3, [v2, f0, b1, tb], [st, co, co, co], big)
    (a,) = call(k_post3, [flags, v2, loc, *h3, *h2, w, fa, fb, tb], [duo], scratch=[st])
    far = lax.ppermute(a, AX, here[1])
    own2 = lax.ppermute(a, AX, partner)
    own2, v2late = lax.optimization_barrier((own2, v2))
    base1, vh = call(k_base, [flags, v2late, *h2, *h3, tb], [(3, 128, 128), (3, 384, 128)], big)
    vprev = lax.ppermute(vh, AX, after)
    far2 = lax.ppermute(far, AX, partner)
    even, odd, e, *p = call(k_begin, [flags, a, far, own2, far2, tb], [(3, 128, 128)] * 2 + faces)

    def trade(p, way):
        below, above, right, left = swap(p, way, (0, 1, 2, 3))
        return above, below, left, right

    def step(e, p, way, r, rows):
        return call(functools.partial(k_chain, rows=rows), [e, *trade(p, way), r, tb], faces)

    a2e, *p = step(e, p, ring, even, 64)
    a1o, *p = step(a2e, p, ring, odd, 0)
    a2o, *p = step(a1o, p, ring, odd, 64)
    (ws,) = call(k_ws, [vprev, tb], [co])
    bk = lax.ppermute(a2o, AX, two_on)
    bk, ws = lax.optimization_barrier((bk, ws))
    b1e, *p = step(bk, p, cross, even, 0)
    b2e, *p = step(b1e, p, ring, even, 64)
    kp, x0, g0 = call(k_x0, [flags, a2e, b2e, bk, ws, q, vprev, *h1, tb], [duo, st, st], big)
    b1o, *p = step(b2e, p, ring, odd, 0)
    ep, x1, g1 = call(k_x1, [flags, even, a1o, b1e, b1o, w, v1, base1, tb], [duo, st, st], big)
    d2, row, inner, toleft, toright = call(
        k_dstart, [flags, b1o, *trade(p, ring), odd, a2e, a2o, b2e, kp, ep, w2, tb], [co] + [pay] * 4
    )
    row, right, left = (lax.ppermute(x, AX, w) for x, w in ((row, pair_row), (toleft, ring[2]), (toright, ring[3])))
    x2, g2 = call(k_x2, [d2, v2, vh, tb], [st, st], big)
    u1, d, *p = call(
        k_xpost, [flags, x0, x1, x2, g0, g1, g2, inner, row, left, right, ta, tb], [st, st] + [pay] * 4
    )
    h = swap(p, here)
    (loc,) = call(k_bulk1, [u1, tb], [st], big)
    (out,) = call(k_last, [flags, u1, d, loc, *h, tb], [st], scratch=[st])
    return out.reshape(initial.shape)


def solution(mesh):
    return jax.shard_map(
        shards,
        mesh=mesh,
        in_specs=(P("tm", None, "space", None, None, None),),
        out_specs=P("tm", None, "space", None, None, None),
        check_vma=False,
    )
```
